32 devices in a mesh: dp: 8 (over z, x), tensor: 4 (over y, core).
Axes of the slice: x: 2, y: 2, z: 4, core: 2. Of those that a mesh axis runs over, the one named last changes fastest.
Arguments:
- tokens: bfloat16 [4096, 2048], P('dp'), may hold values from -6 to 6
- cotangent: bfloat16 [4096, 2048], P('dp'), may hold values from -6 to 6
- routes: int32 [4096, 6], P('dp'), may hold values from 0 to 15, all different within a row
- seq_ids: int32 [4096], P('dp'), may hold values from 0 to 31, as said below
- positions: int32 [4096], P('dp'), may hold values from 0 to 4095, as said below
- gain_attn: bfloat16 [2048], P('dp'), may hold values from 0.5 to 1.5
- w_query: bfloat16 [2048, 3072], P('dp', 'tensor'), may hold values from -0.125 to 0.125
- w_latent: bfloat16 [2048, 576], P('dp'), may hold values from -0.125 to 0.125
- gain_latent: bfloat16 [512], P('dp'), may hold values from 0.5 to 1.5
- w_expand: bfloat16 [512, 4096], P('dp', 'tensor'), may hold values from -0.25 to 0.25
- w_output: bfloat16 [2048, 2048], P('tensor', 'dp'), may hold values from -0.75 to 0.75
- gain_ffn: bfloat16 [2048], P('dp'), may hold values from 0.5 to 1.5
- w_router: bfloat16 [2048, 16], P('dp'), may hold values from -0.0625 to 0.0625
- w_shared_gate: bfloat16 [2048, 2816], P('dp', 'tensor'), may hold values from -0.125 to 0.125
- w_shared_up: bfloat16 [2048, 2816], P('dp', 'tensor'), may hold values from -0.125 to 0.125
- w_shared_down: bfloat16 [2816, 2048], P('tensor', 'dp'), may hold values from -0.21875 to 0.21875
- w_gate: bfloat16 [16, 2048, 1408], P('dp', None, 'tensor'), may hold values from -0.125 to 0.125
- w_up: bfloat16 [16, 2048, 1408], P('dp', None, 'tensor'), may hold values from -0.125 to 0.125
- w_down: bfloat16 [16, 1408, 2048], P('dp', 'tensor'), may hold values from -0.4375 to 0.4375
Outputs:
- result: bfloat16 [4096, 2048], P('dp')
- tokens_grad: bfloat16 [4096, 2048], P('dp')
- gain_attn_grad: float32 [2048], P('dp')
- w_query_grad: float32 [2048, 3072], P('dp', 'tensor')
- w_latent_grad: float32 [2048, 576], P('dp')
- gain_latent_grad: float32 [512], P('dp')
- w_expand_grad: float32 [512, 4096], P('dp', 'tensor')
- w_output_grad: float32 [2048, 2048], P('tensor', 'dp')
- gain_ffn_grad: float32 [2048], P('dp')
- w_router_grad: float32 [2048, 16], P('dp')
- w_shared_gate_grad: float32 [2048, 2816], P('dp', 'tensor')
- w_shared_up_grad: float32 [2048, 2816], P('dp', 'tensor')
- w_shared_down_grad: float32 [2816, 2048], P('tensor', 'dp')
- w_gate_grad: float32 [16, 2048, 1408], P('dp', None, 'tensor')
- w_up_grad: float32 [16, 2048, 1408], P('dp', None, 'tensor')
- w_down_grad: float32 [16, 1408, 2048], P('dp', 'tensor')
The draws below stay inside these ranges and needn't reach their ends.
Inputs may be any that keep to these rules, and one draw needn't show every extreme that they name: `routes`: each token names 6 different experts. `seq_ids`: ids never fall along the tokens, and every sequence lies inside one block of 512 tokens. Within a sequence, positions rise by one from token to token.
All inputs are finite; a program needn't handle non-finite values.
Results may differ from the reference program's by a relative error of at most 0.02.
Values may be sent and summed in bfloat16 or wider, within the bound.
No kernel may reach another device: no remote copies, remote signals or barrier semaphores. Data moves between devices by JAX's collectives and lax.ppermute only.
A program may use at most 384 MiB of HBM per device.

```python
import jax
import jax.numpy as jnp
from jax import lax

D = 2048
HEADS = 16
QK_NOPE = 128
QK_ROPE = 64
V_HEAD = 128
KV_RANK = 512
FF = 1408
SHARED_EXP = 2
TOP = 6
TOK_DEV = 512
EXPERTS = 16
TOKENS = 4096
CAP = 240
N_TENSOR = 4


def sequence_layout(key):
    blocks = TOKENS // TOK_DEV
    base_key = jax.random.fold_in(key, 41)
    cut_key, live_key, start_key, whole_key = jax.random.split(base_key, 4)
    cut_points = jax.random.randint(cut_key, (blocks, 3), 1, TOK_DEV)
    cut_live = jax.random.randint(live_key, (blocks, 3), 0, 2)
    whole_block = jax.random.randint(whole_key, (), 0, blocks - 1)
    block_ids = jnp.arange(blocks, dtype=jnp.int32)
    is_whole = (block_ids == whole_block).astype(jnp.int32)
    is_last = (block_ids == blocks - 1).astype(jnp.int32)
    cut_live = cut_live * (1 - is_whole)[:, None]
    cut_live = jnp.maximum(cut_live, is_last[:, None])
    token_index = jnp.arange(TOK_DEV, dtype=jnp.int32)
    passed = cut_live[:, None, :] * (token_index[None, :, None] >= cut_points[:, None, :]).astype(jnp.int32)
    local_seq = jnp.sum(passed, axis=-1).astype(jnp.int32)
    seg_begin = jnp.max(passed * cut_points[:, None, :], axis=-1).astype(jnp.int32)
    starts = jax.random.randint(start_key, (blocks, 4), 0, 4097 - TOK_DEV)
    seg_zero = (jnp.arange(4, dtype=jnp.int32) == 0)[None, :]
    starts = jnp.where((is_whole[:, None] == 1) & seg_zero, 4096 - TOK_DEV, starts)
    starts = jnp.where((is_last[:, None] == 1) & seg_zero, 0, starts)
    chosen = jnp.sum(starts[:, None, :] * (local_seq[:, :, None] == jnp.arange(4, dtype=jnp.int32)[None, None, :]).astype(jnp.int32), axis=-1)
    seq_local = block_ids[:, None] * 4 + local_seq
    pos_local = chosen + token_index[None, :] - seg_begin
    return (seq_local.reshape(-1).astype(jnp.int32), pos_local.reshape(-1).astype(jnp.int32))


def draw_seq_ids(key, part):
    return sequence_layout(key)[0]


def draw_positions(key, part):
    return sequence_layout(key)[1]


def strengthened(values, stream_key, source, target, shards_of, factor):
    owner, partner = [(jnp.arange(values.shape[position]) // (values.shape[position] // shards_of)).reshape([-1 if axis == position else 1 for axis in range(values.ndim)]) for position in (source, target)]
    chosen = jax.random.permutation(stream_key, shards_of)[partner]
    strong = (owner == chosen) | (owner == (partner + shards_of // 2) % shards_of)
    return jnp.where(strong, factor * values, values)


def block_levels(own_key, extent, cuts, low, high):
    factor_of, own = 1.0, jax.random.fold_in(own_key, 6)
    for position, shards_of in cuts:
        steps = jnp.exp(jax.random.uniform(jax.random.fold_in(own, position), (shards_of,), jnp.float32, low / len(cuts), high / len(cuts)))
        factor_of = factor_of * jnp.repeat(steps, extent[position] // shards_of).reshape([-1 if axis == position else 1 for axis in range(len(extent))])
    return factor_of


def choose_distinct(own_key, rows, number_of, top, lift):
    order = jax.random.permutation(jax.random.fold_in(own_key, 1), number_of)
    pull = order
    for power in range(3):
        pull = pull * pull // number_of
    pull = pull * lift // number_of
    lots = jax.random.randint(jax.random.fold_in(own_key, 2), (rows, number_of), 0, 4096) + pull
    fixed_rows = jax.random.permutation(jax.random.fold_in(own_key, 3), rows)[jnp.arange(number_of) % rows]
    lots = jnp.where(jnp.arange(rows)[:, None] == fixed_rows[None, :], 1 << 14, lots)
    merit = lots * number_of + jnp.arange(number_of)
    return lax.top_k(merit.astype(jnp.int32), top)[1].astype(jnp.int32)


def bell_draw(own_key, extent, deviation, bound, cuts=(), kind=jnp.bfloat16):
    array = jax.random.normal(own_key, extent, jnp.float32) * deviation
    if len(cuts) > 0:
        array = block_levels(own_key, extent, cuts, -0.22, 0.18) * array
    return jnp.clip(array, min=-bound, max=bound).astype(kind)


def heavy_noise(rng, shape, deviation, reach, cuts, heavy, kind=jnp.bfloat16):
    values = deviation * jax.random.normal(rng, shape, jnp.float32)
    if cuts:
        values = values * block_levels(rng, shape, cuts, -0.22, 0.18)
    return jnp.clip(strengthened(values, jax.random.fold_in(rng, 3), *heavy), -reach, reach).astype(kind)


def setup_inputs(seed: int = 0) -> dict:
    streams_of = jax.random.split(jax.random.key(seed), 20)
    return {
        "tokens": heavy_noise(streams_of[0], (TOKENS, D), 1.0, 6.0, ((0, 8),), (0, 1, 8, 2.0)),
        "cotangent": heavy_noise(streams_of[1], (TOKENS, D), 1.0, 6.0, ((0, 8),), (0, 1, 8, 2.0)),
        "routes": choose_distinct(streams_of[2], TOKENS, EXPERTS, TOP, 3072),
        "seq_ids": draw_seq_ids(jax.random.fold_in(streams_of[19], 71), 0),
        "positions": draw_positions(jax.random.fold_in(streams_of[19], 71), 0),
        "gain_attn": jnp.clip(1.0 + 0.1 * jax.random.normal(streams_of[5], (D,), jnp.float32), 0.5, 1.5).astype(jnp.bfloat16),
        "w_query": bell_draw(streams_of[6], (D, HEADS * (QK_NOPE + QK_ROPE)), D ** -0.5, 0.125, ((0, 8), (1, 4))),
        "w_latent": bell_draw(streams_of[7], (D, KV_RANK + QK_ROPE), D ** -0.5, 0.125, ((0, 8),)),
        "gain_latent": jnp.clip(1.0 + 0.1 * jax.random.normal(streams_of[8], (KV_RANK,), jnp.float32), 0.5, 1.5).astype(jnp.bfloat16),
        "w_expand": bell_draw(streams_of[9], (KV_RANK, HEADS * (QK_NOPE + V_HEAD)), KV_RANK ** -0.5, 0.25, ((0, 8), (1, 4))),
        "w_output": bell_draw(streams_of[10], (HEADS * V_HEAD, D), (HEADS * V_HEAD // 32) ** -0.5, 0.75, ((0, 4), (1, 8))),
        "gain_ffn": jnp.clip(1.0 + 0.1 * jax.random.normal(streams_of[11], (D,), jnp.float32), 0.5, 1.5).astype(jnp.bfloat16),
        "w_router": bell_draw(streams_of[12], (D, EXPERTS), (4 * D) ** -0.5, 0.0625, ((0, 8),)),
        "w_shared_gate": bell_draw(streams_of[13], (D, SHARED_EXP * FF), D ** -0.5, 0.125, ((0, 8), (1, 4))),
        "w_shared_up": bell_draw(streams_of[14], (D, SHARED_EXP * FF), D ** -0.5, 0.125, ((0, 8), (1, 4))),
        "w_shared_down": bell_draw(streams_of[15], (SHARED_EXP * FF, D), (SHARED_EXP * FF // 4) ** -0.5, 0.21875, ((0, 4), (1, 8))),
        "w_gate": bell_draw(streams_of[16], (EXPERTS, D, FF), D ** -0.5, 0.125, ((0, 8), (2, 4))),
        "w_up": bell_draw(streams_of[17], (EXPERTS, D, FF), D ** -0.5, 0.125, ((0, 8), (2, 4))),
        "w_down": bell_draw(streams_of[18], (EXPERTS, FF, D), (FF // 8) ** -0.5, 0.4375, ((0, 8), (1, 4))),
    }


@jax.custom_vjp
def low(v):
    return lax.optimization_barrier(v.astype(jnp.bfloat16)).astype(jnp.float32)

@jax.custom_vjp
def low_back(v):
    return v

def low_keep(v):
    return (low(v), None)

def low_pass(kept, grad):
    return (grad,)

def back_keep(v):
    return (v, None)

def back_low(kept, grad):
    return (low(grad),)
low.defvjp(low_keep, low_pass)
low_back.defvjp(back_keep, back_low)
EPSILON = 1e-06
MASKED = -1e+30
HIGHEST = lax.Precision.HIGHEST

def matmul(left_side, right_side):
    return jnp.dot(left_side, right_side, precision=HIGHEST, preferred_element_type=jnp.float32)

def rms_norm(values, gain_full):
    inverse = lax.rsqrt(lax.optimization_barrier(jnp.mean(values * values, axis=-1, keepdims=True)) + EPSILON)
    return values * inverse * gain_full

def rope_tables(positions):
    half_width = QK_ROPE // 2
    frequency = jnp.power(10000.0, -jnp.arange(half_width, dtype=jnp.float32) / half_width)
    angles = positions.astype(jnp.float32)[:, None] * frequency[None, :]
    return (jnp.cos(angles), jnp.sin(angles))

def rotate(values, cosine, sine_part):
    half_width = values.shape[-1] // 2
    front_half = values[..., :half_width]
    back_half = values[..., half_width:]
    return jnp.concatenate([front_half * cosine - back_half * sine_part, back_half * cosine + front_half * sine_part], axis=-1)

def slot_layout(routes, experts, capacity):
    flat_routes = routes.reshape(-1)
    onehot = (flat_routes[:, None] == jnp.arange(experts, dtype=jnp.int32)[None, :]).astype(jnp.int32)
    before = jnp.cumsum(onehot, axis=0).astype(jnp.int32) - onehot
    slot_rank = lax.optimization_barrier(jnp.sum(before * onehot, axis=1)).astype(jnp.int32)
    route_kept = slot_rank < capacity
    slot_index = flat_routes * capacity + jnp.minimum(slot_rank, capacity - 1)
    return (slot_index.reshape(routes.shape).astype(jnp.int32), route_kept.reshape(routes.shape))

def slot_owner(slot_index, route_kept, slot_total):
    pair_count = slot_index.size
    target = jnp.where(route_kept.reshape(-1), slot_index.reshape(-1), slot_total)
    token_rows = (jnp.arange(pair_count, dtype=jnp.int32) // slot_index.shape[-1]).astype(jnp.int32)
    slot_token = jnp.zeros((slot_total,), jnp.int32).at[target].set(token_rows, mode='drop')
    slot_live = jnp.zeros((slot_total,), jnp.bool_).at[target].set(True, mode='drop')
    return (slot_token, slot_live)

def attend_block(inputs):
    query_block, key_block, value_block, seq_block = inputs
    row_count = seq_block.shape[0]
    order = jnp.arange(row_count, dtype=jnp.int32)
    allowed = (seq_block[:, None] == seq_block[None, :]) & (order[None, :] <= order[:, None])
    raw_scores = low_back(jnp.einsum('qhc,khc->hqk', query_block, key_block, precision=HIGHEST) * (QK_NOPE + QK_ROPE) ** (-0.5))
    masked = jnp.where(allowed[None], raw_scores, MASKED)
    weights = low(jax.nn.softmax(masked, axis=-1))
    return jnp.einsum('hqk,khc->qhc', weights, value_block, precision=HIGHEST)

def expert_rows(inputs):
    rows_in, gate_weight, up_weight, down_weight = inputs
    group_width = FF // N_TENSOR
    copies = low_back(jnp.broadcast_to(rows_in[None], (N_TENSOR,) + rows_in.shape))
    gate_pre = low_back(jnp.einsum('psd,dpf->psf', copies, gate_weight.reshape(D, N_TENSOR, group_width), precision=HIGHEST))
    up_pre = low_back(jnp.einsum('psd,dpf->psf', copies, up_weight.reshape(D, N_TENSOR, group_width), precision=HIGHEST))
    act_low = low(jax.nn.silu(gate_pre) * up_pre)
    parts = low(jnp.einsum('psf,pfd->psd', act_low, down_weight.reshape(N_TENSOR, group_width, D), precision=HIGHEST))
    return low_back(lax.optimization_barrier(jnp.sum(parts, axis=0)))

def layer_forward(float_args, routes, seq_ids, positions):
    tokens, gain_attn, w_query, w_latent, gain_latent, w_expand, w_output, gain_ffn, w_router, w_shared_gate, w_shared_up, w_shared_down, w_gate, w_up, w_down = float_args
    total_rows = tokens.shape[0]
    head_width = QK_NOPE + QK_ROPE
    blocks = total_rows // TOK_DEV
    cosine, sine_part = rope_tables(positions)
    normed_attn = low(rms_norm(tokens, gain_attn))
    query_raw = low_back(matmul(normed_attn, w_query)).reshape(total_rows, HEADS, head_width)
    query_all = low(jnp.concatenate([query_raw[..., :QK_NOPE], rotate(query_raw[..., QK_NOPE:], cosine[:, None, :], sine_part[:, None, :])], axis=-1))
    latent_raw = low_back(matmul(normed_attn, w_latent))
    latent_normed = low(rms_norm(latent_raw[:, :KV_RANK], gain_latent))
    key_rope = low(rotate(latent_raw[:, KV_RANK:], cosine, sine_part))
    expanded = low(low_back(matmul(latent_normed, w_expand))).reshape(total_rows, HEADS, QK_NOPE + V_HEAD)
    key_all = jnp.concatenate([expanded[..., :QK_NOPE], jnp.broadcast_to(key_rope[:, None, :], (total_rows, HEADS, QK_ROPE))], axis=-1)
    value_all = expanded[..., QK_NOPE:]
    heads_out = lax.map(jax.checkpoint(attend_block), (query_all.reshape(blocks, TOK_DEV, HEADS, head_width), key_all.reshape(blocks, TOK_DEV, HEADS, head_width), value_all.reshape(blocks, TOK_DEV, HEADS, V_HEAD), seq_ids.reshape(blocks, TOK_DEV)))
    heads_low = low(low_back(heads_out.reshape(total_rows, HEADS * V_HEAD)))
    attn_out = low_back(matmul(heads_low, w_output))
    resid_mid = tokens + attn_out
    normed_ffn = low(rms_norm(resid_mid, gain_ffn))
    logits = low_back(matmul(normed_ffn, w_router))
    router_probs = jax.nn.softmax(logits, axis=-1)
    picked = jnp.take_along_axis(router_probs, routes, axis=-1)
    gates = picked / lax.optimization_barrier(jnp.sum(picked, axis=-1, keepdims=True))
    slot_index, route_kept = jax.vmap(lambda block_routes: slot_layout(block_routes, EXPERTS, CAP))(routes.reshape(blocks, TOK_DEV, TOP))
    slot_token, slot_live = jax.vmap(lambda slot_rows, kept_rows: slot_owner(slot_rows, kept_rows, EXPERTS * CAP))(slot_index, route_kept)
    expert_in = jnp.take_along_axis(normed_ffn.reshape(blocks, TOK_DEV, D), slot_token[:, :, None], axis=1)
    expert_in = expert_in * slot_live[:, :, None].astype(jnp.float32)
    expert_in = expert_in.reshape(blocks, EXPERTS, CAP, D).transpose(1, 0, 2, 3).reshape(EXPERTS, blocks * CAP, D)
    expert_out = lax.map(jax.checkpoint(expert_rows), (expert_in, w_gate, w_up, w_down))
    expert_back = expert_out.reshape(EXPERTS, blocks, CAP, D).transpose(1, 0, 2, 3).reshape(blocks, EXPERTS * CAP, D)
    gathered = jnp.take_along_axis(expert_back, slot_index.reshape(blocks, TOK_DEV * TOP)[:, :, None], axis=1)
    gathered = gathered.reshape(total_rows, TOP, D)
    kept_gates = jnp.where(route_kept.reshape(total_rows, TOP), gates, 0.0)
    routed = lax.optimization_barrier(jnp.sum(gathered * kept_gates[:, :, None], axis=1))
    shared_gate = low_back(matmul(normed_ffn, w_shared_gate))
    shared_up = low_back(matmul(normed_ffn, w_shared_up))
    shared_act = low(jax.nn.silu(shared_gate) * shared_up)
    shared_out = matmul(shared_act, w_shared_down)
    return resid_mid + shared_out + routed

def reference(tokens, cotangent, routes, seq_ids, positions, gain_attn, w_query, w_latent, gain_latent, w_expand, w_output, gain_ffn, w_router, w_shared_gate, w_shared_up, w_shared_down, w_gate, w_up, w_down):
    given_list = (tokens, gain_attn, w_query, w_latent, gain_latent, w_expand, w_output, gain_ffn, w_router, w_shared_gate, w_shared_up, w_shared_down, w_gate, w_up, w_down)
    float_args = tuple((member.astype(jnp.float32) for member in given_list))

    def forward(float_list):
        return layer_forward(float_list, routes, seq_ids, positions)
    result, pullback = jax.vjp(forward, float_args)
    grads = pullback(cotangent.astype(jnp.float32))[0]
    return (result.astype(jnp.bfloat16), grads[0].astype(jnp.bfloat16), grads[1], grads[2], grads[3], grads[4], grads[5], grads[6], grads[7], grads[8], grads[9], grads[10], grads[11], grads[12], grads[13], grads[14])
```

```python
import jax
import jax.numpy as jnp
from jax import lax
from jax.sharding import PartitionSpec as P

QK_NOPE = 128
QK_ROPE = 64
V_HEAD = 128
KV_RANK = 512
TOP = 6


EPSILON = 1e-06
MASKED = -1e30


def norm_forward(values, gain_full):
    inverse = lax.rsqrt(jnp.mean(values * values, axis=-1, keepdims=True) + EPSILON)
    return (values * inverse * gain_full, inverse)


def norm_backward(values, inverse, gain_full, grad_out):
    normed = values * inverse
    scaled = grad_out * gain_full
    grad_in = inverse * (scaled - normed * jnp.mean(scaled * normed, axis=-1, keepdims=True))
    return (grad_in, jnp.sum(grad_out * normed, axis=0))


def rope_tables(positions, width):
    half_width = width // 2
    frequency = jnp.power(10000.0, -jnp.arange(half_width, dtype=jnp.float32) / half_width)
    angles = positions.astype(jnp.float32)[:, None] * frequency[None, :]
    return (jnp.cos(angles), jnp.sin(angles))


def rotate(values, cosine, sine_part):
    half_width = values.shape[-1] // 2
    front_half = values[..., :half_width]
    back_half = values[..., half_width:]
    return jnp.concatenate(
        [front_half * cosine - back_half * sine_part, back_half * cosine + front_half * sine_part],
        axis=-1,
    )


def slot_layout(routes, experts, capacity):
    flat_routes = routes.reshape(-1)
    onehot = (flat_routes[:, None] == jnp.arange(experts, dtype=jnp.int32)[None, :]).astype(
        jnp.int32
    )
    before = jnp.cumsum(onehot, axis=0) - onehot
    slot_rank = jnp.sum(before * onehot, axis=1)
    route_kept = slot_rank < capacity
    slot_index = flat_routes * capacity + jnp.minimum(slot_rank, capacity - 1)
    return (slot_index.reshape(routes.shape), route_kept.reshape(routes.shape))


def slot_owner(slot_index, route_kept, kept_gates, slot_total):
    pair_count = slot_index.size
    target = jnp.where(route_kept.reshape(-1), slot_index.reshape(-1), slot_total)
    token_rows = jnp.arange(pair_count, dtype=jnp.int32) // slot_index.shape[-1]
    slot_token = jnp.zeros((slot_total,), jnp.int32).at[target].set(token_rows, mode="drop")
    slot_live = jnp.zeros((slot_total,), jnp.bool_).at[target].set(True, mode="drop")
    slot_gate = (
        jnp.zeros((slot_total,), jnp.float32).at[target].set(kept_gates.reshape(-1), mode="drop")
    )
    return (slot_token, slot_live, slot_gate)


def block_scores(query_block, key_block, seq_ids, row_start):
    row_count = query_block.shape[0]
    key_count = key_block.shape[0]
    raw_scores = jnp.einsum(
        "qhc,khc->hqk", query_block, key_block, preferred_element_type=jnp.float32
    ) * (QK_NOPE + QK_ROPE) ** (-0.5)
    query_index = row_start + jnp.arange(row_count, dtype=jnp.int32)
    key_index = jnp.arange(key_count, dtype=jnp.int32)
    allowed = (seq_ids[:, None] == seq_ids[None, :]) & (key_index[None, :] <= query_index[:, None])
    return jnp.where(allowed[None], raw_scores, MASKED)


def body(
    tokens,
    cotangent,
    routes,
    seq_ids,
    positions,
    gain_attn,
    w_query,
    w_latent,
    gain_latent,
    w_expand,
    w_output,
    gain_ffn,
    w_router,
    w_shared_gate,
    w_shared_up,
    w_shared_down,
    w_gate,
    w_up,
    w_down,
):
    (
        gain_attn_all,
        query_weight,
        latent_weight,
        gain_latent_all,
        expand_weight,
        output_weight,
        gain_ffn_all,
        router_weight,
        shared_gate_weight,
        shared_up_weight,
        shared_down_weight,
    ) = (
        lax.all_gather(gain_attn, "dp", axis=0, tiled=True),
        lax.all_gather(w_query, "dp", axis=0, tiled=True),
        lax.all_gather(w_latent, "dp", axis=0, tiled=True),
        lax.all_gather(gain_latent, "dp", axis=0, tiled=True),
        lax.all_gather(w_expand, "dp", axis=0, tiled=True),
        lax.all_gather(w_output, "dp", axis=1, tiled=True),
        lax.all_gather(gain_ffn, "dp", axis=0, tiled=True),
        lax.all_gather(w_router, "dp", axis=0, tiled=True),
        lax.all_gather(w_shared_gate, "dp", axis=0, tiled=True),
        lax.all_gather(w_shared_up, "dp", axis=0, tiled=True),
        lax.all_gather(w_shared_down, "dp", axis=1, tiled=True),
    )
    tok_count = tokens.shape[0]
    head_width = QK_NOPE + QK_ROPE
    heads_here = query_weight.shape[1] // head_width
    softmax_scale = head_width ** (-0.5)
    gain_attn_f = gain_attn_all.astype(jnp.float32)
    gain_latent_f = gain_latent_all.astype(jnp.float32)
    resid_in = tokens.astype(jnp.float32)
    normed_attn, inverse_attn = norm_forward(resid_in, gain_attn_f)
    normed_attn_low = normed_attn.astype(jnp.bfloat16)
    cosine, sine_part = rope_tables(positions, QK_ROPE)
    query_raw = jnp.dot(normed_attn_low, query_weight, preferred_element_type=jnp.float32).reshape(
        tok_count, heads_here, head_width
    )
    query_low = jnp.concatenate(
        [
            query_raw[..., :QK_NOPE],
            rotate(query_raw[..., QK_NOPE:], cosine[:, None, :], sine_part[:, None, :]),
        ],
        axis=-1,
    ).astype(jnp.bfloat16)
    latent_raw = jnp.dot(normed_attn_low, latent_weight, preferred_element_type=jnp.float32)
    latent_part = latent_raw[:, :KV_RANK]
    latent_normed, inverse_latent = norm_forward(latent_part, gain_latent_f)
    latent_low = latent_normed.astype(jnp.bfloat16)
    key_rope_low = rotate(latent_raw[:, KV_RANK:], cosine, sine_part).astype(jnp.bfloat16)
    expanded = (
        jnp.dot(latent_low, expand_weight, preferred_element_type=jnp.float32)
        .astype(jnp.bfloat16)
        .reshape(tok_count, heads_here, QK_NOPE + V_HEAD)
    )
    value_low = expanded[..., QK_NOPE:]
    key_full = jnp.concatenate(
        [
            expanded[..., :QK_NOPE],
            jnp.broadcast_to(key_rope_low[:, None, :], (tok_count, heads_here, QK_ROPE)),
        ],
        axis=-1,
    )
    row_start = 0
    row_stop = row_start + tok_count
    masked = block_scores(query_low, key_full, seq_ids, row_start)
    row_max = jnp.max(masked, axis=-1, keepdims=True)
    exponent = jnp.exp(masked - row_max)
    exp_total = jnp.sum(exponent, axis=-1, keepdims=True)
    attn_probs = (exponent / exp_total).astype(jnp.bfloat16)
    log_totals = [row_max + jnp.log(exp_total)]
    head_blocks = jnp.einsum(
        "hqk,khc->qhc", attn_probs, value_low, preferred_element_type=jnp.float32
    )
    heads_low = head_blocks.astype(jnp.bfloat16).reshape(tok_count, heads_here * V_HEAD)
    attn_part = jnp.dot(heads_low, output_weight, preferred_element_type=jnp.float32)
    resid_mid = resid_in + lax.psum(attn_part, "tensor")
    gain_ffn_f = gain_ffn_all.astype(jnp.float32)
    normed_ffn, inverse_ffn = norm_forward(resid_mid, gain_ffn_f)
    normed_ffn_low = normed_ffn.astype(jnp.bfloat16)
    experts = router_weight.shape[1]
    router_probs = jax.nn.softmax(
        jnp.dot(normed_ffn_low, router_weight, preferred_element_type=jnp.float32), axis=-1
    )
    route_hits = routes[:, :, None] == jnp.arange(experts, dtype=jnp.int32)[None, None, :]
    picked = jnp.sum(jnp.where(route_hits, router_probs[:, None, :], 0.0), axis=-1)
    picked_total = jnp.sum(picked, axis=-1, keepdims=True)
    gates = picked / picked_total
    tensor_size = lax.axis_size("tensor")
    dp_size = lax.axis_size("dp")
    exp_here = w_gate.shape[0]
    model_width = tokens.shape[1]
    capacity = tensor_size * -(-(5 * tok_count * TOP) // (4 * experts * tensor_size))
    slot_index, route_kept = slot_layout(routes, experts, capacity)
    kept_gates = jnp.where(route_kept, gates, 0.0)
    kept_float = route_kept.astype(jnp.float32)
    slot_token, slot_live, slot_gate = slot_owner(
        slot_index, route_kept, kept_gates, experts * capacity
    )
    send_rows = jnp.where(
        slot_live[:, None], normed_ffn_low[slot_token], jnp.zeros((), jnp.bfloat16)
    ).reshape(dp_size, exp_here, capacity, model_width)
    grad_send = (
        (cotangent[slot_token].astype(jnp.float32) * slot_gate[:, None])
        .astype(jnp.bfloat16)
        .reshape(dp_size, exp_here, capacity, model_width)
    )
    received, grad_recv = (
        lax.all_to_all(send_rows, "dp", split_axis=0, concat_axis=0, tiled=True),
        lax.all_to_all(grad_send, "dp", split_axis=0, concat_axis=0, tiled=True),
    )
    gate_pre = jnp.einsum("secd,edf->secf", received, w_gate, preferred_element_type=jnp.float32)
    up_pre = jnp.einsum("secd,edf->secf", received, w_up, preferred_element_type=jnp.float32)
    gate_sigmoid = jax.nn.sigmoid(gate_pre)
    gate_silu = gate_pre * gate_sigmoid
    expert_act = (gate_silu * up_pre).astype(jnp.bfloat16)
    expert_out = jnp.einsum(
        "secf,efd->secd", expert_act, w_down, preferred_element_type=jnp.float32
    ).astype(jnp.bfloat16)
    returned = lax.all_to_all(expert_out, "dp", split_axis=0, concat_axis=0, tiled=True).reshape(
        experts * capacity, model_width
    )
    gathered = returned[slot_index].astype(jnp.float32)
    routed_part = jnp.sum(gathered * kept_gates[:, :, None], axis=1)
    shared_gate = jnp.dot(normed_ffn_low, shared_gate_weight, preferred_element_type=jnp.float32)
    shared_up = jnp.dot(normed_ffn_low, shared_up_weight, preferred_element_type=jnp.float32)
    shared_sigmoid = jax.nn.sigmoid(shared_gate)
    shared_silu = shared_gate * shared_sigmoid
    shared_act = (shared_silu * shared_up).astype(jnp.bfloat16)
    shared_part = jnp.dot(shared_act, shared_down_weight, preferred_element_type=jnp.float32)
    moe_total = lax.psum((routed_part + shared_part).astype(jnp.bfloat16), "tensor").astype(
        jnp.float32
    )
    result = (resid_mid + moe_total).astype(jnp.bfloat16)
    cot_float = cotangent.astype(jnp.float32)
    act_grad = jnp.einsum("secd,efd->secf", grad_recv, w_down, preferred_element_type=jnp.float32)
    w_down_grad = jnp.einsum(
        "secf,secd->efd", expert_act, grad_recv, preferred_element_type=jnp.float32
    )
    gate_grad = (act_grad * up_pre * gate_sigmoid * (1.0 + gate_pre * (1.0 - gate_sigmoid))).astype(
        jnp.bfloat16
    )
    up_grad = (act_grad * gate_silu).astype(jnp.bfloat16)
    w_gate_grad = jnp.einsum(
        "secd,secf->edf", received, gate_grad, preferred_element_type=jnp.float32
    )
    w_up_grad = jnp.einsum("secd,secf->edf", received, up_grad, preferred_element_type=jnp.float32)
    rows_grad = (
        jnp.einsum("secf,edf->secd", gate_grad, w_gate, preferred_element_type=jnp.float32)
        + jnp.einsum("secf,edf->secd", up_grad, w_up, preferred_element_type=jnp.float32)
    ).astype(jnp.bfloat16)
    grad_back = lax.all_to_all(rows_grad, "dp", split_axis=0, concat_axis=0, tiled=True).reshape(
        experts * capacity, model_width
    )
    routed_in_grad = jnp.sum(
        grad_back[slot_index].astype(jnp.float32) * kept_float[:, :, None], axis=1
    )
    gate_grad_part = jnp.sum(gathered * cot_float[:, None, :], axis=-1) * kept_float
    shared_act_grad = jnp.einsum(
        "td,fd->tf", cotangent, shared_down_weight, preferred_element_type=jnp.float32
    )
    shared_down_grad = jnp.einsum(
        "tf,td->fd", shared_act, cotangent, preferred_element_type=jnp.float32
    )
    shared_gate_grad = (
        shared_act_grad * shared_up * shared_sigmoid * (1.0 + shared_gate * (1.0 - shared_sigmoid))
    ).astype(jnp.bfloat16)
    shared_up_grad = (shared_act_grad * shared_silu).astype(jnp.bfloat16)
    shared_gate_weight_grad = jnp.einsum(
        "td,tf->df", normed_ffn_low, shared_gate_grad, preferred_element_type=jnp.float32
    )
    shared_up_weight_grad = jnp.einsum(
        "td,tf->df", normed_ffn_low, shared_up_grad, preferred_element_type=jnp.float32
    )
    shared_in_grad = jnp.einsum(
        "tf,df->td", shared_gate_grad, shared_gate_weight, preferred_element_type=jnp.float32
    ) + jnp.einsum(
        "tf,df->td", shared_up_grad, shared_up_weight, preferred_element_type=jnp.float32
    )
    ffn_in_sum, gate_grad_sum = lax.psum(
        (routed_in_grad + shared_in_grad, gate_grad_part), "tensor"
    )
    picked_grad = (
        gate_grad_sum - jnp.sum(gate_grad_sum * gates, axis=-1, keepdims=True)
    ) / picked_total
    probs_grad = jnp.sum(jnp.where(route_hits, picked_grad[:, :, None], 0.0), axis=1)
    logit_grad = (
        router_probs * (probs_grad - jnp.sum(router_probs * probs_grad, axis=-1, keepdims=True))
    ).astype(jnp.bfloat16)
    router_grad = jnp.einsum(
        "td,te->de", normed_ffn_low, logit_grad, preferred_element_type=jnp.float32
    )
    ffn_in = ffn_in_sum + jnp.einsum(
        "te,de->td", logit_grad, router_weight, preferred_element_type=jnp.float32
    )
    ffn_resid_grad, gain_ffn_grad = norm_backward(resid_mid, inverse_ffn, gain_ffn_f, ffn_in)
    mid_grad = cot_float + ffn_resid_grad
    mid_low = mid_grad.astype(jnp.bfloat16)
    output_weight_grad = jnp.einsum(
        "th,td->hd", heads_low, mid_low, preferred_element_type=jnp.float32
    )
    heads_grad = (
        jnp.einsum("td,hd->th", mid_low, output_weight, preferred_element_type=jnp.float32)
        .astype(jnp.bfloat16)
        .reshape(tok_count, heads_here, V_HEAD)
    )
    query_grad_blocks = []
    key_grad = jnp.zeros((tok_count, heads_here, head_width), jnp.float32)
    value_grad = jnp.zeros((tok_count, heads_here, V_HEAD), jnp.float32)
    for block_number, row_start in enumerate(range(0, tok_count, tok_count)):
        row_stop = row_start + tok_count
        masked = block_scores(query_low, key_full, seq_ids, row_start)
        attn_probs = jnp.exp(masked - log_totals[block_number])
        probs_low = attn_probs.astype(jnp.bfloat16)
        prob_grad = jnp.einsum(
            "qhc,khc->hqk", heads_grad, value_low, preferred_element_type=jnp.float32
        )
        row_dot = jnp.sum(attn_probs * prob_grad, axis=-1, keepdims=True)
        score_grad = (attn_probs * (prob_grad - row_dot)).astype(jnp.bfloat16)
        query_grad_blocks.append(
            jnp.einsum("hqk,khc->qhc", score_grad, key_full, preferred_element_type=jnp.float32)
            * softmax_scale
        )
        key_grad = key_grad.at[:row_stop].add(
            jnp.einsum("hqk,qhc->khc", score_grad, query_low, preferred_element_type=jnp.float32)
            * softmax_scale
        )
        value_grad = value_grad.at[:row_stop].add(
            jnp.einsum("hqk,qhc->khc", probs_low, heads_grad, preferred_element_type=jnp.float32)
        )
    query_grad = query_grad_blocks[0]
    query_pre_grad = jnp.concatenate(
        [
            query_grad[..., :QK_NOPE],
            rotate(query_grad[..., QK_NOPE:], cosine[:, None, :], -sine_part[:, None, :]),
        ],
        axis=-1,
    )
    query_pre_grad = query_pre_grad.astype(jnp.bfloat16).reshape(tok_count, heads_here * head_width)
    attn_in_part = jnp.einsum(
        "tq,dq->td", query_pre_grad, query_weight, preferred_element_type=jnp.float32
    )
    query_weight_grad = jnp.einsum(
        "td,tq->dq", normed_attn_low, query_pre_grad, preferred_element_type=jnp.float32
    )
    expand_grad = (
        jnp.concatenate([key_grad[..., :QK_NOPE], value_grad], axis=-1)
        .astype(jnp.bfloat16)
        .reshape(tok_count, heads_here * (QK_NOPE + V_HEAD))
    )
    latent_part_grad = jnp.einsum(
        "te,re->tr", expand_grad, expand_weight, preferred_element_type=jnp.float32
    )
    expand_weight_grad = jnp.einsum(
        "tr,te->re", latent_low, expand_grad, preferred_element_type=jnp.float32
    )
    rope_part_grad = jnp.sum(key_grad[..., QK_NOPE:], axis=1)
    attn_in_sum, latent_sum, rope_sum = lax.psum(
        (attn_in_part, latent_part_grad, rope_part_grad), "tensor"
    )
    latent_pre_grad, gain_latent_grad = norm_backward(
        latent_part, inverse_latent, gain_latent_f, latent_sum
    )
    latent_all_grad = jnp.concatenate(
        [latent_pre_grad, rotate(rope_sum, cosine, -sine_part)], axis=-1
    ).astype(jnp.bfloat16)
    attn_in = attn_in_sum + jnp.einsum(
        "tc,dc->td", latent_all_grad, latent_weight, preferred_element_type=jnp.float32
    )
    latent_weight_grad = jnp.einsum(
        "td,tc->dc", normed_attn_low, latent_all_grad, preferred_element_type=jnp.float32
    )
    input_grad, gain_attn_grad = norm_backward(resid_in, inverse_attn, gain_attn_f, attn_in)
    tokens_grad = (mid_grad + input_grad).astype(jnp.bfloat16)
    (
        gain_attn_share,
        query_share,
        latent_share,
        gain_latent_share,
        expand_share,
        output_share,
        gain_ffn_share,
        router_share,
        shared_gate_share,
        shared_up_share,
        shared_down_share,
    ) = (
        lax.psum_scatter(
            gain_attn_grad.astype(jnp.bfloat16), "dp", scatter_dimension=0, tiled=True
        ).astype(jnp.float32),
        lax.psum_scatter(
            query_weight_grad.astype(jnp.bfloat16), "dp", scatter_dimension=0, tiled=True
        ).astype(jnp.float32),
        lax.psum_scatter(
            latent_weight_grad.astype(jnp.bfloat16), "dp", scatter_dimension=0, tiled=True
        ).astype(jnp.float32),
        lax.psum_scatter(
            gain_latent_grad.astype(jnp.bfloat16), "dp", scatter_dimension=0, tiled=True
        ).astype(jnp.float32),
        lax.psum_scatter(
            expand_weight_grad.astype(jnp.bfloat16), "dp", scatter_dimension=0, tiled=True
        ).astype(jnp.float32),
        lax.psum_scatter(
            output_weight_grad.astype(jnp.bfloat16), "dp", scatter_dimension=1, tiled=True
        ).astype(jnp.float32),
        lax.psum_scatter(
            gain_ffn_grad.astype(jnp.bfloat16), "dp", scatter_dimension=0, tiled=True
        ).astype(jnp.float32),
        lax.psum_scatter(
            router_grad.astype(jnp.bfloat16), "dp", scatter_dimension=0, tiled=True
        ).astype(jnp.float32),
        lax.psum_scatter(
            shared_gate_weight_grad.astype(jnp.bfloat16), "dp", scatter_dimension=0, tiled=True
        ).astype(jnp.float32),
        lax.psum_scatter(
            shared_up_weight_grad.astype(jnp.bfloat16), "dp", scatter_dimension=0, tiled=True
        ).astype(jnp.float32),
        lax.psum_scatter(
            shared_down_grad.astype(jnp.bfloat16), "dp", scatter_dimension=1, tiled=True
        ).astype(jnp.float32),
    )
    return (
        result,
        tokens_grad,
        gain_attn_share,
        query_share,
        latent_share,
        gain_latent_share,
        expand_share,
        output_share,
        gain_ffn_share,
        router_share,
        shared_gate_share,
        shared_up_share,
        shared_down_share,
        w_gate_grad,
        w_up_grad,
        w_down_grad,
    )

def hop(values, axis, bit):
    return lax.ppermute(values, axis, [(i, i ^ bit) for i in range(lax.axis_size(axis))])


def core_hop(values):
    return hop(values, "tensor", 1)


def y_hop(values):
    return hop(values, "tensor", 2)


def x_hop(values):
    return hop(values, "dp", 1)


def z_hop(values):
    count = lax.axis_size("dp")
    return lax.ppermute(values, "dp", [(i, (i + 2) % count) for i in range(count)])


def low(values):
    return values.astype(jnp.bfloat16)


def plane_gather(own):
    half = own.shape[0] // 2
    first, second = own[:half], own[half:]
    first_x = x_hop(first)
    second_y = y_hop(second)
    first_pair = jnp.concatenate([first, first_x])
    second_pair = jnp.concatenate([second, second_y])
    first_y = y_hop(first_pair)
    second_x = x_hop(second_pair)
    parts = [
        first,
        second,
        first_x,
        second_x[:half],
        first_y[:half],
        second_y,
        first_y[half:],
        second_x[half:],
    ]
    quarter = jnp.concatenate(parts)
    return quarter, core_hop(quarter)


def slice_gather(own):
    chunks = []
    piece = own
    planes = lax.axis_size("dp") // 2
    for step in range(planes):
        chunks.append(plane_gather(piece))
        if step + 1 < planes:
            piece = z_hop(piece)
    return chunks


def plane_scatter(part):
    received = core_hop(part[1])
    total = part[0].astype(jnp.float32) + received.astype(jnp.float32)
    first, second = total[:, :, 0], total[:, :, 1]
    first_in = y_hop(low(first[1])).astype(jnp.float32)
    second_in = x_hop(low(second[:, 1])).astype(jnp.float32)
    first_near = first[0] + first_in
    second_near = second[:, 0] + second_in
    first_in = x_hop(low(first_near[1])).astype(jnp.float32)
    second_in = y_hop(low(second_near[1])).astype(jnp.float32)
    return jnp.concatenate([first_near[0] + first_in, second_near[0] + second_in])


def slice_scatter(parts):
    own = parts[0].shape[0] // 8
    width = parts[0].shape[1]
    pieces = [plane_scatter(part.reshape(2, 2, 2, 2, own // 2, width)) for part in parts]
    moving = pieces[1]
    for piece in pieces[2:] + pieces[:1]:
        moving = piece + z_hop(low(moving)).astype(jnp.float32)
    return moving


def tensor_scatter(values, tensor_index):
    rows = values.shape[0] // 4
    width = values.shape[1]
    core = tensor_index % 2
    level = tensor_index // 2
    blocks = values.reshape(2, 2, rows, width)
    mine = lax.dynamic_index_in_dim(blocks, core, 1, keepdims=False)
    other = lax.dynamic_index_in_dim(blocks, 1 - core, 1, keepdims=False)
    total = mine.astype(jnp.float32) + core_hop(low(other)).astype(jnp.float32)
    near = lax.dynamic_index_in_dim(total, level, 0, keepdims=False)
    far = lax.dynamic_index_in_dim(total, 1 - level, 0, keepdims=False)
    return near + y_hop(low(far)).astype(jnp.float32)


def tensor_gather(own, tensor_index):
    own_y = y_hop(own)
    pair = jnp.stack([own, own_y])
    pair_core = core_hop(pair)
    core = tensor_index % 2
    level = tensor_index // 2
    even = jnp.where(core == 0, pair, pair_core)
    odd = jnp.where(core == 0, pair_core, pair)
    near = jnp.concatenate([even[0], odd[0]])
    far = jnp.concatenate([even[1], odd[1]])
    return jnp.concatenate(
        [jnp.where(level == 0, near, far), jnp.where(level == 0, far, near)]
    )


def padded(values, axis, size):
    pads = [(0, 0)] * values.ndim
    pads[axis] = (0, size - values.shape[axis])
    return jnp.pad(values, pads)


def lanes(size):
    return -(-size // 128) * 128


def body_dense(
    tokens,
    cotangent,
    routes,
    seq_ids,
    positions,
    gain_attn,
    w_query,
    w_latent,
    gain_latent,
    w_expand,
    w_output,
    gain_ffn,
    w_router,
    w_shared_gate,
    w_shared_up,
    w_shared_down,
    w_gate,
    w_up,
    w_down,
):
    tensor_size = lax.axis_size("tensor")
    dp_size = lax.axis_size("dp")
    dp_index = lax.axis_index("dp")
    tensor_index = lax.axis_index("tensor")
    tok_count, width = tokens.shape
    own_count = tok_count // tensor_size
    own_start = tensor_index * own_count
    experts = w_router.shape[1]
    exp_here = w_gate.shape[0]
    capacity = tensor_size * -(-(5 * tok_count * TOP) // (4 * experts * tensor_size))

    def own_rows(values):
        return lax.dynamic_slice_in_dim(values, own_start, own_count, 0)

    lat_width = w_latent.shape[1]
    lat_rows = w_latent.shape[0] // tensor_size
    lat_piece = lax.dynamic_slice_in_dim(w_latent, tensor_index * lat_rows, lat_rows, 0)
    gains = jnp.concatenate([gain_attn, gain_ffn, gain_latent])[None]
    gain_rows = gain_attn.shape[0]
    router_piece = lax.dynamic_slice_in_dim(
        w_router, tensor_index * lat_rows, lat_rows, 0
    ).reshape(2, lat_rows * experts // 2)
    pack = jnp.concatenate([lat_piece, gains, padded(router_piece, 1, lat_width)])
    pack_rows = -(-pack.shape[0] // 8) * 8
    packed = lax.all_gather(padded(pack, 0, pack_rows), ("dp", "tensor"), axis=0, tiled=False)
    latent_weight = packed[:, :lat_rows].reshape(width, lat_width)
    gains_all = packed[::tensor_size, lat_rows].astype(jnp.float32)
    gain_attn_f = gains_all[:, :gain_rows].reshape(width)
    gain_ffn_f = gains_all[:, gain_rows : 2 * gain_rows].reshape(width)
    gain_latent_f = gains_all[:, 2 * gain_rows :].reshape(KV_RANK)
    router_weight = packed[:, lat_rows + 1 : lat_rows + 3, : router_piece.shape[1]].reshape(
        width, experts
    )

    query_weight = lax.all_gather(w_query, "dp", axis=0, tiled=True)
    expand_weight = lax.all_gather(w_expand, "dp", axis=0, tiled=True)
    output_weight = lax.all_gather(w_output, "dp", axis=1, tiled=True)

    routed = jnp.sum(
        (routes[:, :, None] == jnp.arange(experts, dtype=jnp.int32)[None, None, :]).astype(
            jnp.float32
        ),
        axis=1,
    )
    order = jnp.arange(tok_count, dtype=jnp.int32)
    earlier = (order[None, :] < order[:, None]).astype(jnp.bfloat16)
    rank = jnp.dot(earlier, low(routed), preferred_element_type=jnp.float32)
    standing = routed * (1.0 + (rank < capacity).astype(jnp.float32))
    cot_own = own_rows(cotangent)
    standing_own = own_rows(standing)
    cot_sent = jnp.concatenate([cot_own, padded(low(standing_own), 1, 128)], axis=1)
    cot_chunks = slice_gather(cot_sent)

    shared_here = w_shared_gate.shape[1] // dp_size
    shared_in = lax.all_to_all(
        jnp.stack([w_shared_gate, w_shared_up]), "dp", split_axis=2, concat_axis=1, tiled=True
    )
    shared_out = lax.all_to_all(w_shared_down, "dp", split_axis=0, concat_axis=1, tiled=True)
    group = w_gate.shape[2]
    group_lanes = lanes(group)
    shared_lanes = lanes(shared_here)

    def joined(routed_weight, shared_weight, axis):
        pieces = [padded(routed_weight[e], axis, group_lanes) for e in range(exp_here)]
        return jnp.concatenate(pieces + [padded(shared_weight, axis, shared_lanes)], axis=axis)

    gate_weight = joined(w_gate, shared_in[0], 1)
    up_weight = joined(w_up, shared_in[1], 1)
    down_weight = joined(w_down, shared_out, 0)
    hidden = gate_weight.shape[1]

    head_width = QK_NOPE + QK_ROPE
    heads_here = query_weight.shape[1] // head_width
    softmax_scale = head_width ** (-0.5)
    resid_in = tokens.astype(jnp.float32)
    normed_attn, inverse_attn = norm_forward(resid_in, gain_attn_f)
    normed_attn_low = low(normed_attn)
    cosine, sine_part = rope_tables(positions, QK_ROPE)
    query_raw = jnp.dot(normed_attn_low, query_weight, preferred_element_type=jnp.float32).reshape(
        tok_count, heads_here, head_width
    )
    query_low = low(
        jnp.concatenate(
            [
                query_raw[..., :QK_NOPE],
                rotate(query_raw[..., QK_NOPE:], cosine[:, None, :], sine_part[:, None, :]),
            ],
            axis=-1,
        )
    )
    latent_raw = jnp.dot(normed_attn_low, latent_weight, preferred_element_type=jnp.float32)
    latent_part = latent_raw[:, :KV_RANK]
    latent_normed, inverse_latent = norm_forward(latent_part, gain_latent_f)
    latent_low = low(latent_normed)
    key_rope_low = low(rotate(latent_raw[:, KV_RANK:], cosine, sine_part))
    expanded = low(
        jnp.dot(latent_low, expand_weight, preferred_element_type=jnp.float32)
    ).reshape(tok_count, heads_here, QK_NOPE + V_HEAD)
    value_low = expanded[..., QK_NOPE:]
    key_full = jnp.concatenate(
        [
            expanded[..., :QK_NOPE],
            jnp.broadcast_to(key_rope_low[:, None, :], (tok_count, heads_here, QK_ROPE)),
        ],
        axis=-1,
    )
    masked = block_scores(query_low, key_full, seq_ids, 0)
    row_max = jnp.max(masked, axis=-1, keepdims=True)
    exponent = jnp.exp(masked - row_max)
    exp_total = jnp.sum(exponent, axis=-1, keepdims=True)
    probs_low = low(exponent / exp_total)
    log_total = row_max + jnp.log(exp_total)
    heads_low = low(
        jnp.einsum("hqk,khc->qhc", probs_low, value_low, preferred_element_type=jnp.float32)
    ).reshape(tok_count, heads_here * V_HEAD)
    attn_part = jnp.dot(heads_low, output_weight, preferred_element_type=jnp.float32)

    resid_own = own_rows(tokens).astype(jnp.float32) + tensor_scatter(attn_part, tensor_index)
    normed_own, inverse_own = norm_forward(resid_own, gain_ffn_f)
    normed_own_low = low(normed_own)
    row_chunks = slice_gather(normed_own_low)

    def gating(rows, standing_rows):
        probs = jax.nn.softmax(
            jnp.dot(rows, router_weight, preferred_element_type=jnp.float32), axis=-1
        )
        gates = jnp.where(standing_rows > 0.5, probs, 0.0)
        picked = jnp.sum(gates, axis=-1, keepdims=True)
        return probs, gates / picked, picked

    expert_index = jnp.arange(experts, dtype=jnp.int32)[None, :]
    column = jnp.arange(hidden, dtype=jnp.int32)[None, :]
    out_parts, in_parts, gate_parts = [], [], []
    gate_weight_grad = up_weight_grad = down_weight_grad = 0.0
    for (near_rows, far_rows), (near_cot, far_cot) in zip(row_chunks, cot_chunks):
        rows = jnp.concatenate([near_rows, far_rows])
        cots = jnp.concatenate([near_cot[:, :width], far_cot[:, :width]])
        marks = jnp.concatenate(
            [near_cot[:, width : width + experts], far_cot[:, width : width + experts]]
        ).astype(jnp.float32)
        _, chunk_gates, _ = gating(rows, marks)
        chunk_gates = jnp.where(marks > 1.5, chunk_gates, 0.0)
        scale = jnp.ones((rows.shape[0], hidden), jnp.float32)
        for e in reversed(range(exp_here)):
            here = expert_index == dp_index * exp_here + e
            gate_column = jnp.sum(jnp.where(here, chunk_gates, 0.0), axis=-1, keepdims=True)
            scale = jnp.where(column < (e + 1) * group_lanes, gate_column, scale)
        gate_pre = jnp.dot(rows, gate_weight, preferred_element_type=jnp.float32)
        up_pre = jnp.dot(rows, up_weight, preferred_element_type=jnp.float32)
        sigmoid = jax.nn.sigmoid(gate_pre)
        silu = gate_pre * sigmoid
        act = silu * up_pre
        act_scaled = low(act * scale)
        out_parts.append(
            low(jnp.dot(act_scaled, down_weight, preferred_element_type=jnp.float32))
        )
        act_grad = jnp.einsum("td,fd->tf", cots, down_weight, preferred_element_type=jnp.float32)
        meeting = act * act_grad
        gate_parts.append(
            jnp.stack(
                [
                    jnp.sum(meeting[:, e * group_lanes : (e + 1) * group_lanes], axis=-1)
                    for e in range(exp_here)
                ]
            )
        )
        scaled_grad = act_grad * scale
        gate_grad = low(scaled_grad * up_pre * sigmoid * (1.0 + gate_pre * (1.0 - sigmoid)))
        up_grad = low(scaled_grad * silu)
        in_parts.append(
            low(
                jnp.einsum("tf,df->td", gate_grad, gate_weight, preferred_element_type=jnp.float32)
                + jnp.einsum("tf,df->td", up_grad, up_weight, preferred_element_type=jnp.float32)
            )
        )
        gate_weight_grad += jnp.einsum(
            "td,tf->df", rows, gate_grad, preferred_element_type=jnp.float32
        )
        up_weight_grad += jnp.einsum("td,tf->df", rows, up_grad, preferred_element_type=jnp.float32)
        down_weight_grad += jnp.einsum(
            "tf,td->fd", act_scaled, cots, preferred_element_type=jnp.float32
        )

    ffn_sum = slice_scatter(in_parts)
    gate_sums = jnp.stack(gate_parts).reshape(-1, exp_here, 2, 2, 2, own_count)
    gate_sums = gate_sums[:, :, 0] + core_hop(gate_sums[:, :, 1])
    gate_sums = gate_sums[:, :, 0] + y_hop(gate_sums[:, :, 1])
    planes = dp_size // 2
    block = jnp.arange(dp_size, dtype=jnp.int32)
    place = ((dp_index // 2 - block // 2) % planes) * 2 + (block + dp_index) % 2
    gate_sums = gate_sums.transpose(0, 2, 1, 3).reshape(dp_size, exp_here, own_count)[place]
    gate_sums = lax.all_to_all(gate_sums, "dp", split_axis=0, concat_axis=0, tiled=True)
    gate_sums = gate_sums.reshape(experts, own_count).T

    probs_own, gates_own, picked_own = gating(normed_own_low, standing_own)
    gate_sums = jnp.where(standing_own > 1.5, gate_sums, 0.0)
    picked_grad = (
        gate_sums - jnp.sum(gate_sums * gates_own, axis=-1, keepdims=True)
    ) / picked_own
    probs_grad = jnp.where(standing_own > 0.5, picked_grad, 0.0)
    logit_grad = low(
        probs_own * (probs_grad - jnp.sum(probs_own * probs_grad, axis=-1, keepdims=True))
    )
    router_grad = jnp.einsum(
        "td,te->de", normed_own_low, logit_grad, preferred_element_type=jnp.float32
    )
    ffn_in = ffn_sum + jnp.einsum(
        "te,de->td", logit_grad, router_weight, preferred_element_type=jnp.float32
    )
    ffn_resid_grad, gain_ffn_grad = norm_backward(resid_own, inverse_own, gain_ffn_f, ffn_in)
    mid_grad_own = cot_own.astype(jnp.float32) + ffn_resid_grad
    mid_low = tensor_gather(low(mid_grad_own), tensor_index)

    output_weight_grad = jnp.einsum(
        "th,td->hd", heads_low, mid_low, preferred_element_type=jnp.float32
    )
    heads_grad = low(
        jnp.einsum("td,hd->th", mid_low, output_weight, preferred_element_type=jnp.float32)
    ).reshape(tok_count, heads_here, V_HEAD)
    masked = block_scores(query_low, key_full, seq_ids, 0)
    attn_probs = jnp.exp(masked - log_total)
    prob_grad = jnp.einsum("qhc,khc->hqk", heads_grad, value_low, preferred_element_type=jnp.float32)
    row_dot = jnp.sum(attn_probs * prob_grad, axis=-1, keepdims=True)
    score_grad = low(attn_probs * (prob_grad - row_dot))
    query_grad = (
        jnp.einsum("hqk,khc->qhc", score_grad, key_full, preferred_element_type=jnp.float32)
        * softmax_scale
    )
    key_grad = (
        jnp.einsum("hqk,qhc->khc", score_grad, query_low, preferred_element_type=jnp.float32)
        * softmax_scale
    )
    value_grad = jnp.einsum(
        "hqk,qhc->khc", low(attn_probs), heads_grad, preferred_element_type=jnp.float32
    )
    query_pre_grad = low(
        jnp.concatenate(
            [
                query_grad[..., :QK_NOPE],
                rotate(query_grad[..., QK_NOPE:], cosine[:, None, :], -sine_part[:, None, :]),
            ],
            axis=-1,
        )
    ).reshape(tok_count, heads_here * head_width)
    query_weight_grad = jnp.einsum(
        "td,tq->dq", normed_attn_low, query_pre_grad, preferred_element_type=jnp.float32
    )
    expand_grad = low(jnp.concatenate([key_grad[..., :QK_NOPE], value_grad], axis=-1)).reshape(
        tok_count, heads_here * (QK_NOPE + V_HEAD)
    )
    latent_grad = jnp.einsum(
        "te,re->tr", expand_grad, expand_weight, preferred_element_type=jnp.float32
    )
    expand_weight_grad = jnp.einsum(
        "tr,te->re", latent_low, expand_grad, preferred_element_type=jnp.float32
    )
    rope_grad = jnp.sum(key_grad[..., QK_NOPE:], axis=1)
    latent_pre_grad, gain_latent_grad = norm_backward(
        latent_part, inverse_latent, gain_latent_f, latent_grad
    )
    latent_all_grad = low(
        jnp.concatenate([latent_pre_grad, rotate(rope_grad, cosine, -sine_part)], axis=-1)
    )
    attn_in = jnp.einsum(
        "tq,dq->td", query_pre_grad, query_weight, preferred_element_type=jnp.float32
    ) + jnp.einsum("tc,dc->td", latent_all_grad, latent_weight, preferred_element_type=jnp.float32)
    latent_weight_grad = jnp.einsum(
        "td,tc->dc", normed_attn_low, latent_all_grad, preferred_element_type=jnp.float32
    )
    gain_attn_grad = jnp.sum(attn_in * (resid_in * inverse_attn), axis=0)
    attn_in_own = tensor_scatter(attn_in, tensor_index)
    input_grad, _ = norm_backward(
        own_rows(resid_in), own_rows(inverse_attn), gain_attn_f, attn_in_own
    )
    tokens_grad = tensor_gather(low(mid_grad_own + input_grad), tensor_index)

    out_sum = slice_scatter(out_parts)
    result = tensor_gather(low(resid_own + out_sum), tensor_index)

    def scattered(values, dimension):
        return lax.psum_scatter(
            low(values), "dp", scatter_dimension=dimension, tiled=True
        ).astype(jnp.float32)

    output_share = scattered(output_weight_grad, 1)
    query_share = scattered(query_weight_grad, 0)
    expand_share = scattered(expand_weight_grad, 0)

    gain_shares = jnp.concatenate(
        [
            gain_attn_grad.reshape(dp_size, -1),
            gain_ffn_grad.reshape(dp_size, -1),
            gain_latent_grad.reshape(dp_size, -1),
        ],
        axis=1,
    )[:, None]
    router_lanes = 512
    router_rows = router_grad.reshape(dp_size, -1, router_lanes)
    lat_block = w_latent.shape[0]
    grad_pack = jnp.concatenate(
        [
            low(latent_weight_grad).reshape(dp_size, lat_block, lat_width),
            low(gain_shares),
            padded(low(router_rows), 2, lat_width),
        ],
        axis=1,
    )
    unit = 8 * tensor_size
    grad_rows = -(-grad_pack.shape[1] // unit) * unit
    grad_pack = padded(grad_pack, 1, grad_rows).reshape(dp_size * grad_rows, lat_width)
    grad_piece = lax.psum_scatter(grad_pack, ("dp", "tensor"), scatter_dimension=0, tiled=True)
    grad_full = tensor_gather(grad_piece, tensor_index).astype(jnp.float32)
    latent_share = grad_full[:lat_block]
    gain_row = grad_full[lat_block]
    gain_attn_share = gain_row[:gain_rows]
    gain_ffn_share = gain_row[gain_rows : 2 * gain_rows]
    gain_latent_share = gain_row[2 * gain_rows :]
    router_share = grad_full[
        lat_block + 1 : lat_block + 1 + router_rows.shape[1], :router_lanes
    ].reshape(lat_block, experts)

    def routed_grad(grad, axis):
        return jnp.stack(
            [
                lax.slice_in_dim(grad, e * group_lanes, e * group_lanes + group, axis=axis)
                for e in range(exp_here)
            ]
        )

    def shared_grad(grad, axis):
        start = exp_here * group_lanes
        return low(lax.slice_in_dim(grad, start, start + shared_here, axis=axis))

    shared_in_grad = lax.all_to_all(
        jnp.stack([shared_grad(gate_weight_grad, 1), shared_grad(up_weight_grad, 1)]),
        "dp",
        split_axis=1,
        concat_axis=2,
        tiled=True,
    ).astype(jnp.float32)
    shared_down_share = lax.all_to_all(
        shared_grad(down_weight_grad, 0), "dp", split_axis=1, concat_axis=0, tiled=True
    ).astype(jnp.float32)

    return (
        result,
        tokens_grad,
        gain_attn_share,
        query_share,
        latent_share,
        gain_latent_share,
        expand_share,
        output_share,
        gain_ffn_share,
        router_share,
        shared_in_grad[0],
        shared_in_grad[1],
        shared_down_share,
        routed_grad(gate_weight_grad, 1),
        routed_grad(up_weight_grad, 1),
        routed_grad(down_weight_grad, 0),
    )


def solution(mesh):
    dense = mesh.shape["dp"] == 8 and mesh.shape["tensor"] == 4
    return jax.shard_map(
        body_dense if dense else body,
        mesh=mesh,
        in_specs=(
            P("dp", None),
            P("dp", None),
            P("dp", None),
            P("dp"),
            P("dp"),
            P("dp"),
            P("dp", "tensor"),
            P("dp", None),
            P("dp"),
            P("dp", "tensor"),
            P("tensor", "dp"),
            P("dp"),
            P("dp", None),
            P("dp", "tensor"),
            P("dp", "tensor"),
            P("tensor", "dp"),
            P("dp", None, "tensor"),
            P("dp", None, "tensor"),
            P("dp", "tensor", None),
        ),
        out_specs=(
            P("dp", None),
            P("dp", None),
            P("dp"),
            P("dp", "tensor"),
            P("dp", None),
            P("dp"),
            P("dp", "tensor"),
            P("tensor", "dp"),
            P("dp"),
            P("dp", None),
            P("dp", "tensor"),
            P("dp", "tensor"),
            P("tensor", "dp"),
            P("dp", None, "tensor"),
            P("dp", None, "tensor"),
            P("dp", "tensor", None),
        ),
        check_vma=False,
    )
```

```python
import jax
import jax.numpy as jnp
from jax import lax
from jax.sharding import PartitionSpec as P

QK_NOPE = 128
QK_ROPE = 64
V_HEAD = 128
KV_RANK = 512
TOP = 6


EPSILON = 1e-06
MASKED = -1e30


def norm_forward(values, gain_full):
    inverse = lax.rsqrt(jnp.mean(values * values, axis=-1, keepdims=True) + EPSILON)
    return (values * inverse * gain_full, inverse)


def norm_backward(values, inverse, gain_full, grad_out):
    normed = values * inverse
    scaled = grad_out * gain_full
    grad_in = inverse * (scaled - normed * jnp.mean(scaled * normed, axis=-1, keepdims=True))
    return (grad_in, jnp.sum(grad_out * normed, axis=0))


def rope_tables(positions, width):
    half_width = width // 2
    frequency = jnp.power(10000.0, -jnp.arange(half_width, dtype=jnp.float32) / half_width)
    angles = positions.astype(jnp.float32)[:, None] * frequency[None, :]
    return (jnp.cos(angles), jnp.sin(angles))


def rotate(values, cosine, sine_part):
    half_width = values.shape[-1] // 2
    front_half = values[..., :half_width]
    back_half = values[..., half_width:]
    return jnp.concatenate(
        [front_half * cosine - back_half * sine_part, back_half * cosine + front_half * sine_part],
        axis=-1,
    )


def slot_layout(routes, experts, capacity):
    flat_routes = routes.reshape(-1)
    onehot = (flat_routes[:, None] == jnp.arange(experts, dtype=jnp.int32)[None, :]).astype(
        jnp.int32
    )
    before = jnp.cumsum(onehot, axis=0) - onehot
    slot_rank = jnp.sum(before * onehot, axis=1)
    route_kept = slot_rank < capacity
    slot_index = flat_routes * capacity + jnp.minimum(slot_rank, capacity - 1)
    return (slot_index.reshape(routes.shape), route_kept.reshape(routes.shape))


def slot_owner(slot_index, route_kept, kept_gates, slot_total):
    pair_count = slot_index.size
    target = jnp.where(route_kept.reshape(-1), slot_index.reshape(-1), slot_total)
    token_rows = jnp.arange(pair_count, dtype=jnp.int32) // slot_index.shape[-1]
    slot_token = jnp.zeros((slot_total,), jnp.int32).at[target].set(token_rows, mode="drop")
    slot_live = jnp.zeros((slot_total,), jnp.bool_).at[target].set(True, mode="drop")
    slot_gate = (
        jnp.zeros((slot_total,), jnp.float32).at[target].set(kept_gates.reshape(-1), mode="drop")
    )
    return (slot_token, slot_live, slot_gate)


def block_scores(query_block, key_block, seq_ids, row_start):
    row_count = query_block.shape[0]
    key_count = key_block.shape[0]
    raw_scores = jnp.einsum(
        "qhc,khc->hqk", query_block, key_block, preferred_element_type=jnp.float32
    ) * (QK_NOPE + QK_ROPE) ** (-0.5)
    query_index = row_start + jnp.arange(row_count, dtype=jnp.int32)
    key_index = jnp.arange(key_count, dtype=jnp.int32)
    allowed = (seq_ids[:, None] == seq_ids[None, :]) & (key_index[None, :] <= query_index[:, None])
    return jnp.where(allowed[None], raw_scores, MASKED)


def body(
    tokens,
    cotangent,
    routes,
    seq_ids,
    positions,
    gain_attn,
    w_query,
    w_latent,
    gain_latent,
    w_expand,
    w_output,
    gain_ffn,
    w_router,
    w_shared_gate,
    w_shared_up,
    w_shared_down,
    w_gate,
    w_up,
    w_down,
):
    (
        gain_attn_all,
        query_weight,
        latent_weight,
        gain_latent_all,
        expand_weight,
        output_weight,
        gain_ffn_all,
        router_weight,
        shared_gate_weight,
        shared_up_weight,
        shared_down_weight,
    ) = (
        lax.all_gather(gain_attn, "dp", axis=0, tiled=True),
        lax.all_gather(w_query, "dp", axis=0, tiled=True),
        lax.all_gather(w_latent, "dp", axis=0, tiled=True),
        lax.all_gather(gain_latent, "dp", axis=0, tiled=True),
        lax.all_gather(w_expand, "dp", axis=0, tiled=True),
        lax.all_gather(w_output, "dp", axis=1, tiled=True),
        lax.all_gather(gain_ffn, "dp", axis=0, tiled=True),
        lax.all_gather(w_router, "dp", axis=0, tiled=True),
        lax.all_gather(w_shared_gate, "dp", axis=0, tiled=True),
        lax.all_gather(w_shared_up, "dp", axis=0, tiled=True),
        lax.all_gather(w_shared_down, "dp", axis=1, tiled=True),
    )
    tok_count = tokens.shape[0]
    head_width = QK_NOPE + QK_ROPE
    heads_here = query_weight.shape[1] // head_width
    softmax_scale = head_width ** (-0.5)
    gain_attn_f = gain_attn_all.astype(jnp.float32)
    gain_latent_f = gain_latent_all.astype(jnp.float32)
    resid_in = tokens.astype(jnp.float32)
    normed_attn, inverse_attn = norm_forward(resid_in, gain_attn_f)
    normed_attn_low = normed_attn.astype(jnp.bfloat16)
    cosine, sine_part = rope_tables(positions, QK_ROPE)
    query_raw = jnp.dot(normed_attn_low, query_weight, preferred_element_type=jnp.float32).reshape(
        tok_count, heads_here, head_width
    )
    query_low = jnp.concatenate(
        [
            query_raw[..., :QK_NOPE],
            rotate(query_raw[..., QK_NOPE:], cosine[:, None, :], sine_part[:, None, :]),
        ],
        axis=-1,
    ).astype(jnp.bfloat16)
    latent_raw = jnp.dot(normed_attn_low, latent_weight, preferred_element_type=jnp.float32)
    latent_part = latent_raw[:, :KV_RANK]
    latent_normed, inverse_latent = norm_forward(latent_part, gain_latent_f)
    latent_low = latent_normed.astype(jnp.bfloat16)
    key_rope_low = rotate(latent_raw[:, KV_RANK:], cosine, sine_part).astype(jnp.bfloat16)
    expanded = (
        jnp.dot(latent_low, expand_weight, preferred_element_type=jnp.float32)
        .astype(jnp.bfloat16)
        .reshape(tok_count, heads_here, QK_NOPE + V_HEAD)
    )
    value_low = expanded[..., QK_NOPE:]
    key_full = jnp.concatenate(
        [
            expanded[..., :QK_NOPE],
            jnp.broadcast_to(key_rope_low[:, None, :], (tok_count, heads_here, QK_ROPE)),
        ],
        axis=-1,
    )
    row_start = 0
    row_stop = row_start + tok_count
    masked = block_scores(query_low, key_full, seq_ids, row_start)
    row_max = jnp.max(masked, axis=-1, keepdims=True)
    exponent = jnp.exp(masked - row_max)
    exp_total = jnp.sum(exponent, axis=-1, keepdims=True)
    attn_probs = (exponent / exp_total).astype(jnp.bfloat16)
    log_totals = [row_max + jnp.log(exp_total)]
    head_blocks = jnp.einsum(
        "hqk,khc->qhc", attn_probs, value_low, preferred_element_type=jnp.float32
    )
    heads_low = head_blocks.astype(jnp.bfloat16).reshape(tok_count, heads_here * V_HEAD)
    attn_part = jnp.dot(heads_low, output_weight, preferred_element_type=jnp.float32)
    resid_mid = resid_in + lax.psum(attn_part, "tensor")
    gain_ffn_f = gain_ffn_all.astype(jnp.float32)
    normed_ffn, inverse_ffn = norm_forward(resid_mid, gain_ffn_f)
    normed_ffn_low = normed_ffn.astype(jnp.bfloat16)
    experts = router_weight.shape[1]
    router_probs = jax.nn.softmax(
        jnp.dot(normed_ffn_low, router_weight, preferred_element_type=jnp.float32), axis=-1
    )
    route_hits = routes[:, :, None] == jnp.arange(experts, dtype=jnp.int32)[None, None, :]
    picked = jnp.sum(jnp.where(route_hits, router_probs[:, None, :], 0.0), axis=-1)
    picked_total = jnp.sum(picked, axis=-1, keepdims=True)
    gates = picked / picked_total
    tensor_size = lax.axis_size("tensor")
    dp_size = lax.axis_size("dp")
    exp_here = w_gate.shape[0]
    model_width = tokens.shape[1]
    capacity = tensor_size * -(-(5 * tok_count * TOP) // (4 * experts * tensor_size))
    slot_index, route_kept = slot_layout(routes, experts, capacity)
    kept_gates = jnp.where(route_kept, gates, 0.0)
    kept_float = route_kept.astype(jnp.float32)
    slot_token, slot_live, slot_gate = slot_owner(
        slot_index, route_kept, kept_gates, experts * capacity
    )
    send_rows = jnp.where(
        slot_live[:, None], normed_ffn_low[slot_token], jnp.zeros((), jnp.bfloat16)
    ).reshape(dp_size, exp_here, capacity, model_width)
    grad_send = (
        (cotangent[slot_token].astype(jnp.float32) * slot_gate[:, None])
        .astype(jnp.bfloat16)
        .reshape(dp_size, exp_here, capacity, model_width)
    )
    received, grad_recv = (
        lax.all_to_all(send_rows, "dp", split_axis=0, concat_axis=0, tiled=True),
        lax.all_to_all(grad_send, "dp", split_axis=0, concat_axis=0, tiled=True),
    )
    gate_pre = jnp.einsum("secd,edf->secf", received, w_gate, preferred_element_type=jnp.float32)
    up_pre = jnp.einsum("secd,edf->secf", received, w_up, preferred_element_type=jnp.float32)
    gate_sigmoid = jax.nn.sigmoid(gate_pre)
    gate_silu = gate_pre * gate_sigmoid
    expert_act = (gate_silu * up_pre).astype(jnp.bfloat16)
    expert_out = jnp.einsum(
        "secf,efd->secd", expert_act, w_down, preferred_element_type=jnp.float32
    ).astype(jnp.bfloat16)
    returned = lax.all_to_all(expert_out, "dp", split_axis=0, concat_axis=0, tiled=True).reshape(
        experts * capacity, model_width
    )
    gathered = returned[slot_index].astype(jnp.float32)
    routed_part = jnp.sum(gathered * kept_gates[:, :, None], axis=1)
    shared_gate = jnp.dot(normed_ffn_low, shared_gate_weight, preferred_element_type=jnp.float32)
    shared_up = jnp.dot(normed_ffn_low, shared_up_weight, preferred_element_type=jnp.float32)
    shared_sigmoid = jax.nn.sigmoid(shared_gate)
    shared_silu = shared_gate * shared_sigmoid
    shared_act = (shared_silu * shared_up).astype(jnp.bfloat16)
    shared_part = jnp.dot(shared_act, shared_down_weight, preferred_element_type=jnp.float32)
    moe_total = lax.psum((routed_part + shared_part).astype(jnp.bfloat16), "tensor").astype(
        jnp.float32
    )
    result = (resid_mid + moe_total).astype(jnp.bfloat16)
    cot_float = cotangent.astype(jnp.float32)
    act_grad = jnp.einsum("secd,efd->secf", grad_recv, w_down, preferred_element_type=jnp.float32)
    w_down_grad = jnp.einsum(
        "secf,secd->efd", expert_act, grad_recv, preferred_element_type=jnp.float32
    )
    gate_grad = (act_grad * up_pre * gate_sigmoid * (1.0 + gate_pre * (1.0 - gate_sigmoid))).astype(
        jnp.bfloat16
    )
    up_grad = (act_grad * gate_silu).astype(jnp.bfloat16)
    w_gate_grad = jnp.einsum(
        "secd,secf->edf", received, gate_grad, preferred_element_type=jnp.float32
    )
    w_up_grad = jnp.einsum("secd,secf->edf", received, up_grad, preferred_element_type=jnp.float32)
    rows_grad = (
        jnp.einsum("secf,edf->secd", gate_grad, w_gate, preferred_element_type=jnp.float32)
        + jnp.einsum("secf,edf->secd", up_grad, w_up, preferred_element_type=jnp.float32)
    ).astype(jnp.bfloat16)
    grad_back = lax.all_to_all(rows_grad, "dp", split_axis=0, concat_axis=0, tiled=True).reshape(
        experts * capacity, model_width
    )
    routed_in_grad = jnp.sum(
        grad_back[slot_index].astype(jnp.float32) * kept_float[:, :, None], axis=1
    )
    gate_grad_part = jnp.sum(gathered * cot_float[:, None, :], axis=-1) * kept_float
    shared_act_grad = jnp.einsum(
        "td,fd->tf", cotangent, shared_down_weight, preferred_element_type=jnp.float32
    )
    shared_down_grad = jnp.einsum(
        "tf,td->fd", shared_act, cotangent, preferred_element_type=jnp.float32
    )
    shared_gate_grad = (
        shared_act_grad * shared_up * shared_sigmoid * (1.0 + shared_gate * (1.0 - shared_sigmoid))
    ).astype(jnp.bfloat16)
    shared_up_grad = (shared_act_grad * shared_silu).astype(jnp.bfloat16)
    shared_gate_weight_grad = jnp.einsum(
        "td,tf->df", normed_ffn_low, shared_gate_grad, preferred_element_type=jnp.float32
    )
    shared_up_weight_grad = jnp.einsum(
        "td,tf->df", normed_ffn_low, shared_up_grad, preferred_element_type=jnp.float32
    )
    shared_in_grad = jnp.einsum(
        "tf,df->td", shared_gate_grad, shared_gate_weight, preferred_element_type=jnp.float32
    ) + jnp.einsum(
        "tf,df->td", shared_up_grad, shared_up_weight, preferred_element_type=jnp.float32
    )
    ffn_in_sum, gate_grad_sum = lax.psum(
        (routed_in_grad + shared_in_grad, gate_grad_part), "tensor"
    )
    picked_grad = (
        gate_grad_sum - jnp.sum(gate_grad_sum * gates, axis=-1, keepdims=True)
    ) / picked_total
    probs_grad = jnp.sum(jnp.where(route_hits, picked_grad[:, :, None], 0.0), axis=1)
    logit_grad = (
        router_probs * (probs_grad - jnp.sum(router_probs * probs_grad, axis=-1, keepdims=True))
    ).astype(jnp.bfloat16)
    router_grad = jnp.einsum(
        "td,te->de", normed_ffn_low, logit_grad, preferred_element_type=jnp.float32
    )
    ffn_in = ffn_in_sum + jnp.einsum(
        "te,de->td", logit_grad, router_weight, preferred_element_type=jnp.float32
    )
    ffn_resid_grad, gain_ffn_grad = norm_backward(resid_mid, inverse_ffn, gain_ffn_f, ffn_in)
    mid_grad = cot_float + ffn_resid_grad
    mid_low = mid_grad.astype(jnp.bfloat16)
    output_weight_grad = jnp.einsum(
        "th,td->hd", heads_low, mid_low, preferred_element_type=jnp.float32
    )
    heads_grad = (
        jnp.einsum("td,hd->th", mid_low, output_weight, preferred_element_type=jnp.float32)
        .astype(jnp.bfloat16)
        .reshape(tok_count, heads_here, V_HEAD)
    )
    query_grad_blocks = []
    key_grad = jnp.zeros((tok_count, heads_here, head_width), jnp.float32)
    value_grad = jnp.zeros((tok_count, heads_here, V_HEAD), jnp.float32)
    for block_number, row_start in enumerate(range(0, tok_count, tok_count)):
        row_stop = row_start + tok_count
        masked = block_scores(query_low, key_full, seq_ids, row_start)
        attn_probs = jnp.exp(masked - log_totals[block_number])
        probs_low = attn_probs.astype(jnp.bfloat16)
        prob_grad = jnp.einsum(
            "qhc,khc->hqk", heads_grad, value_low, preferred_element_type=jnp.float32
        )
        row_dot = jnp.sum(attn_probs * prob_grad, axis=-1, keepdims=True)
        score_grad = (attn_probs * (prob_grad - row_dot)).astype(jnp.bfloat16)
        query_grad_blocks.append(
            jnp.einsum("hqk,khc->qhc", score_grad, key_full, preferred_element_type=jnp.float32)
            * softmax_scale
        )
        key_grad = key_grad.at[:row_stop].add(
            jnp.einsum("hqk,qhc->khc", score_grad, query_low, preferred_element_type=jnp.float32)
            * softmax_scale
        )
        value_grad = value_grad.at[:row_stop].add(
            jnp.einsum("hqk,qhc->khc", probs_low, heads_grad, preferred_element_type=jnp.float32)
        )
    query_grad = query_grad_blocks[0]
    query_pre_grad = jnp.concatenate(
        [
            query_grad[..., :QK_NOPE],
            rotate(query_grad[..., QK_NOPE:], cosine[:, None, :], -sine_part[:, None, :]),
        ],
        axis=-1,
    )
    query_pre_grad = query_pre_grad.astype(jnp.bfloat16).reshape(tok_count, heads_here * head_width)
    attn_in_part = jnp.einsum(
        "tq,dq->td", query_pre_grad, query_weight, preferred_element_type=jnp.float32
    )
    query_weight_grad = jnp.einsum(
        "td,tq->dq", normed_attn_low, query_pre_grad, preferred_element_type=jnp.float32
    )
    expand_grad = (
        jnp.concatenate([key_grad[..., :QK_NOPE], value_grad], axis=-1)
        .astype(jnp.bfloat16)
        .reshape(tok_count, heads_here * (QK_NOPE + V_HEAD))
    )
    latent_part_grad = jnp.einsum(
        "te,re->tr", expand_grad, expand_weight, preferred_element_type=jnp.float32
    )
    expand_weight_grad = jnp.einsum(
        "tr,te->re", latent_low, expand_grad, preferred_element_type=jnp.float32
    )
    rope_part_grad = jnp.sum(key_grad[..., QK_NOPE:], axis=1)
    attn_in_sum, latent_sum, rope_sum = lax.psum(
        (attn_in_part, latent_part_grad, rope_part_grad), "tensor"
    )
    latent_pre_grad, gain_latent_grad = norm_backward(
        latent_part, inverse_latent, gain_latent_f, latent_sum
    )
    latent_all_grad = jnp.concatenate(
        [latent_pre_grad, rotate(rope_sum, cosine, -sine_part)], axis=-1
    ).astype(jnp.bfloat16)
    attn_in = attn_in_sum + jnp.einsum(
        "tc,dc->td", latent_all_grad, latent_weight, preferred_element_type=jnp.float32
    )
    latent_weight_grad = jnp.einsum(
        "td,tc->dc", normed_attn_low, latent_all_grad, preferred_element_type=jnp.float32
    )
    input_grad, gain_attn_grad = norm_backward(resid_in, inverse_attn, gain_attn_f, attn_in)
    tokens_grad = (mid_grad + input_grad).astype(jnp.bfloat16)
    (
        gain_attn_share,
        query_share,
        latent_share,
        gain_latent_share,
        expand_share,
        output_share,
        gain_ffn_share,
        router_share,
        shared_gate_share,
        shared_up_share,
        shared_down_share,
    ) = (
        lax.psum_scatter(
            gain_attn_grad.astype(jnp.bfloat16), "dp", scatter_dimension=0, tiled=True
        ).astype(jnp.float32),
        lax.psum_scatter(
            query_weight_grad.astype(jnp.bfloat16), "dp", scatter_dimension=0, tiled=True
        ).astype(jnp.float32),
        lax.psum_scatter(
            latent_weight_grad.astype(jnp.bfloat16), "dp", scatter_dimension=0, tiled=True
        ).astype(jnp.float32),
        lax.psum_scatter(
            gain_latent_grad.astype(jnp.bfloat16), "dp", scatter_dimension=0, tiled=True
        ).astype(jnp.float32),
        lax.psum_scatter(
            expand_weight_grad.astype(jnp.bfloat16), "dp", scatter_dimension=0, tiled=True
        ).astype(jnp.float32),
        lax.psum_scatter(
            output_weight_grad.astype(jnp.bfloat16), "dp", scatter_dimension=1, tiled=True
        ).astype(jnp.float32),
        lax.psum_scatter(
            gain_ffn_grad.astype(jnp.bfloat16), "dp", scatter_dimension=0, tiled=True
        ).astype(jnp.float32),
        lax.psum_scatter(
            router_grad.astype(jnp.bfloat16), "dp", scatter_dimension=0, tiled=True
        ).astype(jnp.float32),
        lax.psum_scatter(
            shared_gate_weight_grad.astype(jnp.bfloat16), "dp", scatter_dimension=0, tiled=True
        ).astype(jnp.float32),
        lax.psum_scatter(
            shared_up_weight_grad.astype(jnp.bfloat16), "dp", scatter_dimension=0, tiled=True
        ).astype(jnp.float32),
        lax.psum_scatter(
            shared_down_grad.astype(jnp.bfloat16), "dp", scatter_dimension=1, tiled=True
        ).astype(jnp.float32),
    )
    return (
        result,
        tokens_grad,
        gain_attn_share,
        query_share,
        latent_share,
        gain_latent_share,
        expand_share,
        output_share,
        gain_ffn_share,
        router_share,
        shared_gate_share,
        shared_up_share,
        shared_down_share,
        w_gate_grad,
        w_up_grad,
        w_down_grad,
    )

def hop(values, axis, bit):
    return lax.ppermute(values, axis, [(i, i ^ bit) for i in range(lax.axis_size(axis))])


def core_hop(values):
    return hop(values, "tensor", 1)


def y_hop(values):
    return hop(values, "tensor", 2)


def x_hop(values):
    return hop(values, "dp", 1)


def z_hop(values):
    count = lax.axis_size("dp")
    return lax.ppermute(values, "dp", [(i, (i + 2) % count) for i in range(count)])


def low(values):
    return values.astype(jnp.bfloat16)


def plane_gather(own):
    half = own.shape[0] // 2
    first, second = own[:half], own[half:]
    first_x = x_hop(first)
    second_y = y_hop(second)
    first_pair = jnp.concatenate([first, first_x])
    second_pair = jnp.concatenate([second, second_y])
    first_y = y_hop(first_pair)
    second_x = x_hop(second_pair)
    parts = [
        first,
        second,
        first_x,
        second_x[:half],
        first_y[:half],
        second_y,
        first_y[half:],
        second_x[half:],
    ]
    quarter = jnp.concatenate(parts)
    return quarter, core_hop(quarter)


def slice_gather(own):
    chunks = []
    piece = own
    planes = lax.axis_size("dp") // 2
    for step in range(planes):
        chunks.append(plane_gather(piece))
        if step + 1 < planes:
            piece = z_hop(piece)
    return chunks


def plane_scatter(part):
    received = core_hop(part[1])
    total = part[0].astype(jnp.float32) + received.astype(jnp.float32)
    first, second = total[:, :, 0], total[:, :, 1]
    first_in = y_hop(low(first[1])).astype(jnp.float32)
    second_in = x_hop(low(second[:, 1])).astype(jnp.float32)
    first_near = first[0] + first_in
    second_near = second[:, 0] + second_in
    first_in = x_hop(low(first_near[1])).astype(jnp.float32)
    second_in = y_hop(low(second_near[1])).astype(jnp.float32)
    return jnp.concatenate([first_near[0] + first_in, second_near[0] + second_in])


def slice_scatter(parts):
    own = parts[0].shape[0] // 8
    width = parts[0].shape[1]
    pieces = [plane_scatter(part.reshape(2, 2, 2, 2, own // 2, width)) for part in parts]
    moving = pieces[1]
    for piece in pieces[2:] + pieces[:1]:
        moving = piece + z_hop(low(moving)).astype(jnp.float32)
    return moving


def tensor_scatter(values, tensor_index):
    rows = values.shape[0] // 4
    width = values.shape[1]
    core = tensor_index % 2
    level = tensor_index // 2
    blocks = values.reshape(2, 2, rows, width)
    mine = lax.dynamic_index_in_dim(blocks, core, 1, keepdims=False)
    other = lax.dynamic_index_in_dim(blocks, 1 - core, 1, keepdims=False)
    total = mine.astype(jnp.float32) + core_hop(low(other)).astype(jnp.float32)
    near = lax.dynamic_index_in_dim(total, level, 0, keepdims=False)
    far = lax.dynamic_index_in_dim(total, 1 - level, 0, keepdims=False)
    return near + y_hop(low(far)).astype(jnp.float32)


def tensor_gather(own, tensor_index):
    own_y = y_hop(own)
    pair = jnp.stack([own, own_y])
    pair_core = core_hop(pair)
    core = tensor_index % 2
    level = tensor_index // 2
    even = jnp.where(core == 0, pair, pair_core)
    odd = jnp.where(core == 0, pair_core, pair)
    near = jnp.concatenate([even[0], odd[0]])
    far = jnp.concatenate([even[1], odd[1]])
    return jnp.concatenate(
        [jnp.where(level == 0, near, far), jnp.where(level == 0, far, near)]
    )


def dp_gather(own, dp_index, axis):
    planes = lax.axis_size("dp") // 2
    plane = dp_index // 2
    side = dp_index % 2
    if axis == 0:
        whole = jnp.zeros((2 * planes,) + own.shape, own.dtype)
    else:
        whole = jnp.zeros(own.shape[:-1] + (2 * planes * own.shape[-1],), own.dtype)

    def place(whole, piece, index):
        if axis == 0:
            return lax.dynamic_update_index_in_dim(whole, piece, index, 0)
        return lax.dynamic_update_slice_in_dim(whole, piece, index * piece.shape[-1], 1)

    piece = own
    for step in range(planes):
        base = (plane - step) % planes * 2
        whole = place(whole, piece, base + side)
        whole = place(whole, x_hop(piece), base + 1 - side)
        if step + 1 < planes:
            piece = z_hop(piece)
    return whole


def dp_scatter(block, dp_index):
    planes = lax.axis_size("dp") // 2
    plane = dp_index // 2
    side = dp_index % 2
    moving = None
    for step in list(range(1, planes)) + [0]:
        base = (plane - step) % planes * 2
        received = x_hop(low(block(base + 1 - side))).astype(jnp.float32)
        piece = block(base + side) + received
        if moving is not None:
            piece = piece + z_hop(low(moving)).astype(jnp.float32)
        moving = piece
    return moving


def padded(values, axis, size):
    pads = [(0, 0)] * values.ndim
    pads[axis] = (0, size - values.shape[axis])
    return jnp.pad(values, pads)


def lanes(size):
    return -(-size // 128) * 128


def body_dense(
    tokens,
    cotangent,
    routes,
    seq_ids,
    positions,
    gain_attn,
    w_query,
    w_latent,
    gain_latent,
    w_expand,
    w_output,
    gain_ffn,
    w_router,
    w_shared_gate,
    w_shared_up,
    w_shared_down,
    w_gate,
    w_up,
    w_down,
):
    tensor_size = lax.axis_size("tensor")
    dp_size = lax.axis_size("dp")
    dp_index = lax.axis_index("dp")
    tensor_index = lax.axis_index("tensor")
    tok_count, width = tokens.shape
    own_count = tok_count // tensor_size
    own_start = tensor_index * own_count
    experts = w_router.shape[1]
    exp_here = w_gate.shape[0]
    capacity = tensor_size * -(-(5 * tok_count * TOP) // (4 * experts * tensor_size))

    def own_rows(values):
        return lax.dynamic_slice_in_dim(values, own_start, own_count, 0)

    lat_width = w_latent.shape[1]
    lat_block = w_latent.shape[0]
    lat_rows = lat_block // tensor_size
    side = jnp.concatenate(
        [
            w_latent,
            w_router,
            gain_attn[:, None],
            gain_ffn[:, None],
            padded(gain_latent, 0, lat_block)[:, None],
        ],
        axis=1,
    )
    side_width = lanes(side.shape[1])
    side = padded(
        lax.dynamic_slice_in_dim(side, tensor_index * lat_rows, lat_rows, 0), 1, side_width
    )
    side_all = dp_gather(side, dp_index, 0)
    side_pair = jnp.stack([side_all, y_hop(side_all)])
    side_far = core_hop(side_pair)
    core = tensor_index % 2
    level = tensor_index // 2
    side_even = jnp.where(core == 0, side_pair, side_far)
    side_odd = jnp.where(core == 0, side_far, side_pair)
    side_near = jnp.stack([side_even, side_odd], axis=1)
    side_all = jnp.where(level == 0, side_near, side_near[::-1]).reshape(
        tensor_size, dp_size, lat_rows, side_width
    )
    side_all = side_all.transpose(1, 0, 2, 3).reshape(width, side_width)
    latent_weight = side_all[:, :lat_width]
    router_weight = side_all[:, lat_width : lat_width + experts]
    gains_all = side_all[:, lat_width + experts : lat_width + experts + 3].astype(jnp.float32).T
    gain_attn_f = gains_all[0]
    gain_ffn_f = gains_all[1]
    gain_latent_f = gains_all[2].reshape(dp_size, lat_block)[:, : gain_latent.shape[0]].reshape(
        KV_RANK
    )

    query_weight = dp_gather(w_query, dp_index, 0).reshape(width, w_query.shape[1])
    expand_weight = dp_gather(w_expand, dp_index, 0).reshape(KV_RANK, w_expand.shape[1])
    output_weight = dp_gather(w_output, dp_index, 1).reshape(w_output.shape[0], width)

    routed = jnp.sum(
        (routes[:, :, None] == jnp.arange(experts, dtype=jnp.int32)[None, None, :]).astype(
            jnp.float32
        ),
        axis=1,
    )
    order = jnp.arange(tok_count, dtype=jnp.int32)
    earlier = (order[None, :] < order[:, None]).astype(jnp.bfloat16)
    rank = jnp.dot(earlier, low(routed), preferred_element_type=jnp.float32)
    standing = routed * (1.0 + (rank < capacity).astype(jnp.float32))
    standing_own = own_rows(standing)
    marks_all = lax.all_gather(low(standing), "dp", axis=0, tiled=True)
    cot_own = own_rows(cotangent)
    cot_sent, _ = lax.optimization_barrier((cot_own, query_weight))
    cot_chunks = slice_gather(cot_sent)
    planes = dp_size // 2
    marks_all = marks_all.reshape(planes, 8, own_count, experts)
    near = jnp.arange(8, dtype=jnp.int32)
    near_x = near % 2 ^ dp_index % 2
    near_y = near // 2 % 2 ^ level
    near_core = near // 4 ^ core
    near_block = near_x * 4 + near_y * 2 + near_core
    mark_chunks = [
        jnp.take(
            lax.dynamic_index_in_dim(
                marks_all, (dp_index // 2 - step) % planes, 0, keepdims=False
            ),
            near_block,
            axis=0,
        ).reshape(8 * own_count, experts)
        for step in range(planes)
    ]

    shared_here = w_shared_gate.shape[1] // dp_size
    shared_in = lax.all_to_all(
        jnp.stack([w_shared_gate, w_shared_up]), "dp", split_axis=2, concat_axis=1, tiled=True
    )
    shared_out = lax.all_to_all(w_shared_down, "dp", split_axis=0, concat_axis=1, tiled=True)
    group = w_gate.shape[2]
    group_lanes = lanes(group)
    shared_lanes = lanes(shared_here)

    def joined(routed_weight, shared_weight, axis):
        pieces = [padded(routed_weight[e], axis, group_lanes) for e in range(exp_here)]
        return jnp.concatenate(pieces + [padded(shared_weight, axis, shared_lanes)], axis=axis)

    gate_weight = joined(w_gate, shared_in[0], 1)
    up_weight = joined(w_up, shared_in[1], 1)
    down_weight = joined(w_down, shared_out, 0)
    hidden = gate_weight.shape[1]

    head_width = QK_NOPE + QK_ROPE
    heads_here = query_weight.shape[1] // head_width
    softmax_scale = head_width ** (-0.5)
    resid_in = tokens.astype(jnp.float32)
    normed_attn, inverse_attn = norm_forward(resid_in, gain_attn_f)
    normed_attn_low = low(normed_attn)
    cosine, sine_part = rope_tables(positions, QK_ROPE)
    query_raw = jnp.dot(normed_attn_low, query_weight, preferred_element_type=jnp.float32).reshape(
        tok_count, heads_here, head_width
    )
    query_low = low(
        jnp.concatenate(
            [
                query_raw[..., :QK_NOPE],
                rotate(query_raw[..., QK_NOPE:], cosine[:, None, :], sine_part[:, None, :]),
            ],
            axis=-1,
        )
    )
    latent_raw = jnp.dot(normed_attn_low, latent_weight, preferred_element_type=jnp.float32)
    latent_part = latent_raw[:, :KV_RANK]
    latent_normed, inverse_latent = norm_forward(latent_part, gain_latent_f)
    latent_low = low(latent_normed)
    key_rope_low = low(rotate(latent_raw[:, KV_RANK:], cosine, sine_part))
    expanded = low(
        jnp.dot(latent_low, expand_weight, preferred_element_type=jnp.float32)
    ).reshape(tok_count, heads_here, QK_NOPE + V_HEAD)
    value_low = expanded[..., QK_NOPE:]
    key_full = jnp.concatenate(
        [
            expanded[..., :QK_NOPE],
            jnp.broadcast_to(key_rope_low[:, None, :], (tok_count, heads_here, QK_ROPE)),
        ],
        axis=-1,
    )
    masked = block_scores(query_low, key_full, seq_ids, 0)
    row_max = jnp.max(masked, axis=-1, keepdims=True)
    exponent = jnp.exp(masked - row_max)
    exp_total = jnp.sum(exponent, axis=-1, keepdims=True)
    probs_low = low(exponent / exp_total)
    log_total = row_max + jnp.log(exp_total)
    heads_low = low(
        jnp.einsum("hqk,khc->qhc", probs_low, value_low, preferred_element_type=jnp.float32)
    ).reshape(tok_count, heads_here * V_HEAD)
    attn_part = jnp.dot(heads_low, output_weight, preferred_element_type=jnp.float32)

    resid_own = own_rows(tokens).astype(jnp.float32) + tensor_scatter(attn_part, tensor_index)
    normed_own, inverse_own = norm_forward(resid_own, gain_ffn_f)
    normed_own_low = low(normed_own)
    rows_sent, cot_chunks = lax.optimization_barrier((normed_own_low, cot_chunks))
    row_chunks = slice_gather(rows_sent)

    def gating(rows, standing_rows):
        probs = jax.nn.softmax(
            jnp.dot(rows, router_weight, preferred_element_type=jnp.float32), axis=-1
        )
        gates = jnp.where(standing_rows > 0.5, probs, 0.0)
        picked = jnp.sum(gates, axis=-1, keepdims=True)
        return probs, gates / picked, picked

    expert_index = jnp.arange(experts, dtype=jnp.int32)[None, :]
    column = jnp.arange(hidden, dtype=jnp.int32)[None, :]
    out_parts, in_parts, gate_parts, kept_parts = [], [], [], []
    for step in range(planes):
        rows = jnp.concatenate(row_chunks[step])
        cots = jnp.concatenate(cot_chunks[step])
        if step > 0:
            rows, cots, in_parts[-1], out_parts[-1] = lax.optimization_barrier(
                (rows, cots, in_parts[-1], out_parts[-1])
            )
        marks = mark_chunks[step].astype(jnp.float32)
        _, chunk_gates, _ = gating(rows, marks)
        chunk_gates = jnp.where(marks > 1.5, chunk_gates, 0.0)
        scale = jnp.ones((rows.shape[0], hidden), jnp.float32)
        for e in reversed(range(exp_here)):
            here = expert_index == dp_index * exp_here + e
            gate_column = jnp.sum(jnp.where(here, chunk_gates, 0.0), axis=-1, keepdims=True)
            scale = jnp.where(column < (e + 1) * group_lanes, gate_column, scale)
        gate_pre = jnp.dot(rows, gate_weight, preferred_element_type=jnp.float32)
        up_pre = jnp.dot(rows, up_weight, preferred_element_type=jnp.float32)
        sigmoid = jax.nn.sigmoid(gate_pre)
        silu = gate_pre * sigmoid
        act = silu * up_pre
        act_scaled = low(act * scale)
        out_parts.append(
            low(jnp.dot(act_scaled, down_weight, preferred_element_type=jnp.float32))
        )
        act_grad = jnp.einsum("td,fd->tf", cots, down_weight, preferred_element_type=jnp.float32)
        meeting = act * act_grad
        gate_parts.append(
            jnp.stack(
                [
                    jnp.sum(meeting[:, e * group_lanes : (e + 1) * group_lanes], axis=-1)
                    for e in range(exp_here)
                ]
            )
        )
        scaled_grad = act_grad * scale
        gate_grad = low(scaled_grad * up_pre * sigmoid * (1.0 + gate_pre * (1.0 - sigmoid)))
        up_grad = low(scaled_grad * silu)
        in_parts.append(
            low(
                jnp.einsum("tf,df->td", gate_grad, gate_weight, preferred_element_type=jnp.float32)
                + jnp.einsum("tf,df->td", up_grad, up_weight, preferred_element_type=jnp.float32)
            )
        )
        kept_parts.append((rows, cots, gate_grad, up_grad, act_scaled))
    gate_weight_grad = up_weight_grad = down_weight_grad = 0.0
    for rows, cots, gate_grad, up_grad, act_scaled in kept_parts:
        gate_weight_grad += jnp.einsum(
            "td,tf->df", rows, gate_grad, preferred_element_type=jnp.float32
        )
        up_weight_grad += jnp.einsum("td,tf->df", rows, up_grad, preferred_element_type=jnp.float32)
        down_weight_grad += jnp.einsum(
            "tf,td->fd", act_scaled, cots, preferred_element_type=jnp.float32
        )

    ffn_sum = slice_scatter(in_parts)
    gate_sums = jnp.stack(gate_parts).reshape(-1, exp_here, 2, 2, 2, own_count)
    gate_sums = gate_sums[:, :, 0] + core_hop(gate_sums[:, :, 1])
    gate_sums = gate_sums[:, :, 0] + y_hop(gate_sums[:, :, 1])
    block = jnp.arange(dp_size, dtype=jnp.int32)
    place = ((dp_index // 2 - block // 2) % planes) * 2 + (block + dp_index) % 2
    gate_sums = gate_sums.transpose(0, 2, 1, 3).reshape(dp_size, exp_here, own_count)[place]
    gate_sums = lax.all_to_all(gate_sums, "dp", split_axis=0, concat_axis=0, tiled=True)
    gate_sums = gate_sums.reshape(experts, own_count).T

    probs_own, gates_own, picked_own = gating(normed_own_low, standing_own)
    gate_sums = jnp.where(standing_own > 1.5, gate_sums, 0.0)
    picked_grad = (
        gate_sums - jnp.sum(gate_sums * gates_own, axis=-1, keepdims=True)
    ) / picked_own
    probs_grad = jnp.where(standing_own > 0.5, picked_grad, 0.0)
    logit_grad = low(
        probs_own * (probs_grad - jnp.sum(probs_own * probs_grad, axis=-1, keepdims=True))
    )
    router_grad = jnp.einsum(
        "td,te->de", normed_own_low, logit_grad, preferred_element_type=jnp.float32
    )
    ffn_in = ffn_sum + jnp.einsum(
        "te,de->td", logit_grad, router_weight, preferred_element_type=jnp.float32
    )
    ffn_resid_grad, gain_ffn_grad = norm_backward(resid_own, inverse_own, gain_ffn_f, ffn_in)
    mid_grad_own = cot_own.astype(jnp.float32) + ffn_resid_grad
    mid_low = tensor_gather(low(mid_grad_own), tensor_index)

    output_weight_grad = jnp.einsum(
        "th,td->hd", heads_low, mid_low, preferred_element_type=jnp.float32
    )
    heads_grad = low(
        jnp.einsum("td,hd->th", mid_low, output_weight, preferred_element_type=jnp.float32)
    ).reshape(tok_count, heads_here, V_HEAD)
    masked = block_scores(query_low, key_full, seq_ids, 0)
    attn_probs = jnp.exp(masked - log_total)
    prob_grad = jnp.einsum("qhc,khc->hqk", heads_grad, value_low, preferred_element_type=jnp.float32)
    row_dot = jnp.sum(attn_probs * prob_grad, axis=-1, keepdims=True)
    score_grad = low(attn_probs * (prob_grad - row_dot))
    query_grad = (
        jnp.einsum("hqk,khc->qhc", score_grad, key_full, preferred_element_type=jnp.float32)
        * softmax_scale
    )
    key_grad = (
        jnp.einsum("hqk,qhc->khc", score_grad, query_low, preferred_element_type=jnp.float32)
        * softmax_scale
    )
    value_grad = jnp.einsum(
        "hqk,qhc->khc", low(attn_probs), heads_grad, preferred_element_type=jnp.float32
    )
    query_pre_grad = low(
        jnp.concatenate(
            [
                query_grad[..., :QK_NOPE],
                rotate(query_grad[..., QK_NOPE:], cosine[:, None, :], -sine_part[:, None, :]),
            ],
            axis=-1,
        )
    ).reshape(tok_count, heads_here * head_width)
    query_weight_grad = jnp.einsum(
        "td,tq->dq", normed_attn_low, query_pre_grad, preferred_element_type=jnp.float32
    )
    expand_grad = low(jnp.concatenate([key_grad[..., :QK_NOPE], value_grad], axis=-1)).reshape(
        tok_count, heads_here * (QK_NOPE + V_HEAD)
    )
    latent_grad = jnp.einsum(
        "te,re->tr", expand_grad, expand_weight, preferred_element_type=jnp.float32
    )
    expand_weight_grad = jnp.einsum(
        "tr,te->re", latent_low, expand_grad, preferred_element_type=jnp.float32
    )
    rope_grad = jnp.sum(key_grad[..., QK_NOPE:], axis=1)
    latent_pre_grad, gain_latent_grad = norm_backward(
        latent_part, inverse_latent, gain_latent_f, latent_grad
    )
    latent_all_grad = low(
        jnp.concatenate([latent_pre_grad, rotate(rope_grad, cosine, -sine_part)], axis=-1)
    )
    attn_in = jnp.einsum(
        "tq,dq->td", query_pre_grad, query_weight, preferred_element_type=jnp.float32
    ) + jnp.einsum("tc,dc->td", latent_all_grad, latent_weight, preferred_element_type=jnp.float32)
    latent_weight_grad = jnp.einsum(
        "td,tc->dc", normed_attn_low, latent_all_grad, preferred_element_type=jnp.float32
    )
    gain_attn_grad = jnp.sum(attn_in * (resid_in * inverse_attn), axis=0)
    attn_in_own = tensor_scatter(attn_in, tensor_index)
    input_grad, _ = norm_backward(
        own_rows(resid_in), own_rows(inverse_attn), gain_attn_f, attn_in_own
    )
    tokens_grad = tensor_gather(low(mid_grad_own + input_grad), tensor_index)

    out_sum = slice_scatter(out_parts)
    result = tensor_gather(low(resid_own + out_sum), tensor_index)

    output_share = dp_scatter(
        lambda i: lax.dynamic_slice_in_dim(
            output_weight_grad, i * w_output.shape[1], w_output.shape[1], 1
        ),
        dp_index,
    )
    query_share = dp_scatter(
        lambda i: lax.dynamic_slice_in_dim(query_weight_grad, i * lat_block, lat_block, 0),
        dp_index,
    )
    expand_rows = w_expand.shape[0]
    expand_share = dp_scatter(
        lambda i: lax.dynamic_slice_in_dim(expand_weight_grad, i * expand_rows, expand_rows, 0),
        dp_index,
    )

    gain_latent_rows = padded(gain_latent_grad.reshape(dp_size, -1), 1, lat_block).reshape(width)
    side_grad = jnp.concatenate(
        [
            latent_weight_grad,
            router_grad,
            jnp.stack([gain_attn_grad, gain_ffn_grad, gain_latent_rows]).T,
        ],
        axis=1,
    )
    side_grad = padded(side_grad, 1, side_width)
    side_grad = side_grad.reshape(dp_size, 2, 2, lat_rows, side_width)
    kept_side = lax.dynamic_index_in_dim(side_grad, core, 2, keepdims=False)
    sent_side = lax.dynamic_index_in_dim(side_grad, 1 - core, 2, keepdims=False)
    side_grad = kept_side + core_hop(low(sent_side)).astype(jnp.float32)
    kept_side = lax.dynamic_index_in_dim(side_grad, level, 1, keepdims=False)
    sent_side = lax.dynamic_index_in_dim(side_grad, 1 - level, 1, keepdims=False)
    side_grad = kept_side + y_hop(low(sent_side)).astype(jnp.float32)
    side_piece = dp_scatter(
        lambda i: lax.dynamic_index_in_dim(side_grad, i, 0, keepdims=False), dp_index
    )
    grad_full = tensor_gather(low(side_piece), tensor_index).astype(jnp.float32)
    latent_share = grad_full[:, :lat_width]
    router_share = grad_full[:, lat_width : lat_width + experts]
    gain_rows = grad_full[:, lat_width + experts : lat_width + experts + 3].T
    gain_attn_share = gain_rows[0]
    gain_ffn_share = gain_rows[1]
    gain_latent_share = gain_rows[2, : gain_latent.shape[0]]

    def routed_grad(grad, axis):
        return jnp.stack(
            [
                lax.slice_in_dim(grad, e * group_lanes, e * group_lanes + group, axis=axis)
                for e in range(exp_here)
            ]
        )

    def shared_grad(grad, axis):
        start = exp_here * group_lanes
        return low(lax.slice_in_dim(grad, start, start + shared_here, axis=axis))

    shared_in_grad = lax.all_to_all(
        jnp.stack([shared_grad(gate_weight_grad, 1), shared_grad(up_weight_grad, 1)]),
        "dp",
        split_axis=1,
        concat_axis=2,
        tiled=True,
    ).astype(jnp.float32)
    shared_down_share = lax.all_to_all(
        shared_grad(down_weight_grad, 0), "dp", split_axis=1, concat_axis=0, tiled=True
    ).astype(jnp.float32)

    return (
        result,
        tokens_grad,
        gain_attn_share,
        query_share,
        latent_share,
        gain_latent_share,
        expand_share,
        output_share,
        gain_ffn_share,
        router_share,
        shared_in_grad[0],
        shared_in_grad[1],
        shared_down_share,
        routed_grad(gate_weight_grad, 1),
        routed_grad(up_weight_grad, 1),
        routed_grad(down_weight_grad, 0),
    )


def solution(mesh):
    dense = mesh.shape["dp"] == 8 and mesh.shape["tensor"] == 4
    return jax.shard_map(
        body_dense if dense else body,
        mesh=mesh,
        in_specs=(
            P("dp", None),
            P("dp", None),
            P("dp", None),
            P("dp"),
            P("dp"),
            P("dp"),
            P("dp", "tensor"),
            P("dp", None),
            P("dp"),
            P("dp", "tensor"),
            P("tensor", "dp"),
            P("dp"),
            P("dp", None),
            P("dp", "tensor"),
            P("dp", "tensor"),
            P("tensor", "dp"),
            P("dp", None, "tensor"),
            P("dp", None, "tensor"),
            P("dp", "tensor", None),
        ),
        out_specs=(
            P("dp", None),
            P("dp", None),
            P("dp"),
            P("dp", "tensor"),
            P("dp", None),
            P("dp"),
            P("dp", "tensor"),
            P("tensor", "dp"),
            P("dp"),
            P("dp", None),
            P("dp", "tensor"),
            P("dp", "tensor"),
            P("tensor", "dp"),
            P("dp", None, "tensor"),
            P("dp", None, "tensor"),
            P("dp", "tensor", None),
        ),
        check_vma=False,
    )
```

```python
import jax
import jax.numpy as jnp
from jax import lax
from jax.sharding import PartitionSpec as P

QK_NOPE = 128
QK_ROPE = 64
V_HEAD = 128
KV_RANK = 512
TOP = 6


EPSILON = 1e-06
MASKED = -1e30


def norm_forward(values, gain_full):
    inverse = lax.rsqrt(jnp.mean(values * values, axis=-1, keepdims=True) + EPSILON)
    return (values * inverse * gain_full, inverse)


def norm_backward(values, inverse, gain_full, grad_out):
    normed = values * inverse
    scaled = grad_out * gain_full
    grad_in = inverse * (scaled - normed * jnp.mean(scaled * normed, axis=-1, keepdims=True))
    return (grad_in, jnp.sum(grad_out * normed, axis=0))


def rope_tables(positions, width):
    half_width = width // 2
    frequency = jnp.power(10000.0, -jnp.arange(half_width, dtype=jnp.float32) / half_width)
    angles = positions.astype(jnp.float32)[:, None] * frequency[None, :]
    return (jnp.cos(angles), jnp.sin(angles))


def rotate(values, cosine, sine_part):
    half_width = values.shape[-1] // 2
    front_half = values[..., :half_width]
    back_half = values[..., half_width:]
    return jnp.concatenate(
        [front_half * cosine - back_half * sine_part, back_half * cosine + front_half * sine_part],
        axis=-1,
    )


def slot_layout(routes, experts, capacity):
    flat_routes = routes.reshape(-1)
    onehot = (flat_routes[:, None] == jnp.arange(experts, dtype=jnp.int32)[None, :]).astype(
        jnp.int32
    )
    before = jnp.cumsum(onehot, axis=0) - onehot
    slot_rank = jnp.sum(before * onehot, axis=1)
    route_kept = slot_rank < capacity
    slot_index = flat_routes * capacity + jnp.minimum(slot_rank, capacity - 1)
    return (slot_index.reshape(routes.shape), route_kept.reshape(routes.shape))


def slot_owner(slot_index, route_kept, kept_gates, slot_total):
    pair_count = slot_index.size
    target = jnp.where(route_kept.reshape(-1), slot_index.reshape(-1), slot_total)
    token_rows = jnp.arange(pair_count, dtype=jnp.int32) // slot_index.shape[-1]
    slot_token = jnp.zeros((slot_total,), jnp.int32).at[target].set(token_rows, mode="drop")
    slot_live = jnp.zeros((slot_total,), jnp.bool_).at[target].set(True, mode="drop")
    slot_gate = (
        jnp.zeros((slot_total,), jnp.float32).at[target].set(kept_gates.reshape(-1), mode="drop")
    )
    return (slot_token, slot_live, slot_gate)


def block_scores(query_block, key_block, seq_ids, row_start):
    row_count = query_block.shape[0]
    key_count = key_block.shape[0]
    raw_scores = jnp.einsum(
        "qhc,khc->hqk", query_block, key_block, preferred_element_type=jnp.float32
    ) * (QK_NOPE + QK_ROPE) ** (-0.5)
    query_index = row_start + jnp.arange(row_count, dtype=jnp.int32)
    key_index = jnp.arange(key_count, dtype=jnp.int32)
    allowed = (seq_ids[:, None] == seq_ids[None, :]) & (key_index[None, :] <= query_index[:, None])
    return jnp.where(allowed[None], raw_scores, MASKED)


def body(
    tokens,
    cotangent,
    routes,
    seq_ids,
    positions,
    gain_attn,
    w_query,
    w_latent,
    gain_latent,
    w_expand,
    w_output,
    gain_ffn,
    w_router,
    w_shared_gate,
    w_shared_up,
    w_shared_down,
    w_gate,
    w_up,
    w_down,
):
    (
        gain_attn_all,
        query_weight,
        latent_weight,
        gain_latent_all,
        expand_weight,
        output_weight,
        gain_ffn_all,
        router_weight,
        shared_gate_weight,
        shared_up_weight,
        shared_down_weight,
    ) = (
        lax.all_gather(gain_attn, "dp", axis=0, tiled=True),
        lax.all_gather(w_query, "dp", axis=0, tiled=True),
        lax.all_gather(w_latent, "dp", axis=0, tiled=True),
        lax.all_gather(gain_latent, "dp", axis=0, tiled=True),
        lax.all_gather(w_expand, "dp", axis=0, tiled=True),
        lax.all_gather(w_output, "dp", axis=1, tiled=True),
        lax.all_gather(gain_ffn, "dp", axis=0, tiled=True),
        lax.all_gather(w_router, "dp", axis=0, tiled=True),
        lax.all_gather(w_shared_gate, "dp", axis=0, tiled=True),
        lax.all_gather(w_shared_up, "dp", axis=0, tiled=True),
        lax.all_gather(w_shared_down, "dp", axis=1, tiled=True),
    )
    tok_count = tokens.shape[0]
    head_width = QK_NOPE + QK_ROPE
    heads_here = query_weight.shape[1] // head_width
    softmax_scale = head_width ** (-0.5)
    gain_attn_f = gain_attn_all.astype(jnp.float32)
    gain_latent_f = gain_latent_all.astype(jnp.float32)
    resid_in = tokens.astype(jnp.float32)
    normed_attn, inverse_attn = norm_forward(resid_in, gain_attn_f)
    normed_attn_low = normed_attn.astype(jnp.bfloat16)
    cosine, sine_part = rope_tables(positions, QK_ROPE)
    query_raw = jnp.dot(normed_attn_low, query_weight, preferred_element_type=jnp.float32).reshape(
        tok_count, heads_here, head_width
    )
    query_low = jnp.concatenate(
        [
            query_raw[..., :QK_NOPE],
            rotate(query_raw[..., QK_NOPE:], cosine[:, None, :], sine_part[:, None, :]),
        ],
        axis=-1,
    ).astype(jnp.bfloat16)
    latent_raw = jnp.dot(normed_attn_low, latent_weight, preferred_element_type=jnp.float32)
    latent_part = latent_raw[:, :KV_RANK]
    latent_normed, inverse_latent = norm_forward(latent_part, gain_latent_f)
    latent_low = latent_normed.astype(jnp.bfloat16)
    key_rope_low = rotate(latent_raw[:, KV_RANK:], cosine, sine_part).astype(jnp.bfloat16)
    expanded = (
        jnp.dot(latent_low, expand_weight, preferred_element_type=jnp.float32)
        .astype(jnp.bfloat16)
        .reshape(tok_count, heads_here, QK_NOPE + V_HEAD)
    )
    value_low = expanded[..., QK_NOPE:]
    key_full = jnp.concatenate(
        [
            expanded[..., :QK_NOPE],
            jnp.broadcast_to(key_rope_low[:, None, :], (tok_count, heads_here, QK_ROPE)),
        ],
        axis=-1,
    )
    row_start = 0
    row_stop = row_start + tok_count
    masked = block_scores(query_low, key_full, seq_ids, row_start)
    row_max = jnp.max(masked, axis=-1, keepdims=True)
    exponent = jnp.exp(masked - row_max)
    exp_total = jnp.sum(exponent, axis=-1, keepdims=True)
    attn_probs = (exponent / exp_total).astype(jnp.bfloat16)
    log_totals = [row_max + jnp.log(exp_total)]
    head_blocks = jnp.einsum(
        "hqk,khc->qhc", attn_probs, value_low, preferred_element_type=jnp.float32
    )
    heads_low = head_blocks.astype(jnp.bfloat16).reshape(tok_count, heads_here * V_HEAD)
    attn_part = jnp.dot(heads_low, output_weight, preferred_element_type=jnp.float32)
    resid_mid = resid_in + lax.psum(attn_part, "tensor")
    gain_ffn_f = gain_ffn_all.astype(jnp.float32)
    normed_ffn, inverse_ffn = norm_forward(resid_mid, gain_ffn_f)
    normed_ffn_low = normed_ffn.astype(jnp.bfloat16)
    experts = router_weight.shape[1]
    router_probs = jax.nn.softmax(
        jnp.dot(normed_ffn_low, router_weight, preferred_element_type=jnp.float32), axis=-1
    )
    route_hits = routes[:, :, None] == jnp.arange(experts, dtype=jnp.int32)[None, None, :]
    picked = jnp.sum(jnp.where(route_hits, router_probs[:, None, :], 0.0), axis=-1)
    picked_total = jnp.sum(picked, axis=-1, keepdims=True)
    gates = picked / picked_total
    tensor_size = lax.axis_size("tensor")
    dp_size = lax.axis_size("dp")
    exp_here = w_gate.shape[0]
    model_width = tokens.shape[1]
    capacity = tensor_size * -(-(5 * tok_count * TOP) // (4 * experts * tensor_size))
    slot_index, route_kept = slot_layout(routes, experts, capacity)
    kept_gates = jnp.where(route_kept, gates, 0.0)
    kept_float = route_kept.astype(jnp.float32)
    slot_token, slot_live, slot_gate = slot_owner(
        slot_index, route_kept, kept_gates, experts * capacity
    )
    send_rows = jnp.where(
        slot_live[:, None], normed_ffn_low[slot_token], jnp.zeros((), jnp.bfloat16)
    ).reshape(dp_size, exp_here, capacity, model_width)
    grad_send = (
        (cotangent[slot_token].astype(jnp.float32) * slot_gate[:, None])
        .astype(jnp.bfloat16)
        .reshape(dp_size, exp_here, capacity, model_width)
    )
    received, grad_recv = (
        lax.all_to_all(send_rows, "dp", split_axis=0, concat_axis=0, tiled=True),
        lax.all_to_all(grad_send, "dp", split_axis=0, concat_axis=0, tiled=True),
    )
    gate_pre = jnp.einsum("secd,edf->secf", received, w_gate, preferred_element_type=jnp.float32)
    up_pre = jnp.einsum("secd,edf->secf", received, w_up, preferred_element_type=jnp.float32)
    gate_sigmoid = jax.nn.sigmoid(gate_pre)
    gate_silu = gate_pre * gate_sigmoid
    expert_act = (gate_silu * up_pre).astype(jnp.bfloat16)
    expert_out = jnp.einsum(
        "secf,efd->secd", expert_act, w_down, preferred_element_type=jnp.float32
    ).astype(jnp.bfloat16)
    returned = lax.all_to_all(expert_out, "dp", split_axis=0, concat_axis=0, tiled=True).reshape(
        experts * capacity, model_width
    )
    gathered = returned[slot_index].astype(jnp.float32)
    routed_part = jnp.sum(gathered * kept_gates[:, :, None], axis=1)
    shared_gate = jnp.dot(normed_ffn_low, shared_gate_weight, preferred_element_type=jnp.float32)
    shared_up = jnp.dot(normed_ffn_low, shared_up_weight, preferred_element_type=jnp.float32)
    shared_sigmoid = jax.nn.sigmoid(shared_gate)
    shared_silu = shared_gate * shared_sigmoid
    shared_act = (shared_silu * shared_up).astype(jnp.bfloat16)
    shared_part = jnp.dot(shared_act, shared_down_weight, preferred_element_type=jnp.float32)
    moe_total = lax.psum((routed_part + shared_part).astype(jnp.bfloat16), "tensor").astype(
        jnp.float32
    )
    result = (resid_mid + moe_total).astype(jnp.bfloat16)
    cot_float = cotangent.astype(jnp.float32)
    act_grad = jnp.einsum("secd,efd->secf", grad_recv, w_down, preferred_element_type=jnp.float32)
    w_down_grad = jnp.einsum(
        "secf,secd->efd", expert_act, grad_recv, preferred_element_type=jnp.float32
    )
    gate_grad = (act_grad * up_pre * gate_sigmoid * (1.0 + gate_pre * (1.0 - gate_sigmoid))).astype(
        jnp.bfloat16
    )
    up_grad = (act_grad * gate_silu).astype(jnp.bfloat16)
    w_gate_grad = jnp.einsum(
        "secd,secf->edf", received, gate_grad, preferred_element_type=jnp.float32
    )
    w_up_grad = jnp.einsum("secd,secf->edf", received, up_grad, preferred_element_type=jnp.float32)
    rows_grad = (
        jnp.einsum("secf,edf->secd", gate_grad, w_gate, preferred_element_type=jnp.float32)
        + jnp.einsum("secf,edf->secd", up_grad, w_up, preferred_element_type=jnp.float32)
    ).astype(jnp.bfloat16)
    grad_back = lax.all_to_all(rows_grad, "dp", split_axis=0, concat_axis=0, tiled=True).reshape(
        experts * capacity, model_width
    )
    routed_in_grad = jnp.sum(
        grad_back[slot_index].astype(jnp.float32) * kept_float[:, :, None], axis=1
    )
    gate_grad_part = jnp.sum(gathered * cot_float[:, None, :], axis=-1) * kept_float
    shared_act_grad = jnp.einsum(
        "td,fd->tf", cotangent, shared_down_weight, preferred_element_type=jnp.float32
    )
    shared_down_grad = jnp.einsum(
        "tf,td->fd", shared_act, cotangent, preferred_element_type=jnp.float32
    )
    shared_gate_grad = (
        shared_act_grad * shared_up * shared_sigmoid * (1.0 + shared_gate * (1.0 - shared_sigmoid))
    ).astype(jnp.bfloat16)
    shared_up_grad = (shared_act_grad * shared_silu).astype(jnp.bfloat16)
    shared_gate_weight_grad = jnp.einsum(
        "td,tf->df", normed_ffn_low, shared_gate_grad, preferred_element_type=jnp.float32
    )
    shared_up_weight_grad = jnp.einsum(
        "td,tf->df", normed_ffn_low, shared_up_grad, preferred_element_type=jnp.float32
    )
    shared_in_grad = jnp.einsum(
        "tf,df->td", shared_gate_grad, shared_gate_weight, preferred_element_type=jnp.float32
    ) + jnp.einsum(
        "tf,df->td", shared_up_grad, shared_up_weight, preferred_element_type=jnp.float32
    )
    ffn_in_sum, gate_grad_sum = lax.psum(
        (routed_in_grad + shared_in_grad, gate_grad_part), "tensor"
    )
    picked_grad = (
        gate_grad_sum - jnp.sum(gate_grad_sum * gates, axis=-1, keepdims=True)
    ) / picked_total
    probs_grad = jnp.sum(jnp.where(route_hits, picked_grad[:, :, None], 0.0), axis=1)
    logit_grad = (
        router_probs * (probs_grad - jnp.sum(router_probs * probs_grad, axis=-1, keepdims=True))
    ).astype(jnp.bfloat16)
    router_grad = jnp.einsum(
        "td,te->de", normed_ffn_low, logit_grad, preferred_element_type=jnp.float32
    )
    ffn_in = ffn_in_sum + jnp.einsum(
        "te,de->td", logit_grad, router_weight, preferred_element_type=jnp.float32
    )
    ffn_resid_grad, gain_ffn_grad = norm_backward(resid_mid, inverse_ffn, gain_ffn_f, ffn_in)
    mid_grad = cot_float + ffn_resid_grad
    mid_low = mid_grad.astype(jnp.bfloat16)
    output_weight_grad = jnp.einsum(
        "th,td->hd", heads_low, mid_low, preferred_element_type=jnp.float32
    )
    heads_grad = (
        jnp.einsum("td,hd->th", mid_low, output_weight, preferred_element_type=jnp.float32)
        .astype(jnp.bfloat16)
        .reshape(tok_count, heads_here, V_HEAD)
    )
    query_grad_blocks = []
    key_grad = jnp.zeros((tok_count, heads_here, head_width), jnp.float32)
    value_grad = jnp.zeros((tok_count, heads_here, V_HEAD), jnp.float32)
    for block_number, row_start in enumerate(range(0, tok_count, tok_count)):
        row_stop = row_start + tok_count
        masked = block_scores(query_low, key_full, seq_ids, row_start)
        attn_probs = jnp.exp(masked - log_totals[block_number])
        probs_low = attn_probs.astype(jnp.bfloat16)
        prob_grad = jnp.einsum(
            "qhc,khc->hqk", heads_grad, value_low, preferred_element_type=jnp.float32
        )
        row_dot = jnp.sum(attn_probs * prob_grad, axis=-1, keepdims=True)
        score_grad = (attn_probs * (prob_grad - row_dot)).astype(jnp.bfloat16)
        query_grad_blocks.append(
            jnp.einsum("hqk,khc->qhc", score_grad, key_full, preferred_element_type=jnp.float32)
            * softmax_scale
        )
        key_grad = key_grad.at[:row_stop].add(
            jnp.einsum("hqk,qhc->khc", score_grad, query_low, preferred_element_type=jnp.float32)
            * softmax_scale
        )
        value_grad = value_grad.at[:row_stop].add(
            jnp.einsum("hqk,qhc->khc", probs_low, heads_grad, preferred_element_type=jnp.float32)
        )
    query_grad = query_grad_blocks[0]
    query_pre_grad = jnp.concatenate(
        [
            query_grad[..., :QK_NOPE],
            rotate(query_grad[..., QK_NOPE:], cosine[:, None, :], -sine_part[:, None, :]),
        ],
        axis=-1,
    )
    query_pre_grad = query_pre_grad.astype(jnp.bfloat16).reshape(tok_count, heads_here * head_width)
    attn_in_part = jnp.einsum(
        "tq,dq->td", query_pre_grad, query_weight, preferred_element_type=jnp.float32
    )
    query_weight_grad = jnp.einsum(
        "td,tq->dq", normed_attn_low, query_pre_grad, preferred_element_type=jnp.float32
    )
    expand_grad = (
        jnp.concatenate([key_grad[..., :QK_NOPE], value_grad], axis=-1)
        .astype(jnp.bfloat16)
        .reshape(tok_count, heads_here * (QK_NOPE + V_HEAD))
    )
    latent_part_grad = jnp.einsum(
        "te,re->tr", expand_grad, expand_weight, preferred_element_type=jnp.float32
    )
    expand_weight_grad = jnp.einsum(
        "tr,te->re", latent_low, expand_grad, preferred_element_type=jnp.float32
    )
    rope_part_grad = jnp.sum(key_grad[..., QK_NOPE:], axis=1)
    attn_in_sum, latent_sum, rope_sum = lax.psum(
        (attn_in_part, latent_part_grad, rope_part_grad), "tensor"
    )
    latent_pre_grad, gain_latent_grad = norm_backward(
        latent_part, inverse_latent, gain_latent_f, latent_sum
    )
    latent_all_grad = jnp.concatenate(
        [latent_pre_grad, rotate(rope_sum, cosine, -sine_part)], axis=-1
    ).astype(jnp.bfloat16)
    attn_in = attn_in_sum + jnp.einsum(
        "tc,dc->td", latent_all_grad, latent_weight, preferred_element_type=jnp.float32
    )
    latent_weight_grad = jnp.einsum(
        "td,tc->dc", normed_attn_low, latent_all_grad, preferred_element_type=jnp.float32
    )
    input_grad, gain_attn_grad = norm_backward(resid_in, inverse_attn, gain_attn_f, attn_in)
    tokens_grad = (mid_grad + input_grad).astype(jnp.bfloat16)
    (
        gain_attn_share,
        query_share,
        latent_share,
        gain_latent_share,
        expand_share,
        output_share,
        gain_ffn_share,
        router_share,
        shared_gate_share,
        shared_up_share,
        shared_down_share,
    ) = (
        lax.psum_scatter(
            gain_attn_grad.astype(jnp.bfloat16), "dp", scatter_dimension=0, tiled=True
        ).astype(jnp.float32),
        lax.psum_scatter(
            query_weight_grad.astype(jnp.bfloat16), "dp", scatter_dimension=0, tiled=True
        ).astype(jnp.float32),
        lax.psum_scatter(
            latent_weight_grad.astype(jnp.bfloat16), "dp", scatter_dimension=0, tiled=True
        ).astype(jnp.float32),
        lax.psum_scatter(
            gain_latent_grad.astype(jnp.bfloat16), "dp", scatter_dimension=0, tiled=True
        ).astype(jnp.float32),
        lax.psum_scatter(
            expand_weight_grad.astype(jnp.bfloat16), "dp", scatter_dimension=0, tiled=True
        ).astype(jnp.float32),
        lax.psum_scatter(
            output_weight_grad.astype(jnp.bfloat16), "dp", scatter_dimension=1, tiled=True
        ).astype(jnp.float32),
        lax.psum_scatter(
            gain_ffn_grad.astype(jnp.bfloat16), "dp", scatter_dimension=0, tiled=True
        ).astype(jnp.float32),
        lax.psum_scatter(
            router_grad.astype(jnp.bfloat16), "dp", scatter_dimension=0, tiled=True
        ).astype(jnp.float32),
        lax.psum_scatter(
            shared_gate_weight_grad.astype(jnp.bfloat16), "dp", scatter_dimension=0, tiled=True
        ).astype(jnp.float32),
        lax.psum_scatter(
            shared_up_weight_grad.astype(jnp.bfloat16), "dp", scatter_dimension=0, tiled=True
        ).astype(jnp.float32),
        lax.psum_scatter(
            shared_down_grad.astype(jnp.bfloat16), "dp", scatter_dimension=1, tiled=True
        ).astype(jnp.float32),
    )
    return (
        result,
        tokens_grad,
        gain_attn_share,
        query_share,
        latent_share,
        gain_latent_share,
        expand_share,
        output_share,
        gain_ffn_share,
        router_share,
        shared_gate_share,
        shared_up_share,
        shared_down_share,
        w_gate_grad,
        w_up_grad,
        w_down_grad,
    )

def hop(values, axis, bit):
    return lax.ppermute(values, axis, [(i, i ^ bit) for i in range(lax.axis_size(axis))])


def core_hop(values):
    return hop(values, "tensor", 1)


def y_hop(values):
    return hop(values, "tensor", 2)


def x_hop(values):
    return hop(values, "dp", 1)


def z_hop(values):
    count = lax.axis_size("dp")
    return lax.ppermute(values, "dp", [(i, (i + 2) % count) for i in range(count)])


def low(values):
    return values.astype(jnp.bfloat16)


class Flow:
    def __init__(self):
        self.tasks = []

    def launch(self, steps):
        task = Task(steps)
        self.tasks.append(task)
        return task

    def close(self, values):
        live = [task for task in self.tasks if not task.done]
        values, arrived = lax.optimization_barrier((values, [task.sent for task in live]))
        for task, got in zip(live, arrived):
            task.advance(got)
        return values


class Task:
    def __init__(self, steps):
        self.steps, self.done, self.result = steps, False, None
        self.advance(None)

    def advance(self, got):
        try:
            self.sent = self.steps.send(got)
        except StopIteration as stop:
            self.done, self.result = True, stop.value


def held(values, count):
    for _ in range(count):
        (values,) = yield [values]
    return values


def passing(values):
    (got,) = yield [z_hop(values)]
    return got


def plane_gather_split(own):
    half = own.shape[0] // 2
    first, second = own[:half], own[half:]
    first_x, second_y = yield [x_hop(first), y_hop(second)]
    first_pair = jnp.concatenate([first, first_x])
    second_pair = jnp.concatenate([second, second_y])
    first_y, second_x = yield [y_hop(first_pair), x_hop(second_pair)]
    quarter = jnp.concatenate(
        [
            own,
            first_x,
            second_x[:half],
            first_y[:half],
            second_y,
            first_y[half:],
            second_x[half:],
        ]
    )
    (far,) = yield [core_hop(quarter)]
    return jnp.concatenate([quarter, far])


def plane_gather(own, before=0):
    (far,) = yield [x_hop(own)]
    far = yield from held(far, before)
    pair = jnp.concatenate([own, far])
    (far,) = yield [y_hop(pair)]
    quarter = jnp.concatenate([pair, far])
    (far,) = yield [core_hop(quarter)]
    return jnp.concatenate([quarter, far])


def plane_scatter(part, x_first, before=0, between=0):
    part = part.reshape(2, 2, 2, part.shape[0] // 8, part.shape[1])
    (far,) = yield [core_hop(part[1])]
    far = yield from held(far, before)
    total = part[0].astype(jnp.float32) + far.astype(jnp.float32)
    near, away = (total[:, 0], total[:, 1]) if x_first else (total[0], total[1])
    (far,) = yield [x_hop(low(away)) if x_first else y_hop(low(away))]
    far = yield from held(far, between)
    near = near + far.astype(jnp.float32)
    (far,) = yield [y_hop(low(near[1])) if x_first else x_hop(low(near[1]))]
    return near[0] + far.astype(jnp.float32)


def tensor_scatter(values, tensor_index):
    rows = values.shape[0] // 4
    width = values.shape[1]
    core = tensor_index % 2
    level = tensor_index // 2
    blocks = values.reshape(2, 2, rows, width)
    mine = lax.dynamic_index_in_dim(blocks, core, 1, keepdims=False)
    other = lax.dynamic_index_in_dim(blocks, 1 - core, 1, keepdims=False)
    total = mine.astype(jnp.float32) + core_hop(low(other)).astype(jnp.float32)
    near = lax.dynamic_index_in_dim(total, level, 0, keepdims=False)
    far = lax.dynamic_index_in_dim(total, 1 - level, 0, keepdims=False)
    return near + y_hop(low(far)).astype(jnp.float32)


def tensor_gather(own, tensor_index):
    own_y = y_hop(own)
    pair = jnp.stack([own, own_y])
    pair_core = core_hop(pair)
    core = tensor_index % 2
    level = tensor_index // 2
    even = jnp.where(core == 0, pair, pair_core)
    odd = jnp.where(core == 0, pair_core, pair)
    near = jnp.concatenate([even[0], odd[0]])
    far = jnp.concatenate([even[1], odd[1]])
    return jnp.concatenate(
        [jnp.where(level == 0, near, far), jnp.where(level == 0, far, near)]
    )


def laid_out(arrived, axes, dp_index):
    planes = len(arrived[0]) // 2
    plane = dp_index // 2
    side = dp_index % 2
    wholes = []
    for pieces, axis in zip(arrived, axes):
        extent = pieces[0].shape[axis]
        shape = list(pieces[0].shape)
        shape[axis] *= 2 * planes
        whole = jnp.zeros(shape, pieces[0].dtype)
        for k, piece in enumerate(pieces):
            home = (plane - k // 2) % planes * 2 + (side if k % 2 == 0 else 1 - side)
            whole = lax.dynamic_update_slice_in_dim(whole, piece, home * extent, axis)
        wholes.append(whole)
    return wholes


def dp_ring(pieces, axes, dp_index):
    planes = lax.axis_size("dp") // 2
    arrived = [[] for _ in axes]
    for step in range(planes):
        sent = [x_hop(piece) for piece in pieces]
        if step + 1 < planes:
            sent += [z_hop(piece) for piece in pieces]
        got = yield sent
        for i in range(len(axes)):
            arrived[i] += [pieces[i], got[i]]
        pieces = got[len(axes) :]
    return laid_out(arrived, axes, dp_index)


def side_ring(own, dp_index, tensor_index):
    steps = dp_ring([own], [1], dp_index)
    sent = next(steps)
    while True:
        try:
            sent = steps.send(sent)
        except StopIteration as stop:
            (whole,) = stop.value
            break
    (far,) = yield [y_hop(whole)]
    pair = jnp.stack([whole, far])
    (far,) = yield [core_hop(pair)]
    core = tensor_index % 2
    level = tensor_index // 2
    even = jnp.where(core == 0, pair, far)
    odd = jnp.where(core == 0, far, pair)
    near = jnp.stack([even, odd], axis=1)
    whole = jnp.where(level == 0, near, near[::-1])
    return whole.reshape((4 * own.shape[0],) + whole.shape[3:])


def dp_scatter_steps(block, dp_index):
    planes = lax.axis_size("dp") // 2
    plane = dp_index // 2
    side = dp_index % 2
    bases = [(plane - step) % planes * 2 for step in list(range(1, planes)) + [0]]
    half = len(bases) // 2
    away = [low(block(base + 1 - side)) for base in bases]
    first, second = yield [x_hop(jnp.stack(away[:half])), x_hop(jnp.stack(away[half:]))]
    received = [first[i] for i in range(half)] + [second[i] for i in range(len(bases) - half)]
    moving = None
    for base, far in zip(bases, received):
        piece = block(base + side) + far.astype(jnp.float32)
        if moving is not None:
            (got,) = yield [z_hop(low(moving))]
            piece = piece + got.astype(jnp.float32)
        moving = piece
    return moving


def drained(task):
    while not task.done:
        task.advance(task.sent)
    return task.result


def dp_scatter(block, dp_index):
    return drained(Task(dp_scatter_steps(block, dp_index)))


def padded(values, axis, size):
    pads = [(0, 0)] * values.ndim
    pads[axis] = (0, size - values.shape[axis])
    return jnp.pad(values, pads)


def lanes(size):
    return -(-size // 128) * 128


def body_dense(
    tokens,
    cotangent,
    routes,
    seq_ids,
    positions,
    gain_attn,
    w_query,
    w_latent,
    gain_latent,
    w_expand,
    w_output,
    gain_ffn,
    w_router,
    w_shared_gate,
    w_shared_up,
    w_shared_down,
    w_gate,
    w_up,
    w_down,
):
    tensor_size = lax.axis_size("tensor")
    dp_size = lax.axis_size("dp")
    dp_index = lax.axis_index("dp")
    tensor_index = lax.axis_index("tensor")
    tok_count, width = tokens.shape
    own_count = tok_count // tensor_size
    own_start = tensor_index * own_count
    experts = w_router.shape[1]
    exp_here = w_gate.shape[0]
    capacity = tensor_size * -(-(5 * tok_count * TOP) // (4 * experts * tensor_size))

    def own_rows(values):
        return lax.dynamic_slice_in_dim(values, own_start, own_count, 0)

    lat_width = w_latent.shape[1]
    lat_block = w_latent.shape[0]
    routed = jnp.sum(
        (routes[:, :, None] == jnp.arange(experts, dtype=jnp.int32)[None, None, :]).astype(
            jnp.float32
        ),
        axis=1,
    )
    order = jnp.arange(tok_count, dtype=jnp.int32)
    earlier = (order[None, :] < order[:, None]).astype(jnp.bfloat16)
    rank = jnp.dot(earlier, low(routed), preferred_element_type=jnp.float32)
    standing = routed * (1.0 + (rank < capacity).astype(jnp.float32))
    standing_own = own_rows(standing)
    cot_own = own_rows(cotangent)

    folds = tok_count // lat_block
    mark_start = lat_width + experts
    gain_start = mark_start + folds * experts
    side_rows = lanes(gain_start + 3)
    side = jnp.concatenate(
        [w_latent.T, w_router.T]
        + [
            low(standing[fold * lat_block : (fold + 1) * lat_block]).T
            for fold in range(folds)
        ]
        + [jnp.stack([gain_attn, gain_ffn, padded(gain_latent, 0, lat_block)])]
    )
    side_rows_here = side_rows // tensor_size
    side = lax.dynamic_slice_in_dim(
        padded(side, 0, side_rows), tensor_index * side_rows_here, side_rows_here, 0
    )

    flow = Flow()
    side_task = flow.launch(side_ring(side, dp_index, tensor_index))
    unit = w_output.shape[1]
    query_rows = w_query.shape[0] * w_query.shape[1] // unit
    expand_rows = w_expand.shape[0] * w_expand.shape[1] // unit

    def columns(values):
        return [values[:, i : i + unit] for i in range(0, values.shape[1], unit)]

    pack = jnp.concatenate(columns(w_query) + columns(w_expand) + [w_output])
    weight_task = flow.launch(dp_ring([pack], [0], dp_index))
    for _ in range(2):
        flow.close(())

    core = tensor_index % 2
    level = tensor_index // 2
    planes = dp_size // 2
    side_all = side_task.result
    latent_weight = side_all[:lat_width]
    router_weight = side_all[lat_width:mark_start]
    marks_all = side_all[mark_start:gain_start].reshape(folds, experts, dp_size, lat_block)
    marks_all = marks_all.transpose(2, 0, 3, 1).reshape(planes, 8, own_count, experts)
    gains_all = side_all[gain_start : gain_start + 3].astype(jnp.float32)
    gain_attn_f = gains_all[0]
    gain_ffn_f = gains_all[1]
    gain_latent_f = gains_all[2].reshape(dp_size, lat_block)[:, : gain_latent.shape[0]].reshape(
        KV_RANK
    )
    near = jnp.arange(8, dtype=jnp.int32)
    near_x = near % 2 ^ dp_index % 2
    near_y = near // 2 % 2 ^ level
    near_core = near // 4 ^ core
    near_block = near_x * 4 + near_y * 2 + near_core
    mark_chunks = [
        jnp.take(
            lax.dynamic_index_in_dim(
                marks_all, (dp_index // 2 - step) % planes, 0, keepdims=False
            ),
            near_block,
            axis=0,
        ).reshape(8 * own_count, experts)
        for step in range(planes)
    ]
    flow.close(())
    cot_pass = flow.launch(passing(cot_own))

    head_width = QK_NOPE + QK_ROPE
    heads_here = w_query.shape[1] // head_width
    softmax_scale = head_width ** (-0.5)
    resid_in = tokens.astype(jnp.float32)
    normed_attn, inverse_attn = norm_forward(resid_in, gain_attn_f)
    normed_attn_low = low(normed_attn)
    cosine, sine_part = rope_tables(positions, QK_ROPE)
    latent_raw = jnp.einsum(
        "td,cd->tc", normed_attn_low, latent_weight, preferred_element_type=jnp.float32
    )
    latent_part = latent_raw[:, :KV_RANK]
    latent_normed, inverse_latent = norm_forward(latent_part, gain_latent_f)
    latent_low = low(latent_normed)
    key_rope_low = low(rotate(latent_raw[:, KV_RANK:], cosine, sine_part))
    normed_attn_low, latent_low, key_rope_low, w_shared_gate, w_shared_up, w_shared_down = (
        flow.close(
            (normed_attn_low, latent_low, key_rope_low, w_shared_gate, w_shared_up, w_shared_down)
        )
    )

    (packed,) = weight_task.result
    packed = packed.reshape(dp_size, pack.shape[0], unit)

    def rejoined(values, rows):
        values = values.reshape(dp_size, -1, rows, unit).transpose(0, 2, 1, 3)
        return values.reshape(dp_size * rows, -1)

    query_weight = rejoined(packed[:, :query_rows], w_query.shape[0])
    expand_weight = rejoined(packed[:, query_rows : query_rows + expand_rows], w_expand.shape[0])
    output_weight = packed[:, query_rows + expand_rows :].transpose(1, 0, 2)
    output_weight = output_weight.reshape(w_output.shape[0], width)
    cot_tasks = [flow.launch(plane_gather(cot_own))]
    cot_piece = cot_pass.result
    cot_pass = flow.launch(passing(cot_piece))
    query_raw = jnp.dot(normed_attn_low, query_weight, preferred_element_type=jnp.float32).reshape(
        tok_count, heads_here, head_width
    )
    query_low = low(
        jnp.concatenate(
            [
                query_raw[..., :QK_NOPE],
                rotate(query_raw[..., QK_NOPE:], cosine[:, None, :], sine_part[:, None, :]),
            ],
            axis=-1,
        )
    )
    expanded = low(jnp.dot(latent_low, expand_weight, preferred_element_type=jnp.float32))
    query_low, expanded = flow.close((query_low, expanded))

    cot_tasks.append(flow.launch(plane_gather(cot_piece, 4)))
    cot_piece = cot_pass.result
    cot_pass = flow.launch(passing(cot_piece))
    expanded = expanded.reshape(tok_count, heads_here, QK_NOPE + V_HEAD)
    value_low = expanded[..., QK_NOPE:]
    key_full = jnp.concatenate(
        [
            expanded[..., :QK_NOPE],
            jnp.broadcast_to(key_rope_low[:, None, :], (tok_count, heads_here, QK_ROPE)),
        ],
        axis=-1,
    )
    masked = block_scores(query_low, key_full, seq_ids, 0)
    row_max = jnp.max(masked, axis=-1, keepdims=True)
    exponent = jnp.exp(masked - row_max)
    exp_total = jnp.sum(exponent, axis=-1, keepdims=True)
    probs_low = low(exponent / exp_total)
    log_total = row_max + jnp.log(exp_total)
    heads_low = low(
        jnp.einsum("hqk,khc->qhc", probs_low, value_low, preferred_element_type=jnp.float32)
    ).reshape(tok_count, heads_here * V_HEAD)
    attn_part = jnp.dot(heads_low, output_weight, preferred_element_type=jnp.float32)
    attn_part = flow.close(attn_part)

    cot_tasks.append(flow.launch(plane_gather(cot_piece, 6)))
    cot_piece = cot_pass.result
    resid_own = own_rows(tokens).astype(jnp.float32) + tensor_scatter(attn_part, tensor_index)
    normed_own, inverse_own = norm_forward(resid_own, gain_ffn_f)
    normed_own_low = flow.close(low(normed_own))

    row_tasks = [flow.launch(plane_gather_split(normed_own_low))]
    row_pass = flow.launch(passing(normed_own_low))
    shared_here = w_shared_gate.shape[1] // dp_size
    shared = lax.all_to_all(
        jnp.stack([w_shared_gate.T, w_shared_up.T, w_shared_down]),
        "dp",
        split_axis=1,
        concat_axis=2,
        tiled=True,
    )
    group = w_gate.shape[2]
    routed_here = exp_here * group
    hidden = routed_here + shared_here
    gate_weight = jnp.concatenate([w_gate.swapaxes(1, 2).reshape(routed_here, width), shared[0]])
    up_weight = jnp.concatenate([w_up.swapaxes(1, 2).reshape(routed_here, width), shared[1]])
    down_weight = jnp.concatenate([w_down.reshape(routed_here, width), shared[2]])
    gate_weight, up_weight, down_weight = flow.close((gate_weight, up_weight, down_weight))
    for _ in range(2):
        flow.close(())

    def gating(rows, standing_rows):
        probs = jax.nn.softmax(
            jnp.einsum("td,ed->te", rows, router_weight, preferred_element_type=jnp.float32),
            axis=-1,
        )
        gates = jnp.where(standing_rows > 0.5, probs, 0.0)
        picked = jnp.sum(gates, axis=-1, keepdims=True)
        return probs, gates / picked, picked

    expert_index = jnp.arange(experts, dtype=jnp.int32)[None, :]
    column = jnp.arange(hidden, dtype=jnp.int32)[None, :]
    row_piece = row_pass.result
    in_tasks, out_tasks, gate_parts, kept_parts = [], [], [], []
    in_part = None
    for step in range(planes):
        rows = row_tasks[step].result
        if step + 1 < planes:
            row_tasks.append(flow.launch(plane_gather(row_piece)))
            if step + 2 < planes:
                row_pass = flow.launch(passing(row_piece))
        if step > 0:
            in_tasks.append(flow.launch(plane_scatter(in_part, True)))
        if step == planes - 1:
            in_moving = flow.launch(passing(low(in_tasks[1].result)))
        gate_pre = jnp.einsum("td,fd->tf", rows, gate_weight, preferred_element_type=jnp.float32)
        up_pre = jnp.einsum("td,fd->tf", rows, up_weight, preferred_element_type=jnp.float32)
        gate_pre, up_pre, rows = flow.close((gate_pre, up_pre, rows))
        if step + 2 < planes:
            row_piece = row_pass.result

        cots = cot_tasks[step].result
        marks = mark_chunks[step].astype(jnp.float32)
        _, chunk_gates, _ = gating(rows, marks)
        chunk_gates = jnp.where(marks > 1.5, chunk_gates, 0.0)
        scale = jnp.ones((rows.shape[0], hidden), jnp.float32)
        for e in reversed(range(exp_here)):
            here = expert_index == dp_index * exp_here + e
            gate_column = jnp.sum(jnp.where(here, chunk_gates, 0.0), axis=-1, keepdims=True)
            scale = jnp.where(column < (e + 1) * group, gate_column, scale)
        sigmoid = jax.nn.sigmoid(gate_pre)
        silu = gate_pre * sigmoid
        act = silu * up_pre
        act_scaled = low(act * scale)
        out_part = low(jnp.dot(act_scaled, down_weight, preferred_element_type=jnp.float32))
        act_grad = jnp.einsum("td,fd->tf", cots, down_weight, preferred_element_type=jnp.float32)
        meeting = act * act_grad
        gate_parts.append(
            jnp.stack(
                [
                    jnp.sum(jnp.where(column // group == e, meeting, 0.0), axis=-1)
                    for e in range(exp_here)
                ]
            )
        )
        scaled_grad = act_grad * scale
        gate_grad = low(scaled_grad * up_pre * sigmoid * (1.0 + gate_pre * (1.0 - sigmoid)))
        up_grad = low(scaled_grad * silu)
        gate_grad, up_grad, act_scaled, out_part, rows, cots = flow.close(
            (gate_grad, up_grad, act_scaled, out_part, rows, cots)
        )

        after = (planes - 1 - step) * 3
        places = {0: (after + 6, 0), 1: (after, 1), 2: (after + 3, 0), 3: (after + 5, 0)}[step]
        out_tasks.append(flow.launch(plane_scatter(out_part, False, *places)))
        if step == 0:
            cot_tasks.append(flow.launch(plane_gather(cot_piece, 3)))
        in_part = low(
            jnp.dot(gate_grad, gate_weight, preferred_element_type=jnp.float32)
            + jnp.dot(up_grad, up_weight, preferred_element_type=jnp.float32)
        )
        in_part, gate_grad, up_grad, act_scaled, rows, cots = flow.close(
            (in_part, gate_grad, up_grad, act_scaled, rows, cots)
        )
        kept_parts.append((rows, cots, gate_grad, up_grad, act_scaled))

    in_tasks.append(flow.launch(plane_scatter(in_part, True)))
    in_moving = flow.launch(
        passing(low(in_tasks[2].result + in_moving.result.astype(jnp.float32)))
    )
    kept_parts = flow.close(kept_parts)
    gate_weight_grad = sum(
        jnp.einsum("tf,td->fd", gate_grad, rows, preferred_element_type=jnp.float32)
        for rows, _, gate_grad, _, _ in kept_parts
    )
    gate_weight_grad, kept_parts = flow.close((gate_weight_grad, kept_parts))
    flow.close(())
    in_moving = flow.launch(
        passing(low(in_tasks[3].result + in_moving.result.astype(jnp.float32)))
    )
    out_moving = flow.launch(passing(low(out_tasks[1].result)))

    kept_parts = flow.close(kept_parts)
    ffn_sum = in_tasks[0].result + in_moving.result.astype(jnp.float32)
    gate_sums = jnp.stack(gate_parts).reshape(-1, exp_here, 2, 2, 2, own_count)
    gate_sums = gate_sums[:, :, 0] + core_hop(gate_sums[:, :, 1])
    gate_sums = gate_sums[:, :, 0] + y_hop(gate_sums[:, :, 1])
    block = jnp.arange(dp_size, dtype=jnp.int32)
    place = ((dp_index // 2 - block // 2) % planes) * 2 + (block + dp_index) % 2
    gate_sums = gate_sums.transpose(0, 2, 1, 3).reshape(dp_size, exp_here, own_count)[place]
    gate_sums = lax.all_to_all(gate_sums, "dp", split_axis=0, concat_axis=0, tiled=True)
    gate_sums = gate_sums.reshape(experts, own_count).T

    probs_own, gates_own, picked_own = gating(normed_own_low, standing_own)
    gate_sums = jnp.where(standing_own > 1.5, gate_sums, 0.0)
    picked_grad = (
        gate_sums - jnp.sum(gate_sums * gates_own, axis=-1, keepdims=True)
    ) / picked_own
    probs_grad = jnp.where(standing_own > 0.5, picked_grad, 0.0)
    logit_grad = low(
        probs_own * (probs_grad - jnp.sum(probs_own * probs_grad, axis=-1, keepdims=True))
    )
    router_grad = jnp.einsum(
        "te,td->ed", logit_grad, normed_own_low, preferred_element_type=jnp.float32
    )
    ffn_in = ffn_sum + jnp.dot(logit_grad, router_weight, preferred_element_type=jnp.float32)
    ffn_resid_grad, gain_ffn_grad = norm_backward(resid_own, inverse_own, gain_ffn_f, ffn_in)
    mid_grad_own = cot_own.astype(jnp.float32) + ffn_resid_grad
    mid_low, kept_parts = flow.close(
        (tensor_gather(low(mid_grad_own), tensor_index), kept_parts)
    )
    up_weight_grad = sum(
        jnp.einsum("tf,td->fd", up_grad, rows, preferred_element_type=jnp.float32)
        for rows, _, _, up_grad, _ in kept_parts
    )
    out_moving = flow.launch(
        passing(low(out_tasks[2].result + out_moving.result.astype(jnp.float32)))
    )

    output_weight_grad = jnp.einsum(
        "th,td->hd", heads_low, mid_low, preferred_element_type=jnp.float32
    )
    heads_grad = low(
        jnp.einsum("td,hd->th", mid_low, output_weight, preferred_element_type=jnp.float32)
    ).reshape(tok_count, heads_here, V_HEAD)
    heads_grad, output_weight_grad, up_weight_grad, kept_parts = flow.close(
        (heads_grad, output_weight_grad, up_weight_grad, kept_parts)
    )
    down_weight_grad = sum(
        jnp.einsum("tf,td->fd", act_scaled, cots, preferred_element_type=jnp.float32)
        for _, cots, _, _, act_scaled in kept_parts
    )
    output_task = flow.launch(
        dp_scatter_steps(
            lambda i: lax.dynamic_slice_in_dim(
                output_weight_grad, i * w_output.shape[1], w_output.shape[1], 1
            ),
            dp_index,
        )
    )
    masked = block_scores(query_low, key_full, seq_ids, 0)
    attn_probs = jnp.exp(masked - log_total)
    prob_grad = jnp.einsum("qhc,khc->hqk", heads_grad, value_low, preferred_element_type=jnp.float32)
    row_dot = jnp.sum(attn_probs * prob_grad, axis=-1, keepdims=True)
    score_grad = low(attn_probs * (prob_grad - row_dot))
    score_grad, probs_low, down_weight_grad = flow.close(
        (score_grad, low(attn_probs), down_weight_grad)
    )
    out_moving = flow.launch(
        passing(low(out_tasks[3].result + out_moving.result.astype(jnp.float32)))
    )
    query_grad = (
        jnp.einsum("hqk,khc->qhc", score_grad, key_full, preferred_element_type=jnp.float32)
        * softmax_scale
    )
    key_grad = (
        jnp.einsum("hqk,qhc->khc", score_grad, query_low, preferred_element_type=jnp.float32)
        * softmax_scale
    )
    value_grad = jnp.einsum(
        "hqk,qhc->khc", probs_low, heads_grad, preferred_element_type=jnp.float32
    )
    query_grad, key_grad, value_grad = flow.close((query_grad, key_grad, value_grad))
    query_pre_grad = low(
        jnp.concatenate(
            [
                query_grad[..., :QK_NOPE],
                rotate(query_grad[..., QK_NOPE:], cosine[:, None, :], -sine_part[:, None, :]),
            ],
            axis=-1,
        )
    ).reshape(tok_count, heads_here * head_width)
    query_weight_grad = jnp.einsum(
        "td,tq->dq", normed_attn_low, query_pre_grad, preferred_element_type=jnp.float32
    )
    expand_grad = low(jnp.concatenate([key_grad[..., :QK_NOPE], value_grad], axis=-1)).reshape(
        tok_count, heads_here * (QK_NOPE + V_HEAD)
    )
    latent_grad = jnp.einsum(
        "te,re->tr", expand_grad, expand_weight, preferred_element_type=jnp.float32
    )
    expand_weight_grad = jnp.einsum(
        "tr,te->re", latent_low, expand_grad, preferred_element_type=jnp.float32
    )
    latent_grad, query_weight_grad, expand_weight_grad = flow.close(
        (latent_grad, query_weight_grad, expand_weight_grad)
    )
    rope_grad = jnp.sum(key_grad[..., QK_NOPE:], axis=1)
    latent_pre_grad, gain_latent_grad = norm_backward(
        latent_part, inverse_latent, gain_latent_f, latent_grad
    )
    latent_all_grad = low(
        jnp.concatenate([latent_pre_grad, rotate(rope_grad, cosine, -sine_part)], axis=-1)
    )
    attn_in = jnp.einsum(
        "tq,dq->td", query_pre_grad, query_weight, preferred_element_type=jnp.float32
    ) + jnp.dot(latent_all_grad, latent_weight, preferred_element_type=jnp.float32)
    latent_weight_grad = jnp.einsum(
        "tc,td->cd", latent_all_grad, normed_attn_low, preferred_element_type=jnp.float32
    )
    gain_attn_grad = jnp.sum(attn_in * (resid_in * inverse_attn), axis=0)
    attn_in_own = tensor_scatter(attn_in, tensor_index)
    input_grad, _ = norm_backward(
        own_rows(resid_in), own_rows(inverse_attn), gain_attn_f, attn_in_own
    )
    tokens_grad = tensor_gather(low(mid_grad_own + input_grad), tensor_index)

    out_sum = out_tasks[0].result + out_moving.result.astype(jnp.float32)
    result = tensor_gather(low(resid_own + out_sum), tensor_index)

    output_share = drained(output_task)
    query_share = dp_scatter(
        lambda i: lax.dynamic_slice_in_dim(query_weight_grad, i * lat_block, lat_block, 0),
        dp_index,
    )
    expand_block = w_expand.shape[0]
    expand_share = dp_scatter(
        lambda i: lax.dynamic_slice_in_dim(expand_weight_grad, i * expand_block, expand_block, 0),
        dp_index,
    )

    gain_latent_rows = padded(gain_latent_grad.reshape(dp_size, -1), 1, lat_block).reshape(width)
    gain_grads = jnp.stack([gain_attn_grad, gain_ffn_grad, gain_latent_rows])
    side_grad = jnp.concatenate(
        [
            low(latent_weight_grad),
            low(router_grad),
            padded(low(gain_grads), 0, side_rows - mark_start),
        ]
    ).reshape(2, 2, side_rows_here, width)
    kept_side = lax.dynamic_index_in_dim(side_grad, core, 1, keepdims=False)
    sent_side = lax.dynamic_index_in_dim(side_grad, 1 - core, 1, keepdims=False)
    side_grad = kept_side.astype(jnp.float32) + core_hop(sent_side).astype(jnp.float32)
    kept_side = lax.dynamic_index_in_dim(side_grad, level, 0, keepdims=False)
    sent_side = lax.dynamic_index_in_dim(side_grad, 1 - level, 0, keepdims=False)
    side_grad = kept_side + y_hop(low(sent_side)).astype(jnp.float32)
    side_piece = dp_scatter(
        lambda i: lax.dynamic_slice_in_dim(side_grad, i * lat_block, lat_block, 1), dp_index
    )
    grad_full = tensor_gather(low(side_piece), tensor_index).astype(jnp.float32)
    latent_share = grad_full[:lat_width].T
    router_share = grad_full[lat_width:mark_start].T
    gain_attn_share = grad_full[mark_start]
    gain_ffn_share = grad_full[mark_start + 1]
    gain_latent_share = grad_full[mark_start + 2, : gain_latent.shape[0]]

    def routed_grad(grad):
        return grad[:routed_here].reshape(exp_here, group, width)

    routed_grads = (
        routed_grad(gate_weight_grad).swapaxes(1, 2),
        routed_grad(up_weight_grad).swapaxes(1, 2),
        routed_grad(down_weight_grad),
    )
    shared_grads = jnp.stack(
        [low(grad[routed_here:]) for grad in (gate_weight_grad, up_weight_grad, down_weight_grad)]
    )
    shared_grads = lax.all_to_all(
        shared_grads, "dp", split_axis=2, concat_axis=1, tiled=True
    ).astype(jnp.float32)

    return (
        result,
        tokens_grad,
        gain_attn_share,
        query_share,
        latent_share,
        gain_latent_share,
        expand_share,
        output_share,
        gain_ffn_share,
        router_share,
        shared_grads[0].T,
        shared_grads[1].T,
        shared_grads[2],
        *routed_grads,
    )


def solution(mesh):
    dense = mesh.shape["dp"] == 8 and mesh.shape["tensor"] == 4
    return jax.shard_map(
        body_dense if dense else body,
        mesh=mesh,
        in_specs=(
            P("dp", None),
            P("dp", None),
            P("dp", None),
            P("dp"),
            P("dp"),
            P("dp"),
            P("dp", "tensor"),
            P("dp", None),
            P("dp"),
            P("dp", "tensor"),
            P("tensor", "dp"),
            P("dp"),
            P("dp", None),
            P("dp", "tensor"),
            P("dp", "tensor"),
            P("tensor", "dp"),
            P("dp", None, "tensor"),
            P("dp", None, "tensor"),
            P("dp", "tensor", None),
        ),
        out_specs=(
            P("dp", None),
            P("dp", None),
            P("dp"),
            P("dp", "tensor"),
            P("dp", None),
            P("dp"),
            P("dp", "tensor"),
            P("tensor", "dp"),
            P("dp"),
            P("dp", None),
            P("dp", "tensor"),
            P("dp", "tensor"),
            P("tensor", "dp"),
            P("dp", None, "tensor"),
            P("dp", None, "tensor"),
            P("dp", "tensor", None),
        ),
        check_vma=False,
    )
```

```python
import jax
import jax.numpy as jnp
from jax import lax
from jax.sharding import PartitionSpec as P

QK_NOPE = 128
QK_ROPE = 64
V_HEAD = 128
KV_RANK = 512
TOP = 6


EPSILON = 1e-06
MASKED = -1e30


def norm_forward(values, gain_full):
    inverse = lax.rsqrt(jnp.mean(values * values, axis=-1, keepdims=True) + EPSILON)
    return (values * inverse * gain_full, inverse)


def norm_backward(values, inverse, gain_full, grad_out):
    normed = values * inverse
    scaled = grad_out * gain_full
    grad_in = inverse * (scaled - normed * jnp.mean(scaled * normed, axis=-1, keepdims=True))
    return (grad_in, jnp.sum(grad_out * normed, axis=0))


def rope_tables(positions, width):
    half_width = width // 2
    frequency = jnp.power(10000.0, -jnp.arange(half_width, dtype=jnp.float32) / half_width)
    angles = positions.astype(jnp.float32)[:, None] * frequency[None, :]
    return (jnp.cos(angles), jnp.sin(angles))


def rotate(values, cosine, sine_part):
    half_width = values.shape[-1] // 2
    front_half = values[..., :half_width]
    back_half = values[..., half_width:]
    return jnp.concatenate(
        [front_half * cosine - back_half * sine_part, back_half * cosine + front_half * sine_part],
        axis=-1,
    )


def slot_layout(routes, experts, capacity):
    flat_routes = routes.reshape(-1)
    onehot = (flat_routes[:, None] == jnp.arange(experts, dtype=jnp.int32)[None, :]).astype(
        jnp.int32
    )
    before = jnp.cumsum(onehot, axis=0) - onehot
    slot_rank = jnp.sum(before * onehot, axis=1)
    route_kept = slot_rank < capacity
    slot_index = flat_routes * capacity + jnp.minimum(slot_rank, capacity - 1)
    return (slot_index.reshape(routes.shape), route_kept.reshape(routes.shape))


def slot_owner(slot_index, route_kept, kept_gates, slot_total):
    pair_count = slot_index.size
    target = jnp.where(route_kept.reshape(-1), slot_index.reshape(-1), slot_total)
    token_rows = jnp.arange(pair_count, dtype=jnp.int32) // slot_index.shape[-1]
    slot_token = jnp.zeros((slot_total,), jnp.int32).at[target].set(token_rows, mode="drop")
    slot_live = jnp.zeros((slot_total,), jnp.bool_).at[target].set(True, mode="drop")
    slot_gate = (
        jnp.zeros((slot_total,), jnp.float32).at[target].set(kept_gates.reshape(-1), mode="drop")
    )
    return (slot_token, slot_live, slot_gate)


def block_scores(query_block, key_block, seq_ids, row_start):
    row_count = query_block.shape[0]
    key_count = key_block.shape[0]
    raw_scores = jnp.einsum(
        "qhc,khc->hqk", query_block, key_block, preferred_element_type=jnp.float32
    ) * (QK_NOPE + QK_ROPE) ** (-0.5)
    query_index = row_start + jnp.arange(row_count, dtype=jnp.int32)
    key_index = jnp.arange(key_count, dtype=jnp.int32)
    allowed = (seq_ids[:, None] == seq_ids[None, :]) & (key_index[None, :] <= query_index[:, None])
    return jnp.where(allowed[None], raw_scores, MASKED)


def body(
    tokens,
    cotangent,
    routes,
    seq_ids,
    positions,
    gain_attn,
    w_query,
    w_latent,
    gain_latent,
    w_expand,
    w_output,
    gain_ffn,
    w_router,
    w_shared_gate,
    w_shared_up,
    w_shared_down,
    w_gate,
    w_up,
    w_down,
):
    (
        gain_attn_all,
        query_weight,
        latent_weight,
        gain_latent_all,
        expand_weight,
        output_weight,
        gain_ffn_all,
        router_weight,
        shared_gate_weight,
        shared_up_weight,
        shared_down_weight,
    ) = (
        lax.all_gather(gain_attn, "dp", axis=0, tiled=True),
        lax.all_gather(w_query, "dp", axis=0, tiled=True),
        lax.all_gather(w_latent, "dp", axis=0, tiled=True),
        lax.all_gather(gain_latent, "dp", axis=0, tiled=True),
        lax.all_gather(w_expand, "dp", axis=0, tiled=True),
        lax.all_gather(w_output, "dp", axis=1, tiled=True),
        lax.all_gather(gain_ffn, "dp", axis=0, tiled=True),
        lax.all_gather(w_router, "dp", axis=0, tiled=True),
        lax.all_gather(w_shared_gate, "dp", axis=0, tiled=True),
        lax.all_gather(w_shared_up, "dp", axis=0, tiled=True),
        lax.all_gather(w_shared_down, "dp", axis=1, tiled=True),
    )
    tok_count = tokens.shape[0]
    head_width = QK_NOPE + QK_ROPE
    heads_here = query_weight.shape[1] // head_width
    softmax_scale = head_width ** (-0.5)
    gain_attn_f = gain_attn_all.astype(jnp.float32)
    gain_latent_f = gain_latent_all.astype(jnp.float32)
    resid_in = tokens.astype(jnp.float32)
    normed_attn, inverse_attn = norm_forward(resid_in, gain_attn_f)
    normed_attn_low = normed_attn.astype(jnp.bfloat16)
    cosine, sine_part = rope_tables(positions, QK_ROPE)
    query_raw = jnp.dot(normed_attn_low, query_weight, preferred_element_type=jnp.float32).reshape(
        tok_count, heads_here, head_width
    )
    query_low = jnp.concatenate(
        [
            query_raw[..., :QK_NOPE],
            rotate(query_raw[..., QK_NOPE:], cosine[:, None, :], sine_part[:, None, :]),
        ],
        axis=-1,
    ).astype(jnp.bfloat16)
    latent_raw = jnp.dot(normed_attn_low, latent_weight, preferred_element_type=jnp.float32)
    latent_part = latent_raw[:, :KV_RANK]
    latent_normed, inverse_latent = norm_forward(latent_part, gain_latent_f)
    latent_low = latent_normed.astype(jnp.bfloat16)
    key_rope_low = rotate(latent_raw[:, KV_RANK:], cosine, sine_part).astype(jnp.bfloat16)
    expanded = (
        jnp.dot(latent_low, expand_weight, preferred_element_type=jnp.float32)
        .astype(jnp.bfloat16)
        .reshape(tok_count, heads_here, QK_NOPE + V_HEAD)
    )
    value_low = expanded[..., QK_NOPE:]
    key_full = jnp.concatenate(
        [
            expanded[..., :QK_NOPE],
            jnp.broadcast_to(key_rope_low[:, None, :], (tok_count, heads_here, QK_ROPE)),
        ],
        axis=-1,
    )
    row_start = 0
    row_stop = row_start + tok_count
    masked = block_scores(query_low, key_full, seq_ids, row_start)
    row_max = jnp.max(masked, axis=-1, keepdims=True)
    exponent = jnp.exp(masked - row_max)
    exp_total = jnp.sum(exponent, axis=-1, keepdims=True)
    attn_probs = (exponent / exp_total).astype(jnp.bfloat16)
    log_totals = [row_max + jnp.log(exp_total)]
    head_blocks = jnp.einsum(
        "hqk,khc->qhc", attn_probs, value_low, preferred_element_type=jnp.float32
    )
    heads_low = head_blocks.astype(jnp.bfloat16).reshape(tok_count, heads_here * V_HEAD)
    attn_part = jnp.dot(heads_low, output_weight, preferred_element_type=jnp.float32)
    resid_mid = resid_in + lax.psum(attn_part, "tensor")
    gain_ffn_f = gain_ffn_all.astype(jnp.float32)
    normed_ffn, inverse_ffn = norm_forward(resid_mid, gain_ffn_f)
    normed_ffn_low = normed_ffn.astype(jnp.bfloat16)
    experts = router_weight.shape[1]
    router_probs = jax.nn.softmax(
        jnp.dot(normed_ffn_low, router_weight, preferred_element_type=jnp.float32), axis=-1
    )
    route_hits = routes[:, :, None] == jnp.arange(experts, dtype=jnp.int32)[None, None, :]
    picked = jnp.sum(jnp.where(route_hits, router_probs[:, None, :], 0.0), axis=-1)
    picked_total = jnp.sum(picked, axis=-1, keepdims=True)
    gates = picked / picked_total
    tensor_size = lax.axis_size("tensor")
    dp_size = lax.axis_size("dp")
    exp_here = w_gate.shape[0]
    model_width = tokens.shape[1]
    capacity = tensor_size * -(-(5 * tok_count * TOP) // (4 * experts * tensor_size))
    slot_index, route_kept = slot_layout(routes, experts, capacity)
    kept_gates = jnp.where(route_kept, gates, 0.0)
    kept_float = route_kept.astype(jnp.float32)
    slot_token, slot_live, slot_gate = slot_owner(
        slot_index, route_kept, kept_gates, experts * capacity
    )
    send_rows = jnp.where(
        slot_live[:, None], normed_ffn_low[slot_token], jnp.zeros((), jnp.bfloat16)
    ).reshape(dp_size, exp_here, capacity, model_width)
    grad_send = (
        (cotangent[slot_token].astype(jnp.float32) * slot_gate[:, None])
        .astype(jnp.bfloat16)
        .reshape(dp_size, exp_here, capacity, model_width)
    )
    received, grad_recv = (
        lax.all_to_all(send_rows, "dp", split_axis=0, concat_axis=0, tiled=True),
        lax.all_to_all(grad_send, "dp", split_axis=0, concat_axis=0, tiled=True),
    )
    gate_pre = jnp.einsum("secd,edf->secf", received, w_gate, preferred_element_type=jnp.float32)
    up_pre = jnp.einsum("secd,edf->secf", received, w_up, preferred_element_type=jnp.float32)
    gate_sigmoid = jax.nn.sigmoid(gate_pre)
    gate_silu = gate_pre * gate_sigmoid
    expert_act = (gate_silu * up_pre).astype(jnp.bfloat16)
    expert_out = jnp.einsum(
        "secf,efd->secd", expert_act, w_down, preferred_element_type=jnp.float32
    ).astype(jnp.bfloat16)
    returned = lax.all_to_all(expert_out, "dp", split_axis=0, concat_axis=0, tiled=True).reshape(
        experts * capacity, model_width
    )
    gathered = returned[slot_index].astype(jnp.float32)
    routed_part = jnp.sum(gathered * kept_gates[:, :, None], axis=1)
    shared_gate = jnp.dot(normed_ffn_low, shared_gate_weight, preferred_element_type=jnp.float32)
    shared_up = jnp.dot(normed_ffn_low, shared_up_weight, preferred_element_type=jnp.float32)
    shared_sigmoid = jax.nn.sigmoid(shared_gate)
    shared_silu = shared_gate * shared_sigmoid
    shared_act = (shared_silu * shared_up).astype(jnp.bfloat16)
    shared_part = jnp.dot(shared_act, shared_down_weight, preferred_element_type=jnp.float32)
    moe_total = lax.psum((routed_part + shared_part).astype(jnp.bfloat16), "tensor").astype(
        jnp.float32
    )
    result = (resid_mid + moe_total).astype(jnp.bfloat16)
    cot_float = cotangent.astype(jnp.float32)
    act_grad = jnp.einsum("secd,efd->secf", grad_recv, w_down, preferred_element_type=jnp.float32)
    w_down_grad = jnp.einsum(
        "secf,secd->efd", expert_act, grad_recv, preferred_element_type=jnp.float32
    )
    gate_grad = (act_grad * up_pre * gate_sigmoid * (1.0 + gate_pre * (1.0 - gate_sigmoid))).astype(
        jnp.bfloat16
    )
    up_grad = (act_grad * gate_silu).astype(jnp.bfloat16)
    w_gate_grad = jnp.einsum(
        "secd,secf->edf", received, gate_grad, preferred_element_type=jnp.float32
    )
    w_up_grad = jnp.einsum("secd,secf->edf", received, up_grad, preferred_element_type=jnp.float32)
    rows_grad = (
        jnp.einsum("secf,edf->secd", gate_grad, w_gate, preferred_element_type=jnp.float32)
        + jnp.einsum("secf,edf->secd", up_grad, w_up, preferred_element_type=jnp.float32)
    ).astype(jnp.bfloat16)
    grad_back = lax.all_to_all(rows_grad, "dp", split_axis=0, concat_axis=0, tiled=True).reshape(
        experts * capacity, model_width
    )
    routed_in_grad = jnp.sum(
        grad_back[slot_index].astype(jnp.float32) * kept_float[:, :, None], axis=1
    )
    gate_grad_part = jnp.sum(gathered * cot_float[:, None, :], axis=-1) * kept_float
    shared_act_grad = jnp.einsum(
        "td,fd->tf", cotangent, shared_down_weight, preferred_element_type=jnp.float32
    )
    shared_down_grad = jnp.einsum(
        "tf,td->fd", shared_act, cotangent, preferred_element_type=jnp.float32
    )
    shared_gate_grad = (
        shared_act_grad * shared_up * shared_sigmoid * (1.0 + shared_gate * (1.0 - shared_sigmoid))
    ).astype(jnp.bfloat16)
    shared_up_grad = (shared_act_grad * shared_silu).astype(jnp.bfloat16)
    shared_gate_weight_grad = jnp.einsum(
        "td,tf->df", normed_ffn_low, shared_gate_grad, preferred_element_type=jnp.float32
    )
    shared_up_weight_grad = jnp.einsum(
        "td,tf->df", normed_ffn_low, shared_up_grad, preferred_element_type=jnp.float32
    )
    shared_in_grad = jnp.einsum(
        "tf,df->td", shared_gate_grad, shared_gate_weight, preferred_element_type=jnp.float32
    ) + jnp.einsum(
        "tf,df->td", shared_up_grad, shared_up_weight, preferred_element_type=jnp.float32
    )
    ffn_in_sum, gate_grad_sum = lax.psum(
        (routed_in_grad + shared_in_grad, gate_grad_part), "tensor"
    )
    picked_grad = (
        gate_grad_sum - jnp.sum(gate_grad_sum * gates, axis=-1, keepdims=True)
    ) / picked_total
    probs_grad = jnp.sum(jnp.where(route_hits, picked_grad[:, :, None], 0.0), axis=1)
    logit_grad = (
        router_probs * (probs_grad - jnp.sum(router_probs * probs_grad, axis=-1, keepdims=True))
    ).astype(jnp.bfloat16)
    router_grad = jnp.einsum(
        "td,te->de", normed_ffn_low, logit_grad, preferred_element_type=jnp.float32
    )
    ffn_in = ffn_in_sum + jnp.einsum(
        "te,de->td", logit_grad, router_weight, preferred_element_type=jnp.float32
    )
    ffn_resid_grad, gain_ffn_grad = norm_backward(resid_mid, inverse_ffn, gain_ffn_f, ffn_in)
    mid_grad = cot_float + ffn_resid_grad
    mid_low = mid_grad.astype(jnp.bfloat16)
    output_weight_grad = jnp.einsum(
        "th,td->hd", heads_low, mid_low, preferred_element_type=jnp.float32
    )
    heads_grad = (
        jnp.einsum("td,hd->th", mid_low, output_weight, preferred_element_type=jnp.float32)
        .astype(jnp.bfloat16)
        .reshape(tok_count, heads_here, V_HEAD)
    )
    query_grad_blocks = []
    key_grad = jnp.zeros((tok_count, heads_here, head_width), jnp.float32)
    value_grad = jnp.zeros((tok_count, heads_here, V_HEAD), jnp.float32)
    for block_number, row_start in enumerate(range(0, tok_count, tok_count)):
        row_stop = row_start + tok_count
        masked = block_scores(query_low, key_full, seq_ids, row_start)
        attn_probs = jnp.exp(masked - log_totals[block_number])
        probs_low = attn_probs.astype(jnp.bfloat16)
        prob_grad = jnp.einsum(
            "qhc,khc->hqk", heads_grad, value_low, preferred_element_type=jnp.float32
        )
        row_dot = jnp.sum(attn_probs * prob_grad, axis=-1, keepdims=True)
        score_grad = (attn_probs * (prob_grad - row_dot)).astype(jnp.bfloat16)
        query_grad_blocks.append(
            jnp.einsum("hqk,khc->qhc", score_grad, key_full, preferred_element_type=jnp.float32)
            * softmax_scale
        )
        key_grad = key_grad.at[:row_stop].add(
            jnp.einsum("hqk,qhc->khc", score_grad, query_low, preferred_element_type=jnp.float32)
            * softmax_scale
        )
        value_grad = value_grad.at[:row_stop].add(
            jnp.einsum("hqk,qhc->khc", probs_low, heads_grad, preferred_element_type=jnp.float32)
        )
    query_grad = query_grad_blocks[0]
    query_pre_grad = jnp.concatenate(
        [
            query_grad[..., :QK_NOPE],
            rotate(query_grad[..., QK_NOPE:], cosine[:, None, :], -sine_part[:, None, :]),
        ],
        axis=-1,
    )
    query_pre_grad = query_pre_grad.astype(jnp.bfloat16).reshape(tok_count, heads_here * head_width)
    attn_in_part = jnp.einsum(
        "tq,dq->td", query_pre_grad, query_weight, preferred_element_type=jnp.float32
    )
    query_weight_grad = jnp.einsum(
        "td,tq->dq", normed_attn_low, query_pre_grad, preferred_element_type=jnp.float32
    )
    expand_grad = (
        jnp.concatenate([key_grad[..., :QK_NOPE], value_grad], axis=-1)
        .astype(jnp.bfloat16)
        .reshape(tok_count, heads_here * (QK_NOPE + V_HEAD))
    )
    latent_part_grad = jnp.einsum(
        "te,re->tr", expand_grad, expand_weight, preferred_element_type=jnp.float32
    )
    expand_weight_grad = jnp.einsum(
        "tr,te->re", latent_low, expand_grad, preferred_element_type=jnp.float32
    )
    rope_part_grad = jnp.sum(key_grad[..., QK_NOPE:], axis=1)
    attn_in_sum, latent_sum, rope_sum = lax.psum(
        (attn_in_part, latent_part_grad, rope_part_grad), "tensor"
    )
    latent_pre_grad, gain_latent_grad = norm_backward(
        latent_part, inverse_latent, gain_latent_f, latent_sum
    )
    latent_all_grad = jnp.concatenate(
        [latent_pre_grad, rotate(rope_sum, cosine, -sine_part)], axis=-1
    ).astype(jnp.bfloat16)
    attn_in = attn_in_sum + jnp.einsum(
        "tc,dc->td", latent_all_grad, latent_weight, preferred_element_type=jnp.float32
    )
    latent_weight_grad = jnp.einsum(
        "td,tc->dc", normed_attn_low, latent_all_grad, preferred_element_type=jnp.float32
    )
    input_grad, gain_attn_grad = norm_backward(resid_in, inverse_attn, gain_attn_f, attn_in)
    tokens_grad = (mid_grad + input_grad).astype(jnp.bfloat16)
    (
        gain_attn_share,
        query_share,
        latent_share,
        gain_latent_share,
        expand_share,
        output_share,
        gain_ffn_share,
        router_share,
        shared_gate_share,
        shared_up_share,
        shared_down_share,
    ) = (
        lax.psum_scatter(
            gain_attn_grad.astype(jnp.bfloat16), "dp", scatter_dimension=0, tiled=True
        ).astype(jnp.float32),
        lax.psum_scatter(
            query_weight_grad.astype(jnp.bfloat16), "dp", scatter_dimension=0, tiled=True
        ).astype(jnp.float32),
        lax.psum_scatter(
            latent_weight_grad.astype(jnp.bfloat16), "dp", scatter_dimension=0, tiled=True
        ).astype(jnp.float32),
        lax.psum_scatter(
            gain_latent_grad.astype(jnp.bfloat16), "dp", scatter_dimension=0, tiled=True
        ).astype(jnp.float32),
        lax.psum_scatter(
            expand_weight_grad.astype(jnp.bfloat16), "dp", scatter_dimension=0, tiled=True
        ).astype(jnp.float32),
        lax.psum_scatter(
            output_weight_grad.astype(jnp.bfloat16), "dp", scatter_dimension=1, tiled=True
        ).astype(jnp.float32),
        lax.psum_scatter(
            gain_ffn_grad.astype(jnp.bfloat16), "dp", scatter_dimension=0, tiled=True
        ).astype(jnp.float32),
        lax.psum_scatter(
            router_grad.astype(jnp.bfloat16), "dp", scatter_dimension=0, tiled=True
        ).astype(jnp.float32),
        lax.psum_scatter(
            shared_gate_weight_grad.astype(jnp.bfloat16), "dp", scatter_dimension=0, tiled=True
        ).astype(jnp.float32),
        lax.psum_scatter(
            shared_up_weight_grad.astype(jnp.bfloat16), "dp", scatter_dimension=0, tiled=True
        ).astype(jnp.float32),
        lax.psum_scatter(
            shared_down_grad.astype(jnp.bfloat16), "dp", scatter_dimension=1, tiled=True
        ).astype(jnp.float32),
    )
    return (
        result,
        tokens_grad,
        gain_attn_share,
        query_share,
        latent_share,
        gain_latent_share,
        expand_share,
        output_share,
        gain_ffn_share,
        router_share,
        shared_gate_share,
        shared_up_share,
        shared_down_share,
        w_gate_grad,
        w_up_grad,
        w_down_grad,
    )

def hop(values, axis, bit):
    return lax.ppermute(values, axis, [(i, i ^ bit) for i in range(lax.axis_size(axis))])


def core_hop(values):
    return hop(values, "tensor", 1)


def y_hop(values):
    return hop(values, "tensor", 2)


def x_hop(values):
    return hop(values, "dp", 1)


def z_hop(values):
    count = lax.axis_size("dp")
    return lax.ppermute(values, "dp", [(i, (i + 2) % count) for i in range(count)])


def low(values):
    return values.astype(jnp.bfloat16)


class Flow:
    def __init__(self):
        self.tasks = []

    def launch(self, steps):
        task = Task(steps)
        self.tasks.append(task)
        return task

    def close(self, values):
        live = [task for task in self.tasks if not task.done]
        values, arrived = lax.optimization_barrier((values, [task.sent for task in live]))
        for task, got in zip(live, arrived):
            task.advance(got)
        return values


class Task:
    def __init__(self, steps):
        self.steps, self.done, self.result = steps, False, None
        self.advance(None)

    def advance(self, got):
        try:
            self.sent = self.steps.send(got)
        except StopIteration as stop:
            self.done, self.result = True, stop.value


def held(values, count):
    for _ in range(count):
        (values,) = yield [values]
    return values


def passing(values):
    (got,) = yield [z_hop(values)]
    return got


def plane_gather_split(own):
    half = own.shape[0] // 2
    first, second = own[:half], own[half:]
    first_x, second_y = yield [x_hop(first), y_hop(second)]
    first_pair = jnp.concatenate([first, first_x])
    second_pair = jnp.concatenate([second, second_y])
    first_y, second_x = yield [y_hop(first_pair), x_hop(second_pair)]
    quarter = jnp.concatenate(
        [
            own,
            first_x,
            second_x[:half],
            first_y[:half],
            second_y,
            first_y[half:],
            second_x[half:],
        ]
    )
    (far,) = yield [core_hop(quarter)]
    return jnp.concatenate([quarter, far])


def plane_gather(own, before=0):
    (far,) = yield [x_hop(own)]
    far = yield from held(far, before)
    pair = jnp.concatenate([own, far])
    (far,) = yield [y_hop(pair)]
    quarter = jnp.concatenate([pair, far])
    (far,) = yield [core_hop(quarter)]
    return jnp.concatenate([quarter, far])


def plane_scatter(part, x_first, before=0, between=0):
    part = part.reshape(2, 2, 2, part.shape[0] // 8, part.shape[1])
    (far,) = yield [core_hop(part[1])]
    far = yield from held(far, before)
    total = part[0].astype(jnp.float32) + far.astype(jnp.float32)
    near, away = (total[:, 0], total[:, 1]) if x_first else (total[0], total[1])
    (far,) = yield [x_hop(low(away)) if x_first else y_hop(low(away))]
    far = yield from held(far, between)
    near = near + far.astype(jnp.float32)
    (far,) = yield [y_hop(low(near[1])) if x_first else x_hop(low(near[1]))]
    return near[0] + far.astype(jnp.float32)


def tensor_scatter(values, tensor_index):
    rows = values.shape[0] // 4
    width = values.shape[1]
    core = tensor_index % 2
    level = tensor_index // 2
    blocks = values.reshape(2, 2, rows, width)
    mine = lax.dynamic_index_in_dim(blocks, core, 1, keepdims=False)
    other = lax.dynamic_index_in_dim(blocks, 1 - core, 1, keepdims=False)
    total = mine.astype(jnp.float32) + core_hop(low(other)).astype(jnp.float32)
    near = lax.dynamic_index_in_dim(total, level, 0, keepdims=False)
    far = lax.dynamic_index_in_dim(total, 1 - level, 0, keepdims=False)
    return near + y_hop(low(far)).astype(jnp.float32)


def tensor_gather(own, tensor_index):
    own_y = y_hop(own)
    pair = jnp.stack([own, own_y])
    pair_core = core_hop(pair)
    core = tensor_index % 2
    level = tensor_index // 2
    even = jnp.where(core == 0, pair, pair_core)
    odd = jnp.where(core == 0, pair_core, pair)
    near = jnp.concatenate([even[0], odd[0]])
    far = jnp.concatenate([even[1], odd[1]])
    return jnp.concatenate(
        [jnp.where(level == 0, near, far), jnp.where(level == 0, far, near)]
    )


def laid_out(arrived, axes, dp_index):
    planes = len(arrived[0]) // 2
    plane = dp_index // 2
    side = dp_index % 2
    wholes = []
    for pieces, axis in zip(arrived, axes):
        extent = pieces[0].shape[axis]
        shape = list(pieces[0].shape)
        shape[axis] *= 2 * planes
        whole = jnp.zeros(shape, pieces[0].dtype)
        for k, piece in enumerate(pieces):
            home = (plane - k // 2) % planes * 2 + (side if k % 2 == 0 else 1 - side)
            whole = lax.dynamic_update_slice_in_dim(whole, piece, home * extent, axis)
        wholes.append(whole)
    return wholes


def dp_ring(pieces, axes, dp_index):
    planes = lax.axis_size("dp") // 2
    arrived = [[] for _ in axes]
    for step in range(planes):
        sent = [x_hop(piece) for piece in pieces]
        if step + 1 < planes:
            sent += [z_hop(piece) for piece in pieces]
        got = yield sent
        for i in range(len(axes)):
            arrived[i] += [pieces[i], got[i]]
        pieces = got[len(axes) :]
    return laid_out(arrived, axes, dp_index)


def side_ring(own, dp_index, tensor_index):
    steps = dp_ring([own], [1], dp_index)
    sent = next(steps)
    while True:
        try:
            sent = steps.send(sent)
        except StopIteration as stop:
            (whole,) = stop.value
            break
    (whole,) = yield [whole]
    (far,) = yield [y_hop(whole)]
    pair = jnp.stack([whole, far])
    (far,) = yield [core_hop(pair)]
    core = tensor_index % 2
    level = tensor_index // 2
    even = jnp.where(core == 0, pair, far)
    odd = jnp.where(core == 0, far, pair)
    near = jnp.stack([even, odd], axis=1)
    whole = jnp.where(level == 0, near, near[::-1])
    return whole.reshape((4 * own.shape[0],) + whole.shape[3:])


def dp_scatter_steps(block, dp_index):
    planes = lax.axis_size("dp") // 2
    plane = dp_index // 2
    side = dp_index % 2
    bases = [(plane - step) % planes * 2 for step in list(range(1, planes)) + [0]]
    half = len(bases) // 2
    away = [low(block(base + 1 - side)) for base in bases]
    first, second = yield [x_hop(jnp.stack(away[:half])), x_hop(jnp.stack(away[half:]))]
    received = [first[i] for i in range(half)] + [second[i] for i in range(len(bases) - half)]
    moving = None
    for base, far in zip(bases, received):
        piece = block(base + side) + far.astype(jnp.float32)
        if moving is not None:
            (got,) = yield [z_hop(low(moving))]
            piece = piece + got.astype(jnp.float32)
        moving = piece
    return moving


def drained(task):
    while not task.done:
        task.advance(task.sent)
    return task.result


def dp_scatter(block, dp_index):
    return drained(Task(dp_scatter_steps(block, dp_index)))


def padded(values, axis, size):
    pads = [(0, 0)] * values.ndim
    pads[axis] = (0, size - values.shape[axis])
    return jnp.pad(values, pads)


def lanes(size):
    return -(-size // 128) * 128


def body_dense(
    tokens,
    cotangent,
    routes,
    seq_ids,
    positions,
    gain_attn,
    w_query,
    w_latent,
    gain_latent,
    w_expand,
    w_output,
    gain_ffn,
    w_router,
    w_shared_gate,
    w_shared_up,
    w_shared_down,
    w_gate,
    w_up,
    w_down,
):
    tensor_size = lax.axis_size("tensor")
    dp_size = lax.axis_size("dp")
    dp_index = lax.axis_index("dp")
    tensor_index = lax.axis_index("tensor")
    tok_count, width = tokens.shape
    own_count = tok_count // tensor_size
    own_start = tensor_index * own_count
    experts = w_router.shape[1]
    exp_here = w_gate.shape[0]
    capacity = tensor_size * -(-(5 * tok_count * TOP) // (4 * experts * tensor_size))

    def own_rows(values):
        return lax.dynamic_slice_in_dim(values, own_start, own_count, 0)

    lat_width = w_latent.shape[1]
    lat_block = w_latent.shape[0]
    routed = jnp.sum(
        (routes[:, :, None] == jnp.arange(experts, dtype=jnp.int32)[None, None, :]).astype(
            jnp.float32
        ),
        axis=1,
    )
    order = jnp.arange(tok_count, dtype=jnp.int32)
    earlier = (order[None, :] < order[:, None]).astype(jnp.bfloat16)
    rank = jnp.dot(earlier, low(routed), preferred_element_type=jnp.float32)
    standing = routed * (1.0 + (rank < capacity).astype(jnp.float32))
    standing_own = own_rows(standing)
    cot_own = own_rows(cotangent)

    folds = tok_count // lat_block
    mark_start = lat_width + experts
    gain_start = mark_start + folds * experts
    side_rows = lanes(gain_start + 3)
    side = jnp.concatenate(
        [w_latent.T, w_router.T]
        + [
            low(standing[fold * lat_block : (fold + 1) * lat_block]).T
            for fold in range(folds)
        ]
        + [jnp.stack([gain_attn, gain_ffn, padded(gain_latent, 0, lat_block)])]
    )
    side_rows_here = side_rows // tensor_size
    side = lax.dynamic_slice_in_dim(
        padded(side, 0, side_rows), tensor_index * side_rows_here, side_rows_here, 0
    )

    flow = Flow()
    side_task = flow.launch(side_ring(side, dp_index, tensor_index))
    weights = flow.close((w_query, w_expand, w_output))
    weight_task = flow.launch(dp_ring(weights, [0, 0, 1], dp_index))
    for _ in range(2):
        flow.close(())

    core = tensor_index % 2
    level = tensor_index // 2
    planes = dp_size // 2
    side_all = side_task.result
    latent_weight = side_all[:lat_width]
    router_weight = side_all[lat_width:mark_start]
    marks_all = side_all[mark_start:gain_start].reshape(folds, experts, dp_size, lat_block)
    marks_all = marks_all.transpose(2, 0, 3, 1).reshape(planes, 8, own_count, experts)
    gains_all = side_all[gain_start : gain_start + 3].astype(jnp.float32)
    gain_attn_f = gains_all[0]
    gain_ffn_f = gains_all[1]
    gain_latent_f = gains_all[2].reshape(dp_size, lat_block)[:, : gain_latent.shape[0]].reshape(
        KV_RANK
    )
    near = jnp.arange(8, dtype=jnp.int32)
    near_x = near % 2 ^ dp_index % 2
    near_y = near // 2 % 2 ^ level
    near_core = near // 4 ^ core
    near_block = near_x * 4 + near_y * 2 + near_core
    mark_chunks = [
        jnp.take(
            lax.dynamic_index_in_dim(
                marks_all, (dp_index // 2 - step) % planes, 0, keepdims=False
            ),
            near_block,
            axis=0,
        ).reshape(8 * own_count, experts)
        for step in range(planes)
    ]
    flow.close(())
    cot_pass = flow.launch(passing(cot_own))

    head_width = QK_NOPE + QK_ROPE
    heads_here = w_query.shape[1] // head_width
    softmax_scale = head_width ** (-0.5)
    resid_in = tokens.astype(jnp.float32)
    normed_attn, inverse_attn = norm_forward(resid_in, gain_attn_f)
    normed_attn_low = low(normed_attn)
    cosine, sine_part = rope_tables(positions, QK_ROPE)
    latent_raw = jnp.einsum(
        "td,cd->tc", normed_attn_low, latent_weight, preferred_element_type=jnp.float32
    )
    latent_part = latent_raw[:, :KV_RANK]
    latent_normed, inverse_latent = norm_forward(latent_part, gain_latent_f)
    latent_low = low(latent_normed)
    key_rope_low = low(rotate(latent_raw[:, KV_RANK:], cosine, sine_part))
    normed_attn_low, latent_low, key_rope_low, w_shared_gate, w_shared_up, w_shared_down = (
        flow.close(
            (normed_attn_low, latent_low, key_rope_low, w_shared_gate, w_shared_up, w_shared_down)
        )
    )

    query_weight, expand_weight, output_weight = weight_task.result
    cot_tasks = [flow.launch(plane_gather(cot_own))]
    cot_piece = cot_pass.result
    cot_pass = flow.launch(passing(cot_piece))
    query_raw = jnp.dot(normed_attn_low, query_weight, preferred_element_type=jnp.float32).reshape(
        tok_count, heads_here, head_width
    )
    query_low = low(
        jnp.concatenate(
            [
                query_raw[..., :QK_NOPE],
                rotate(query_raw[..., QK_NOPE:], cosine[:, None, :], sine_part[:, None, :]),
            ],
            axis=-1,
        )
    )
    expanded = low(jnp.dot(latent_low, expand_weight, preferred_element_type=jnp.float32))
    query_low, expanded = flow.close((query_low, expanded))

    cot_tasks.append(flow.launch(plane_gather(cot_piece, 4)))
    cot_piece = cot_pass.result
    cot_pass = flow.launch(passing(cot_piece))
    expanded = expanded.reshape(tok_count, heads_here, QK_NOPE + V_HEAD)
    value_low = expanded[..., QK_NOPE:]
    key_full = jnp.concatenate(
        [
            expanded[..., :QK_NOPE],
            jnp.broadcast_to(key_rope_low[:, None, :], (tok_count, heads_here, QK_ROPE)),
        ],
        axis=-1,
    )
    masked = block_scores(query_low, key_full, seq_ids, 0)
    row_max = jnp.max(masked, axis=-1, keepdims=True)
    exponent = jnp.exp(masked - row_max)
    exp_total = jnp.sum(exponent, axis=-1, keepdims=True)
    probs_low = low(exponent / exp_total)
    log_total = row_max + jnp.log(exp_total)
    heads_low = low(
        jnp.einsum("hqk,khc->qhc", probs_low, value_low, preferred_element_type=jnp.float32)
    ).reshape(tok_count, heads_here * V_HEAD)
    attn_part = jnp.dot(heads_low, output_weight, preferred_element_type=jnp.float32)
    attn_part = flow.close(attn_part)

    cot_tasks.append(flow.launch(plane_gather(cot_piece, 6)))
    cot_piece = cot_pass.result
    resid_own = own_rows(tokens).astype(jnp.float32) + tensor_scatter(attn_part, tensor_index)
    normed_own, inverse_own = norm_forward(resid_own, gain_ffn_f)
    normed_own_low = flow.close(low(normed_own))

    row_tasks = [flow.launch(plane_gather_split(normed_own_low))]
    row_pass = flow.launch(passing(normed_own_low))
    shared_here = w_shared_gate.shape[1] // dp_size
    shared = lax.all_to_all(
        jnp.stack([w_shared_gate.T, w_shared_up.T, w_shared_down]),
        "dp",
        split_axis=1,
        concat_axis=2,
        tiled=True,
    )
    group = w_gate.shape[2]
    routed_here = exp_here * group
    hidden = routed_here + shared_here
    gate_weight = jnp.concatenate([w_gate.swapaxes(1, 2).reshape(routed_here, width), shared[0]])
    up_weight = jnp.concatenate([w_up.swapaxes(1, 2).reshape(routed_here, width), shared[1]])
    down_weight = jnp.concatenate([w_down.reshape(routed_here, width), shared[2]])
    gate_weight, up_weight, down_weight = flow.close((gate_weight, up_weight, down_weight))
    for _ in range(2):
        flow.close(())

    def gating(rows, standing_rows):
        probs = jax.nn.softmax(
            jnp.einsum("td,ed->te", rows, router_weight, preferred_element_type=jnp.float32),
            axis=-1,
        )
        gates = jnp.where(standing_rows > 0.5, probs, 0.0)
        picked = jnp.sum(gates, axis=-1, keepdims=True)
        return probs, gates / picked, picked

    expert_index = jnp.arange(experts, dtype=jnp.int32)[None, :]
    column = jnp.arange(hidden, dtype=jnp.int32)[None, :]
    row_piece = row_pass.result
    in_tasks, out_tasks, gate_parts, kept_parts = [], [], [], []
    in_part = None
    for step in range(planes):
        rows = row_tasks[step].result
        if step + 1 < planes:
            row_tasks.append(flow.launch(plane_gather(row_piece)))
            if step + 2 < planes:
                row_pass = flow.launch(passing(row_piece))
        if step > 0:
            in_tasks.append(flow.launch(plane_scatter(in_part, True)))
        if step == planes - 1:
            in_moving = flow.launch(passing(low(in_tasks[1].result)))
        gate_pre = jnp.einsum("td,fd->tf", rows, gate_weight, preferred_element_type=jnp.float32)
        up_pre = jnp.einsum("td,fd->tf", rows, up_weight, preferred_element_type=jnp.float32)
        gate_pre, up_pre, rows = flow.close((gate_pre, up_pre, rows))
        if step + 2 < planes:
            row_piece = row_pass.result

        cots = cot_tasks[step].result
        marks = mark_chunks[step].astype(jnp.float32)
        _, chunk_gates, _ = gating(rows, marks)
        chunk_gates = jnp.where(marks > 1.5, chunk_gates, 0.0)
        scale = jnp.ones((rows.shape[0], hidden), jnp.float32)
        for e in reversed(range(exp_here)):
            here = expert_index == dp_index * exp_here + e
            gate_column = jnp.sum(jnp.where(here, chunk_gates, 0.0), axis=-1, keepdims=True)
            scale = jnp.where(column < (e + 1) * group, gate_column, scale)
        sigmoid = jax.nn.sigmoid(gate_pre)
        silu = gate_pre * sigmoid
        act = silu * up_pre
        act_scaled = low(act * scale)
        out_part = low(jnp.dot(act_scaled, down_weight, preferred_element_type=jnp.float32))
        act_grad = jnp.einsum("td,fd->tf", cots, down_weight, preferred_element_type=jnp.float32)
        meeting = act * act_grad
        gate_parts.append(
            jnp.stack(
                [
                    jnp.sum(jnp.where(column // group == e, meeting, 0.0), axis=-1)
                    for e in range(exp_here)
                ]
            )
        )
        scaled_grad = act_grad * scale
        gate_grad = low(scaled_grad * up_pre * sigmoid * (1.0 + gate_pre * (1.0 - sigmoid)))
        up_grad = low(scaled_grad * silu)
        gate_grad, up_grad, act_scaled, out_part, rows, cots = flow.close(
            (gate_grad, up_grad, act_scaled, out_part, rows, cots)
        )

        after = (planes - 1 - step) * 3
        places = {0: (after + 6, 0), 1: (after, 1), 2: (after + 3, 0), 3: (after + 5, 0)}[step]
        out_tasks.append(flow.launch(plane_scatter(out_part, False, *places)))
        if step == 0:
            cot_tasks.append(flow.launch(plane_gather(cot_piece, 3)))
        in_part = low(
            jnp.dot(gate_grad, gate_weight, preferred_element_type=jnp.float32)
            + jnp.dot(up_grad, up_weight, preferred_element_type=jnp.float32)
        )
        in_part, gate_grad, up_grad, act_scaled, rows, cots = flow.close(
            (in_part, gate_grad, up_grad, act_scaled, rows, cots)
        )
        kept_parts.append((rows, cots, gate_grad, up_grad, act_scaled))

    in_tasks.append(flow.launch(plane_scatter(in_part, True)))
    in_moving = flow.launch(
        passing(low(in_tasks[2].result + in_moving.result.astype(jnp.float32)))
    )
    gate_sums = jnp.stack(gate_parts).reshape(-1, exp_here, 2, 2, 2, own_count)
    gate_sums = gate_sums[:, :, 0] + core_hop(gate_sums[:, :, 1])
    gate_sums = gate_sums[:, :, 0] + y_hop(gate_sums[:, :, 1])
    block = jnp.arange(dp_size, dtype=jnp.int32)
    place = ((dp_index // 2 - block // 2) % planes) * 2 + (block + dp_index) % 2
    gate_sums = gate_sums.transpose(0, 2, 1, 3).reshape(dp_size, exp_here, own_count)[place]
    gate_weight_grad = sum(
        jnp.einsum("tf,td->fd", gate_grad, rows, preferred_element_type=jnp.float32)
        for rows, _, gate_grad, _, _ in kept_parts
    )
    gate_weight_grad, kept_parts, gate_sums = flow.close(
        (gate_weight_grad, kept_parts, gate_sums)
    )
    gate_sums = lax.all_to_all(gate_sums, "dp", split_axis=0, concat_axis=0, tiled=True)
    gate_sums = gate_sums.reshape(experts, own_count).T
    up_weight_grad = sum(
        jnp.einsum("tf,td->fd", up_grad, rows, preferred_element_type=jnp.float32)
        for rows, _, _, up_grad, _ in kept_parts
    )
    gate_sums, up_weight_grad, kept_parts = flow.close((gate_sums, up_weight_grad, kept_parts))
    flow.close(())
    in_moving = flow.launch(
        passing(low(in_tasks[3].result + in_moving.result.astype(jnp.float32)))
    )
    out_moving = flow.launch(passing(low(out_tasks[1].result)))

    kept_parts = flow.close(kept_parts)
    ffn_sum = in_tasks[0].result + in_moving.result.astype(jnp.float32)
    probs_own, gates_own, picked_own = gating(normed_own_low, standing_own)
    gate_sums = jnp.where(standing_own > 1.5, gate_sums, 0.0)
    picked_grad = (
        gate_sums - jnp.sum(gate_sums * gates_own, axis=-1, keepdims=True)
    ) / picked_own
    probs_grad = jnp.where(standing_own > 0.5, picked_grad, 0.0)
    logit_grad = low(
        probs_own * (probs_grad - jnp.sum(probs_own * probs_grad, axis=-1, keepdims=True))
    )
    router_grad = jnp.einsum(
        "te,td->ed", logit_grad, normed_own_low, preferred_element_type=jnp.float32
    )
    ffn_in = ffn_sum + jnp.dot(logit_grad, router_weight, preferred_element_type=jnp.float32)
    ffn_resid_grad, gain_ffn_grad = norm_backward(resid_own, inverse_own, gain_ffn_f, ffn_in)
    mid_grad_own = cot_own.astype(jnp.float32) + ffn_resid_grad
    shared_parts = [gate_weight_grad, up_weight_grad]
    mid_low, kept_parts, shared_parts = flow.close(
        (tensor_gather(low(mid_grad_own), tensor_index), kept_parts, shared_parts)
    )
    out_moving = flow.launch(
        passing(low(out_tasks[2].result + out_moving.result.astype(jnp.float32)))
    )
    down_weight_grad = sum(
        jnp.einsum("tf,td->fd", act_scaled, cots, preferred_element_type=jnp.float32)
        for _, cots, _, _, act_scaled in kept_parts[: planes // 2]
    )

    def shared_sum(grads):
        grads = jnp.stack([low(grad[routed_here:]) for grad in grads])
        return lax.all_to_all(grads, "dp", split_axis=2, concat_axis=1, tiled=True).astype(
            jnp.float32
        )

    shared_grads = shared_sum(shared_parts)
    output_weight_grad = jnp.einsum(
        "th,td->hd", heads_low, mid_low, preferred_element_type=jnp.float32
    )
    heads_grad = low(
        jnp.einsum("td,hd->th", mid_low, output_weight, preferred_element_type=jnp.float32)
    ).reshape(tok_count, heads_here, V_HEAD)
    heads_grad, output_weight_grad, down_weight_grad, kept_parts = flow.close(
        (heads_grad, output_weight_grad, down_weight_grad, kept_parts)
    )
    down_weight_grad += sum(
        jnp.einsum("tf,td->fd", act_scaled, cots, preferred_element_type=jnp.float32)
        for _, cots, _, _, act_scaled in kept_parts[planes // 2 :]
    )
    output_task = flow.launch(
        dp_scatter_steps(
            lambda i: lax.dynamic_slice_in_dim(
                output_weight_grad, i * w_output.shape[1], w_output.shape[1], 1
            ),
            dp_index,
        )
    )
    masked = block_scores(query_low, key_full, seq_ids, 0)
    attn_probs = jnp.exp(masked - log_total)
    prob_grad = jnp.einsum("qhc,khc->hqk", heads_grad, value_low, preferred_element_type=jnp.float32)
    row_dot = jnp.sum(attn_probs * prob_grad, axis=-1, keepdims=True)
    score_grad = low(attn_probs * (prob_grad - row_dot))
    score_grad, probs_low, down_weight_grad = flow.close(
        (score_grad, low(attn_probs), down_weight_grad)
    )
    out_moving = flow.launch(
        passing(low(out_tasks[3].result + out_moving.result.astype(jnp.float32)))
    )
    query_grad = (
        jnp.einsum("hqk,khc->qhc", score_grad, key_full, preferred_element_type=jnp.float32)
        * softmax_scale
    )
    key_grad = (
        jnp.einsum("hqk,qhc->khc", score_grad, query_low, preferred_element_type=jnp.float32)
        * softmax_scale
    )
    value_grad = jnp.einsum(
        "hqk,qhc->khc", probs_low, heads_grad, preferred_element_type=jnp.float32
    )
    query_grad, key_grad, value_grad = flow.close((query_grad, key_grad, value_grad))
    query_pre_grad = low(
        jnp.concatenate(
            [
                query_grad[..., :QK_NOPE],
                rotate(query_grad[..., QK_NOPE:], cosine[:, None, :], -sine_part[:, None, :]),
            ],
            axis=-1,
        )
    ).reshape(tok_count, heads_here * head_width)
    query_weight_grad = jnp.einsum(
        "td,tq->dq", normed_attn_low, query_pre_grad, preferred_element_type=jnp.float32
    )
    expand_grad = low(jnp.concatenate([key_grad[..., :QK_NOPE], value_grad], axis=-1)).reshape(
        tok_count, heads_here * (QK_NOPE + V_HEAD)
    )
    latent_grad = jnp.einsum(
        "te,re->tr", expand_grad, expand_weight, preferred_element_type=jnp.float32
    )
    expand_weight_grad = jnp.einsum(
        "tr,te->re", latent_low, expand_grad, preferred_element_type=jnp.float32
    )
    latent_grad, query_weight_grad, expand_weight_grad = flow.close(
        (latent_grad, query_weight_grad, expand_weight_grad)
    )
    rope_grad = jnp.sum(key_grad[..., QK_NOPE:], axis=1)
    latent_pre_grad, gain_latent_grad = norm_backward(
        latent_part, inverse_latent, gain_latent_f, latent_grad
    )
    latent_all_grad = low(
        jnp.concatenate([latent_pre_grad, rotate(rope_grad, cosine, -sine_part)], axis=-1)
    )
    attn_in = jnp.einsum(
        "tq,dq->td", query_pre_grad, query_weight, preferred_element_type=jnp.float32
    ) + jnp.dot(latent_all_grad, latent_weight, preferred_element_type=jnp.float32)
    latent_weight_grad = jnp.einsum(
        "tc,td->cd", latent_all_grad, normed_attn_low, preferred_element_type=jnp.float32
    )
    gain_attn_grad = jnp.sum(attn_in * (resid_in * inverse_attn), axis=0)
    attn_in_own = tensor_scatter(attn_in, tensor_index)
    input_grad, _ = norm_backward(
        own_rows(resid_in), own_rows(inverse_attn), gain_attn_f, attn_in_own
    )
    tokens_grad = tensor_gather(low(mid_grad_own + input_grad), tensor_index)

    out_sum = out_tasks[0].result + out_moving.result.astype(jnp.float32)
    result = tensor_gather(low(resid_own + out_sum), tensor_index)

    output_share = drained(output_task)
    query_share = dp_scatter(
        lambda i: lax.dynamic_slice_in_dim(query_weight_grad, i * lat_block, lat_block, 0),
        dp_index,
    )
    expand_block = w_expand.shape[0]
    expand_share = dp_scatter(
        lambda i: lax.dynamic_slice_in_dim(expand_weight_grad, i * expand_block, expand_block, 0),
        dp_index,
    )

    gain_latent_rows = padded(gain_latent_grad.reshape(dp_size, -1), 1, lat_block).reshape(width)
    gain_grads = jnp.stack([gain_attn_grad, gain_ffn_grad, gain_latent_rows])
    side_grad = jnp.concatenate(
        [
            low(latent_weight_grad),
            low(router_grad),
            padded(low(gain_grads), 0, side_rows - mark_start),
        ]
    ).reshape(2, 2, side_rows_here, width)
    kept_side = lax.dynamic_index_in_dim(side_grad, core, 1, keepdims=False)
    sent_side = lax.dynamic_index_in_dim(side_grad, 1 - core, 1, keepdims=False)
    side_grad = kept_side.astype(jnp.float32) + core_hop(sent_side).astype(jnp.float32)
    kept_side = lax.dynamic_index_in_dim(side_grad, level, 0, keepdims=False)
    sent_side = lax.dynamic_index_in_dim(side_grad, 1 - level, 0, keepdims=False)
    side_grad = kept_side + y_hop(low(sent_side)).astype(jnp.float32)
    side_piece = dp_scatter(
        lambda i: lax.dynamic_slice_in_dim(side_grad, i * lat_block, lat_block, 1), dp_index
    )
    grad_full = tensor_gather(low(side_piece), tensor_index).astype(jnp.float32)
    latent_share = grad_full[:lat_width].T
    router_share = grad_full[lat_width:mark_start].T
    gain_attn_share = grad_full[mark_start]
    gain_ffn_share = grad_full[mark_start + 1]
    gain_latent_share = grad_full[mark_start + 2, : gain_latent.shape[0]]

    def routed_grad(grad):
        return grad[:routed_here].reshape(exp_here, group, width)

    routed_grads = (
        routed_grad(gate_weight_grad).swapaxes(1, 2),
        routed_grad(up_weight_grad).swapaxes(1, 2),
        routed_grad(down_weight_grad),
    )
    shared_down_grad = lax.all_to_all(
        low(down_weight_grad[routed_here:]), "dp", split_axis=1, concat_axis=0, tiled=True
    ).astype(jnp.float32)

    return (
        result,
        tokens_grad,
        gain_attn_share,
        query_share,
        latent_share,
        gain_latent_share,
        expand_share,
        output_share,
        gain_ffn_share,
        router_share,
        shared_grads[0].T,
        shared_grads[1].T,
        shared_down_grad,
        *routed_grads,
    )


def solution(mesh):
    dense = mesh.shape["dp"] == 8 and mesh.shape["tensor"] == 4
    return jax.shard_map(
        body_dense if dense else body,
        mesh=mesh,
        in_specs=(
            P("dp", None),
            P("dp", None),
            P("dp", None),
            P("dp"),
            P("dp"),
            P("dp"),
            P("dp", "tensor"),
            P("dp", None),
            P("dp"),
            P("dp", "tensor"),
            P("tensor", "dp"),
            P("dp"),
            P("dp", None),
            P("dp", "tensor"),
            P("dp", "tensor"),
            P("tensor", "dp"),
            P("dp", None, "tensor"),
            P("dp", None, "tensor"),
            P("dp", "tensor", None),
        ),
        out_specs=(
            P("dp", None),
            P("dp", None),
            P("dp"),
            P("dp", "tensor"),
            P("dp", None),
            P("dp"),
            P("dp", "tensor"),
            P("tensor", "dp"),
            P("dp"),
            P("dp", None),
            P("dp", "tensor"),
            P("dp", "tensor"),
            P("tensor", "dp"),
            P("dp", None, "tensor"),
            P("dp", None, "tensor"),
            P("dp", "tensor", None),
        ),
        check_vma=False,
    )
```

```python
import jax
import jax.numpy as jnp
from jax import lax
from jax.sharding import PartitionSpec as P

QK_NOPE = 128
QK_ROPE = 64
V_HEAD = 128
KV_RANK = 512
TOP = 6


EPSILON = 1e-06
MASKED = -1e30


def norm_forward(values, gain_full):
    inverse = lax.rsqrt(jnp.mean(values * values, axis=-1, keepdims=True) + EPSILON)
    return (values * inverse * gain_full, inverse)


def norm_backward(values, inverse, gain_full, grad_out):
    normed = values * inverse
    scaled = grad_out * gain_full
    grad_in = inverse * (scaled - normed * jnp.mean(scaled * normed, axis=-1, keepdims=True))
    return (grad_in, jnp.sum(grad_out * normed, axis=0))


def rope_tables(positions, width):
    half_width = width // 2
    frequency = jnp.power(10000.0, -jnp.arange(half_width, dtype=jnp.float32) / half_width)
    angles = positions.astype(jnp.float32)[:, None] * frequency[None, :]
    return (jnp.cos(angles), jnp.sin(angles))


def rotate(values, cosine, sine_part):
    half_width = values.shape[-1] // 2
    front_half = values[..., :half_width]
    back_half = values[..., half_width:]
    return jnp.concatenate(
        [front_half * cosine - back_half * sine_part, back_half * cosine + front_half * sine_part],
        axis=-1,
    )


def slot_layout(routes, experts, capacity):
    flat_routes = routes.reshape(-1)
    onehot = (flat_routes[:, None] == jnp.arange(experts, dtype=jnp.int32)[None, :]).astype(
        jnp.int32
    )
    before = jnp.cumsum(onehot, axis=0) - onehot
    slot_rank = jnp.sum(before * onehot, axis=1)
    route_kept = slot_rank < capacity
    slot_index = flat_routes * capacity + jnp.minimum(slot_rank, capacity - 1)
    return (slot_index.reshape(routes.shape), route_kept.reshape(routes.shape))


def slot_owner(slot_index, route_kept, kept_gates, slot_total):
    pair_count = slot_index.size
    target = jnp.where(route_kept.reshape(-1), slot_index.reshape(-1), slot_total)
    token_rows = jnp.arange(pair_count, dtype=jnp.int32) // slot_index.shape[-1]
    slot_token = jnp.zeros((slot_total,), jnp.int32).at[target].set(token_rows, mode="drop")
    slot_live = jnp.zeros((slot_total,), jnp.bool_).at[target].set(True, mode="drop")
    slot_gate = (
        jnp.zeros((slot_total,), jnp.float32).at[target].set(kept_gates.reshape(-1), mode="drop")
    )
    return (slot_token, slot_live, slot_gate)


def block_scores(query_block, key_block, seq_ids, row_start):
    row_count = query_block.shape[0]
    key_count = key_block.shape[0]
    raw_scores = jnp.einsum(
        "qhc,khc->hqk", query_block, key_block, preferred_element_type=jnp.float32
    ) * (QK_NOPE + QK_ROPE) ** (-0.5)
    query_index = row_start + jnp.arange(row_count, dtype=jnp.int32)
    key_index = jnp.arange(key_count, dtype=jnp.int32)
    allowed = (seq_ids[:, None] == seq_ids[None, :]) & (key_index[None, :] <= query_index[:, None])
    return jnp.where(allowed[None], raw_scores, MASKED)


def body(
    tokens,
    cotangent,
    routes,
    seq_ids,
    positions,
    gain_attn,
    w_query,
    w_latent,
    gain_latent,
    w_expand,
    w_output,
    gain_ffn,
    w_router,
    w_shared_gate,
    w_shared_up,
    w_shared_down,
    w_gate,
    w_up,
    w_down,
):
    (
        gain_attn_all,
        query_weight,
        latent_weight,
        gain_latent_all,
        expand_weight,
        output_weight,
        gain_ffn_all,
        router_weight,
        shared_gate_weight,
        shared_up_weight,
        shared_down_weight,
    ) = (
        lax.all_gather(gain_attn, "dp", axis=0, tiled=True),
        lax.all_gather(w_query, "dp", axis=0, tiled=True),
        lax.all_gather(w_latent, "dp", axis=0, tiled=True),
        lax.all_gather(gain_latent, "dp", axis=0, tiled=True),
        lax.all_gather(w_expand, "dp", axis=0, tiled=True),
        lax.all_gather(w_output, "dp", axis=1, tiled=True),
        lax.all_gather(gain_ffn, "dp", axis=0, tiled=True),
        lax.all_gather(w_router, "dp", axis=0, tiled=True),
        lax.all_gather(w_shared_gate, "dp", axis=0, tiled=True),
        lax.all_gather(w_shared_up, "dp", axis=0, tiled=True),
        lax.all_gather(w_shared_down, "dp", axis=1, tiled=True),
    )
    tok_count = tokens.shape[0]
    head_width = QK_NOPE + QK_ROPE
    heads_here = query_weight.shape[1] // head_width
    softmax_scale = head_width ** (-0.5)
    gain_attn_f = gain_attn_all.astype(jnp.float32)
    gain_latent_f = gain_latent_all.astype(jnp.float32)
    resid_in = tokens.astype(jnp.float32)
    normed_attn, inverse_attn = norm_forward(resid_in, gain_attn_f)
    normed_attn_low = normed_attn.astype(jnp.bfloat16)
    cosine, sine_part = rope_tables(positions, QK_ROPE)
    query_raw = jnp.dot(normed_attn_low, query_weight, preferred_element_type=jnp.float32).reshape(
        tok_count, heads_here, head_width
    )
    query_low = jnp.concatenate(
        [
            query_raw[..., :QK_NOPE],
            rotate(query_raw[..., QK_NOPE:], cosine[:, None, :], sine_part[:, None, :]),
        ],
        axis=-1,
    ).astype(jnp.bfloat16)
    latent_raw = jnp.dot(normed_attn_low, latent_weight, preferred_element_type=jnp.float32)
    latent_part = latent_raw[:, :KV_RANK]
    latent_normed, inverse_latent = norm_forward(latent_part, gain_latent_f)
    latent_low = latent_normed.astype(jnp.bfloat16)
    key_rope_low = rotate(latent_raw[:, KV_RANK:], cosine, sine_part).astype(jnp.bfloat16)
    expanded = (
        jnp.dot(latent_low, expand_weight, preferred_element_type=jnp.float32)
        .astype(jnp.bfloat16)
        .reshape(tok_count, heads_here, QK_NOPE + V_HEAD)
    )
    value_low = expanded[..., QK_NOPE:]
    key_full = jnp.concatenate(
        [
            expanded[..., :QK_NOPE],
            jnp.broadcast_to(key_rope_low[:, None, :], (tok_count, heads_here, QK_ROPE)),
        ],
        axis=-1,
    )
    row_start = 0
    row_stop = row_start + tok_count
    masked = block_scores(query_low, key_full, seq_ids, row_start)
    row_max = jnp.max(masked, axis=-1, keepdims=True)
    exponent = jnp.exp(masked - row_max)
    exp_total = jnp.sum(exponent, axis=-1, keepdims=True)
    attn_probs = (exponent / exp_total).astype(jnp.bfloat16)
    log_totals = [row_max + jnp.log(exp_total)]
    head_blocks = jnp.einsum(
        "hqk,khc->qhc", attn_probs, value_low, preferred_element_type=jnp.float32
    )
    heads_low = head_blocks.astype(jnp.bfloat16).reshape(tok_count, heads_here * V_HEAD)
    attn_part = jnp.dot(heads_low, output_weight, preferred_element_type=jnp.float32)
    resid_mid = resid_in + lax.psum(attn_part, "tensor")
    gain_ffn_f = gain_ffn_all.astype(jnp.float32)
    normed_ffn, inverse_ffn = norm_forward(resid_mid, gain_ffn_f)
    normed_ffn_low = normed_ffn.astype(jnp.bfloat16)
    experts = router_weight.shape[1]
    router_probs = jax.nn.softmax(
        jnp.dot(normed_ffn_low, router_weight, preferred_element_type=jnp.float32), axis=-1
    )
    route_hits = routes[:, :, None] == jnp.arange(experts, dtype=jnp.int32)[None, None, :]
    picked = jnp.sum(jnp.where(route_hits, router_probs[:, None, :], 0.0), axis=-1)
    picked_total = jnp.sum(picked, axis=-1, keepdims=True)
    gates = picked / picked_total
    tensor_size = lax.axis_size("tensor")
    dp_size = lax.axis_size("dp")
    exp_here = w_gate.shape[0]
    model_width = tokens.shape[1]
    capacity = tensor_size * -(-(5 * tok_count * TOP) // (4 * experts * tensor_size))
    slot_index, route_kept = slot_layout(routes, experts, capacity)
    kept_gates = jnp.where(route_kept, gates, 0.0)
    kept_float = route_kept.astype(jnp.float32)
    slot_token, slot_live, slot_gate = slot_owner(
        slot_index, route_kept, kept_gates, experts * capacity
    )
    send_rows = jnp.where(
        slot_live[:, None], normed_ffn_low[slot_token], jnp.zeros((), jnp.bfloat16)
    ).reshape(dp_size, exp_here, capacity, model_width)
    grad_send = (
        (cotangent[slot_token].astype(jnp.float32) * slot_gate[:, None])
        .astype(jnp.bfloat16)
        .reshape(dp_size, exp_here, capacity, model_width)
    )
    received, grad_recv = (
        lax.all_to_all(send_rows, "dp", split_axis=0, concat_axis=0, tiled=True),
        lax.all_to_all(grad_send, "dp", split_axis=0, concat_axis=0, tiled=True),
    )
    gate_pre = jnp.einsum("secd,edf->secf", received, w_gate, preferred_element_type=jnp.float32)
    up_pre = jnp.einsum("secd,edf->secf", received, w_up, preferred_element_type=jnp.float32)
    gate_sigmoid = jax.nn.sigmoid(gate_pre)
    gate_silu = gate_pre * gate_sigmoid
    expert_act = (gate_silu * up_pre).astype(jnp.bfloat16)
    expert_out = jnp.einsum(
        "secf,efd->secd", expert_act, w_down, preferred_element_type=jnp.float32
    ).astype(jnp.bfloat16)
    returned = lax.all_to_all(expert_out, "dp", split_axis=0, concat_axis=0, tiled=True).reshape(
        experts * capacity, model_width
    )
    gathered = returned[slot_index].astype(jnp.float32)
    routed_part = jnp.sum(gathered * kept_gates[:, :, None], axis=1)
    shared_gate = jnp.dot(normed_ffn_low, shared_gate_weight, preferred_element_type=jnp.float32)
    shared_up = jnp.dot(normed_ffn_low, shared_up_weight, preferred_element_type=jnp.float32)
    shared_sigmoid = jax.nn.sigmoid(shared_gate)
    shared_silu = shared_gate * shared_sigmoid
    shared_act = (shared_silu * shared_up).astype(jnp.bfloat16)
    shared_part = jnp.dot(shared_act, shared_down_weight, preferred_element_type=jnp.float32)
    moe_total = lax.psum((routed_part + shared_part).astype(jnp.bfloat16), "tensor").astype(
        jnp.float32
    )
    result = (resid_mid + moe_total).astype(jnp.bfloat16)
    cot_float = cotangent.astype(jnp.float32)
    act_grad = jnp.einsum("secd,efd->secf", grad_recv, w_down, preferred_element_type=jnp.float32)
    w_down_grad = jnp.einsum(
        "secf,secd->efd", expert_act, grad_recv, preferred_element_type=jnp.float32
    )
    gate_grad = (act_grad * up_pre * gate_sigmoid * (1.0 + gate_pre * (1.0 - gate_sigmoid))).astype(
        jnp.bfloat16
    )
    up_grad = (act_grad * gate_silu).astype(jnp.bfloat16)
    w_gate_grad = jnp.einsum(
        "secd,secf->edf", received, gate_grad, preferred_element_type=jnp.float32
    )
    w_up_grad = jnp.einsum("secd,secf->edf", received, up_grad, preferred_element_type=jnp.float32)
    rows_grad = (
        jnp.einsum("secf,edf->secd", gate_grad, w_gate, preferred_element_type=jnp.float32)
        + jnp.einsum("secf,edf->secd", up_grad, w_up, preferred_element_type=jnp.float32)
    ).astype(jnp.bfloat16)
    grad_back = lax.all_to_all(rows_grad, "dp", split_axis=0, concat_axis=0, tiled=True).reshape(
        experts * capacity, model_width
    )
    routed_in_grad = jnp.sum(
        grad_back[slot_index].astype(jnp.float32) * kept_float[:, :, None], axis=1
    )
    gate_grad_part = jnp.sum(gathered * cot_float[:, None, :], axis=-1) * kept_float
    shared_act_grad = jnp.einsum(
        "td,fd->tf", cotangent, shared_down_weight, preferred_element_type=jnp.float32
    )
    shared_down_grad = jnp.einsum(
        "tf,td->fd", shared_act, cotangent, preferred_element_type=jnp.float32
    )
    shared_gate_grad = (
        shared_act_grad * shared_up * shared_sigmoid * (1.0 + shared_gate * (1.0 - shared_sigmoid))
    ).astype(jnp.bfloat16)
    shared_up_grad = (shared_act_grad * shared_silu).astype(jnp.bfloat16)
    shared_gate_weight_grad = jnp.einsum(
        "td,tf->df", normed_ffn_low, shared_gate_grad, preferred_element_type=jnp.float32
    )
    shared_up_weight_grad = jnp.einsum(
        "td,tf->df", normed_ffn_low, shared_up_grad, preferred_element_type=jnp.float32
    )
    shared_in_grad = jnp.einsum(
        "tf,df->td", shared_gate_grad, shared_gate_weight, preferred_element_type=jnp.float32
    ) + jnp.einsum(
        "tf,df->td", shared_up_grad, shared_up_weight, preferred_element_type=jnp.float32
    )
    ffn_in_sum, gate_grad_sum = lax.psum(
        (routed_in_grad + shared_in_grad, gate_grad_part), "tensor"
    )
    picked_grad = (
        gate_grad_sum - jnp.sum(gate_grad_sum * gates, axis=-1, keepdims=True)
    ) / picked_total
    probs_grad = jnp.sum(jnp.where(route_hits, picked_grad[:, :, None], 0.0), axis=1)
    logit_grad = (
        router_probs * (probs_grad - jnp.sum(router_probs * probs_grad, axis=-1, keepdims=True))
    ).astype(jnp.bfloat16)
    router_grad = jnp.einsum(
        "td,te->de", normed_ffn_low, logit_grad, preferred_element_type=jnp.float32
    )
    ffn_in = ffn_in_sum + jnp.einsum(
        "te,de->td", logit_grad, router_weight, preferred_element_type=jnp.float32
    )
    ffn_resid_grad, gain_ffn_grad = norm_backward(resid_mid, inverse_ffn, gain_ffn_f, ffn_in)
    mid_grad = cot_float + ffn_resid_grad
    mid_low = mid_grad.astype(jnp.bfloat16)
    output_weight_grad = jnp.einsum(
        "th,td->hd", heads_low, mid_low, preferred_element_type=jnp.float32
    )
    heads_grad = (
        jnp.einsum("td,hd->th", mid_low, output_weight, preferred_element_type=jnp.float32)
        .astype(jnp.bfloat16)
        .reshape(tok_count, heads_here, V_HEAD)
    )
    query_grad_blocks = []
    key_grad = jnp.zeros((tok_count, heads_here, head_width), jnp.float32)
    value_grad = jnp.zeros((tok_count, heads_here, V_HEAD), jnp.float32)
    for block_number, row_start in enumerate(range(0, tok_count, tok_count)):
        row_stop = row_start + tok_count
        masked = block_scores(query_low, key_full, seq_ids, row_start)
        attn_probs = jnp.exp(masked - log_totals[block_number])
        probs_low = attn_probs.astype(jnp.bfloat16)
        prob_grad = jnp.einsum(
            "qhc,khc->hqk", heads_grad, value_low, preferred_element_type=jnp.float32
        )
        row_dot = jnp.sum(attn_probs * prob_grad, axis=-1, keepdims=True)
        score_grad = (attn_probs * (prob_grad - row_dot)).astype(jnp.bfloat16)
        query_grad_blocks.append(
            jnp.einsum("hqk,khc->qhc", score_grad, key_full, preferred_element_type=jnp.float32)
            * softmax_scale
        )
        key_grad = key_grad.at[:row_stop].add(
            jnp.einsum("hqk,qhc->khc", score_grad, query_low, preferred_element_type=jnp.float32)
            * softmax_scale
        )
        value_grad = value_grad.at[:row_stop].add(
            jnp.einsum("hqk,qhc->khc", probs_low, heads_grad, preferred_element_type=jnp.float32)
        )
    query_grad = query_grad_blocks[0]
    query_pre_grad = jnp.concatenate(
        [
            query_grad[..., :QK_NOPE],
            rotate(query_grad[..., QK_NOPE:], cosine[:, None, :], -sine_part[:, None, :]),
        ],
        axis=-1,
    )
    query_pre_grad = query_pre_grad.astype(jnp.bfloat16).reshape(tok_count, heads_here * head_width)
    attn_in_part = jnp.einsum(
        "tq,dq->td", query_pre_grad, query_weight, preferred_element_type=jnp.float32
    )
    query_weight_grad = jnp.einsum(
        "td,tq->dq", normed_attn_low, query_pre_grad, preferred_element_type=jnp.float32
    )
    expand_grad = (
        jnp.concatenate([key_grad[..., :QK_NOPE], value_grad], axis=-1)
        .astype(jnp.bfloat16)
        .reshape(tok_count, heads_here * (QK_NOPE + V_HEAD))
    )
    latent_part_grad = jnp.einsum(
        "te,re->tr", expand_grad, expand_weight, preferred_element_type=jnp.float32
    )
    expand_weight_grad = jnp.einsum(
        "tr,te->re", latent_low, expand_grad, preferred_element_type=jnp.float32
    )
    rope_part_grad = jnp.sum(key_grad[..., QK_NOPE:], axis=1)
    attn_in_sum, latent_sum, rope_sum = lax.psum(
        (attn_in_part, latent_part_grad, rope_part_grad), "tensor"
    )
    latent_pre_grad, gain_latent_grad = norm_backward(
        latent_part, inverse_latent, gain_latent_f, latent_sum
    )
    latent_all_grad = jnp.concatenate(
        [latent_pre_grad, rotate(rope_sum, cosine, -sine_part)], axis=-1
    ).astype(jnp.bfloat16)
    attn_in = attn_in_sum + jnp.einsum(
        "tc,dc->td", latent_all_grad, latent_weight, preferred_element_type=jnp.float32
    )
    latent_weight_grad = jnp.einsum(
        "td,tc->dc", normed_attn_low, latent_all_grad, preferred_element_type=jnp.float32
    )
    input_grad, gain_attn_grad = norm_backward(resid_in, inverse_attn, gain_attn_f, attn_in)
    tokens_grad = (mid_grad + input_grad).astype(jnp.bfloat16)
    (
        gain_attn_share,
        query_share,
        latent_share,
        gain_latent_share,
        expand_share,
        output_share,
        gain_ffn_share,
        router_share,
        shared_gate_share,
        shared_up_share,
        shared_down_share,
    ) = (
        lax.psum_scatter(
            gain_attn_grad.astype(jnp.bfloat16), "dp", scatter_dimension=0, tiled=True
        ).astype(jnp.float32),
        lax.psum_scatter(
            query_weight_grad.astype(jnp.bfloat16), "dp", scatter_dimension=0, tiled=True
        ).astype(jnp.float32),
        lax.psum_scatter(
            latent_weight_grad.astype(jnp.bfloat16), "dp", scatter_dimension=0, tiled=True
        ).astype(jnp.float32),
        lax.psum_scatter(
            gain_latent_grad.astype(jnp.bfloat16), "dp", scatter_dimension=0, tiled=True
        ).astype(jnp.float32),
        lax.psum_scatter(
            expand_weight_grad.astype(jnp.bfloat16), "dp", scatter_dimension=0, tiled=True
        ).astype(jnp.float32),
        lax.psum_scatter(
            output_weight_grad.astype(jnp.bfloat16), "dp", scatter_dimension=1, tiled=True
        ).astype(jnp.float32),
        lax.psum_scatter(
            gain_ffn_grad.astype(jnp.bfloat16), "dp", scatter_dimension=0, tiled=True
        ).astype(jnp.float32),
        lax.psum_scatter(
            router_grad.astype(jnp.bfloat16), "dp", scatter_dimension=0, tiled=True
        ).astype(jnp.float32),
        lax.psum_scatter(
            shared_gate_weight_grad.astype(jnp.bfloat16), "dp", scatter_dimension=0, tiled=True
        ).astype(jnp.float32),
        lax.psum_scatter(
            shared_up_weight_grad.astype(jnp.bfloat16), "dp", scatter_dimension=0, tiled=True
        ).astype(jnp.float32),
        lax.psum_scatter(
            shared_down_grad.astype(jnp.bfloat16), "dp", scatter_dimension=1, tiled=True
        ).astype(jnp.float32),
    )
    return (
        result,
        tokens_grad,
        gain_attn_share,
        query_share,
        latent_share,
        gain_latent_share,
        expand_share,
        output_share,
        gain_ffn_share,
        router_share,
        shared_gate_share,
        shared_up_share,
        shared_down_share,
        w_gate_grad,
        w_up_grad,
        w_down_grad,
    )

def hop(values, axis, bit):
    return lax.ppermute(values, axis, [(i, i ^ bit) for i in range(lax.axis_size(axis))])


def core_hop(values):
    return hop(values, "tensor", 1)


def y_hop(values):
    return hop(values, "tensor", 2)


def x_hop(values):
    return hop(values, "dp", 1)


def z_hop(values):
    count = lax.axis_size("dp")
    return lax.ppermute(values, "dp", [(i, (i + 2) % count) for i in range(count)])


def low(values):
    return values.astype(jnp.bfloat16)


class Flow:
    def __init__(self):
        self.tasks = []

    def launch(self, steps):
        task = Task(steps)
        self.tasks.append(task)
        return task

    def close(self, values):
        live = [task for task in self.tasks if not task.done]
        values, arrived = lax.optimization_barrier((values, [task.sent for task in live]))
        for task, got in zip(live, arrived):
            task.advance(got)
        return values


class Task:
    def __init__(self, steps):
        self.steps, self.done, self.result = steps, False, None
        self.advance(None)

    def advance(self, got):
        try:
            self.sent = self.steps.send(got)
        except StopIteration as stop:
            self.done, self.result = True, stop.value


def held(values, count):
    for _ in range(count):
        (values,) = yield [values]
    return values


def passing(values):
    (got,) = yield [z_hop(values)]
    return got


def plane_gather_split(own):
    half = own.shape[0] // 2
    first, second = own[:half], own[half:]
    first_x, second_y = yield [x_hop(first), y_hop(second)]
    first_pair = jnp.concatenate([first, first_x])
    second_pair = jnp.concatenate([second, second_y])
    first_y, second_x = yield [y_hop(first_pair), x_hop(second_pair)]
    quarter = jnp.concatenate(
        [
            own,
            first_x,
            second_x[:half],
            first_y[:half],
            second_y,
            first_y[half:],
            second_x[half:],
        ]
    )
    (far,) = yield [core_hop(quarter)]
    return jnp.concatenate([quarter, far])


def plane_gather(own, before=0, windows=1):
    (far,) = yield [x_hop(own)]
    far = yield from held(far, before)
    pair = jnp.concatenate([own, far])
    far = y_hop(pair)
    for _ in range(windows - 1):
        yield []
    (far,) = yield [far]
    quarter = jnp.concatenate([pair, far])
    (far,) = yield [core_hop(quarter)]
    return jnp.concatenate([quarter, far])


def plane_scatter(part, x_first, before=0, between=0):
    part = part.reshape(2, 2, 2, part.shape[0] // 8, part.shape[1])
    (far,) = yield [core_hop(part[1])]
    far = yield from held(far, before)
    total = part[0].astype(jnp.float32) + far.astype(jnp.float32)
    near, away = (total[:, 0], total[:, 1]) if x_first else (total[0], total[1])
    (far,) = yield [x_hop(low(away)) if x_first else y_hop(low(away))]
    far = yield from held(far, between)
    near = near + far.astype(jnp.float32)
    (far,) = yield [y_hop(low(near[1])) if x_first else x_hop(low(near[1]))]
    return near[0] + far.astype(jnp.float32)


def tensor_scatter(values, tensor_index):
    rows = values.shape[0] // 4
    width = values.shape[1]
    core = tensor_index % 2
    level = tensor_index // 2
    blocks = values.reshape(2, 2, rows, width)
    mine = lax.dynamic_index_in_dim(blocks, core, 1, keepdims=False)
    other = lax.dynamic_index_in_dim(blocks, 1 - core, 1, keepdims=False)
    total = mine.astype(jnp.float32) + core_hop(low(other)).astype(jnp.float32)
    near = lax.dynamic_index_in_dim(total, level, 0, keepdims=False)
    far = lax.dynamic_index_in_dim(total, 1 - level, 0, keepdims=False)
    return near + y_hop(low(far)).astype(jnp.float32)


def tensor_gather(own, tensor_index):
    own_y = y_hop(own)
    pair = jnp.stack([own, own_y])
    pair_core = core_hop(pair)
    core = tensor_index % 2
    level = tensor_index // 2
    even = jnp.where(core == 0, pair, pair_core)
    odd = jnp.where(core == 0, pair_core, pair)
    near = jnp.concatenate([even[0], odd[0]])
    far = jnp.concatenate([even[1], odd[1]])
    return jnp.concatenate(
        [jnp.where(level == 0, near, far), jnp.where(level == 0, far, near)]
    )


def laid_out(arrived, axes, dp_index):
    planes = len(arrived[0]) // 2
    plane = dp_index // 2
    side = dp_index % 2
    wholes = []
    for pieces, axis in zip(arrived, axes):
        extent = pieces[0].shape[axis]
        shape = list(pieces[0].shape)
        shape[axis] *= 2 * planes
        whole = jnp.zeros(shape, pieces[0].dtype)
        for k, piece in enumerate(pieces):
            home = (plane - k // 2) % planes * 2 + (side if k % 2 == 0 else 1 - side)
            whole = lax.dynamic_update_slice_in_dim(whole, piece, home * extent, axis)
        wholes.append(whole)
    return wholes


def dp_ring(pieces, axes, dp_index):
    planes = lax.axis_size("dp") // 2
    arrived = [[] for _ in axes]
    for step in range(planes):
        sent = [x_hop(piece) for piece in pieces]
        if step + 1 < planes:
            sent += [z_hop(piece) for piece in pieces]
        got = yield sent
        for i in range(len(axes)):
            arrived[i] += [pieces[i], got[i]]
        pieces = got[len(axes) :]
    return laid_out(arrived, axes, dp_index)


def side_ring(own, dp_index, tensor_index):
    steps = dp_ring([own], [1], dp_index)
    sent = next(steps)
    while True:
        try:
            sent = steps.send(sent)
        except StopIteration as stop:
            (whole,) = stop.value
            break
    (whole,) = yield [whole]
    (far,) = yield [y_hop(whole)]
    pair = jnp.stack([whole, far])
    (far,) = yield [core_hop(pair)]
    core = tensor_index % 2
    level = tensor_index // 2
    even = jnp.where(core == 0, pair, far)
    odd = jnp.where(core == 0, far, pair)
    near = jnp.stack([even, odd], axis=1)
    whole = jnp.where(level == 0, near, near[::-1])
    return whole.reshape((4 * own.shape[0],) + whole.shape[3:])


def dp_scatter_steps(block, dp_index):
    planes = lax.axis_size("dp") // 2
    plane = dp_index // 2
    side = dp_index % 2
    bases = [(plane - step) % planes * 2 for step in list(range(1, planes)) + [0]]
    half = len(bases) // 2
    away = [low(block(base + 1 - side)) for base in bases]
    first, second = yield [x_hop(jnp.stack(away[:half])), x_hop(jnp.stack(away[half:]))]
    received = [first[i] for i in range(half)] + [second[i] for i in range(len(bases) - half)]
    moving = None
    for base, far in zip(bases, received):
        piece = block(base + side) + far.astype(jnp.float32)
        if moving is not None:
            (got,) = yield [z_hop(low(moving))]
            piece = piece + got.astype(jnp.float32)
        moving = piece
    return moving


def drained(task):
    while not task.done:
        task.advance(task.sent)
    return task.result


def dp_scatter(block, dp_index):
    return drained(Task(dp_scatter_steps(block, dp_index)))


def padded(values, axis, size):
    pads = [(0, 0)] * values.ndim
    pads[axis] = (0, size - values.shape[axis])
    return jnp.pad(values, pads)


def lanes(size):
    return -(-size // 128) * 128


def body_dense(
    tokens,
    cotangent,
    routes,
    seq_ids,
    positions,
    gain_attn,
    w_query,
    w_latent,
    gain_latent,
    w_expand,
    w_output,
    gain_ffn,
    w_router,
    w_shared_gate,
    w_shared_up,
    w_shared_down,
    w_gate,
    w_up,
    w_down,
):
    tensor_size = lax.axis_size("tensor")
    dp_size = lax.axis_size("dp")
    dp_index = lax.axis_index("dp")
    tensor_index = lax.axis_index("tensor")
    tok_count, width = tokens.shape
    own_count = tok_count // tensor_size
    own_start = tensor_index * own_count
    experts = w_router.shape[1]
    exp_here = w_gate.shape[0]
    capacity = tensor_size * -(-(5 * tok_count * TOP) // (4 * experts * tensor_size))

    def own_rows(values):
        return lax.dynamic_slice_in_dim(values, own_start, own_count, 0)

    lat_width = w_latent.shape[1]
    lat_block = w_latent.shape[0]
    routed = jnp.sum(
        (routes[:, :, None] == jnp.arange(experts, dtype=jnp.int32)[None, None, :]).astype(
            jnp.float32
        ),
        axis=1,
    )
    order = jnp.arange(tok_count, dtype=jnp.int32)
    earlier = (order[None, :] < order[:, None]).astype(jnp.bfloat16)
    rank = jnp.dot(earlier, low(routed), preferred_element_type=jnp.float32)
    standing = routed * (1.0 + (rank < capacity).astype(jnp.float32))
    standing_own = own_rows(standing)
    cot_own = own_rows(cotangent)

    folds = tok_count // lat_block
    mark_start = lat_width + experts
    gain_start = mark_start + folds * experts
    side_rows = lanes(gain_start + 3)
    side = jnp.concatenate(
        [w_latent.T, w_router.T]
        + [
            low(standing[fold * lat_block : (fold + 1) * lat_block]).T
            for fold in range(folds)
        ]
        + [jnp.stack([gain_attn, gain_ffn, padded(gain_latent, 0, lat_block)])]
    )
    side_rows_here = side_rows // tensor_size
    side = lax.dynamic_slice_in_dim(
        padded(side, 0, side_rows), tensor_index * side_rows_here, side_rows_here, 0
    )

    flow = Flow()
    side_task = flow.launch(side_ring(side, dp_index, tensor_index))
    weights = flow.close((w_query, w_expand, w_output))
    weight_task = flow.launch(dp_ring(weights, [0, 0, 1], dp_index))
    for _ in range(2):
        flow.close(())

    core = tensor_index % 2
    level = tensor_index // 2
    planes = dp_size // 2
    side_all = side_task.result
    latent_weight = side_all[:lat_width]
    router_weight = side_all[lat_width:mark_start]
    marks_all = side_all[mark_start:gain_start].reshape(folds, experts, dp_size, lat_block)
    marks_all = marks_all.transpose(2, 0, 3, 1).reshape(planes, 8, own_count, experts)
    gains_all = side_all[gain_start : gain_start + 3].astype(jnp.float32)
    gain_attn_f = gains_all[0]
    gain_ffn_f = gains_all[1]
    gain_latent_f = gains_all[2].reshape(dp_size, lat_block)[:, : gain_latent.shape[0]].reshape(
        KV_RANK
    )
    near = jnp.arange(8, dtype=jnp.int32)
    near_x = near % 2 ^ dp_index % 2
    near_y = near // 2 % 2 ^ level
    near_core = near // 4 ^ core
    near_block = near_x * 4 + near_y * 2 + near_core
    mark_chunks = [
        jnp.take(
            lax.dynamic_index_in_dim(
                marks_all, (dp_index // 2 - step) % planes, 0, keepdims=False
            ),
            near_block,
            axis=0,
        ).reshape(8 * own_count, experts)
        for step in range(planes)
    ]
    flow.close(())
    cot_pass = flow.launch(passing(cot_own))

    head_width = QK_NOPE + QK_ROPE
    heads_here = w_query.shape[1] // head_width
    softmax_scale = head_width ** (-0.5)
    resid_in = tokens.astype(jnp.float32)
    normed_attn, inverse_attn = norm_forward(resid_in, gain_attn_f)
    normed_attn_low = low(normed_attn)
    cosine, sine_part = rope_tables(positions, QK_ROPE)
    latent_raw = jnp.einsum(
        "td,cd->tc", normed_attn_low, latent_weight, preferred_element_type=jnp.float32
    )
    latent_part = latent_raw[:, :KV_RANK]
    latent_normed, inverse_latent = norm_forward(latent_part, gain_latent_f)
    latent_low = low(latent_normed)
    key_rope_low = low(rotate(latent_raw[:, KV_RANK:], cosine, sine_part))
    normed_attn_low, latent_low, key_rope_low, w_shared_gate, w_shared_up, w_shared_down = (
        flow.close(
            (normed_attn_low, latent_low, key_rope_low, w_shared_gate, w_shared_up, w_shared_down)
        )
    )

    query_weight, expand_weight, output_weight = weight_task.result
    cot_tasks = [flow.launch(plane_gather(cot_own))]
    cot_piece = cot_pass.result
    cot_pass = flow.launch(passing(cot_piece))
    query_raw = jnp.dot(normed_attn_low, query_weight, preferred_element_type=jnp.float32).reshape(
        tok_count, heads_here, head_width
    )
    query_low = low(
        jnp.concatenate(
            [
                query_raw[..., :QK_NOPE],
                rotate(query_raw[..., QK_NOPE:], cosine[:, None, :], sine_part[:, None, :]),
            ],
            axis=-1,
        )
    )
    expanded = low(jnp.dot(latent_low, expand_weight, preferred_element_type=jnp.float32))
    query_low, expanded = flow.close((query_low, expanded))

    cot_tasks.append(flow.launch(plane_gather(cot_piece, 4, 2)))
    cot_piece = cot_pass.result
    cot_pass = flow.launch(passing(cot_piece))
    expanded = expanded.reshape(tok_count, heads_here, QK_NOPE + V_HEAD)
    value_low = expanded[..., QK_NOPE:]
    key_full = jnp.concatenate(
        [
            expanded[..., :QK_NOPE],
            jnp.broadcast_to(key_rope_low[:, None, :], (tok_count, heads_here, QK_ROPE)),
        ],
        axis=-1,
    )
    masked = block_scores(query_low, key_full, seq_ids, 0)
    row_max = jnp.max(masked, axis=-1, keepdims=True)
    exponent = jnp.exp(masked - row_max)
    exp_total = jnp.sum(exponent, axis=-1, keepdims=True)
    probs_low = low(exponent / exp_total)
    log_total = row_max + jnp.log(exp_total)
    heads_low = low(
        jnp.einsum("hqk,khc->qhc", probs_low, value_low, preferred_element_type=jnp.float32)
    ).reshape(tok_count, heads_here * V_HEAD)
    attn_part = jnp.dot(heads_low, output_weight, preferred_element_type=jnp.float32)
    attn_part = flow.close(attn_part)

    cot_tasks.append(flow.launch(plane_gather(cot_piece, 6, 2)))
    cot_piece = cot_pass.result
    resid_own = own_rows(tokens).astype(jnp.float32) + tensor_scatter(attn_part, tensor_index)
    normed_own, inverse_own = norm_forward(resid_own, gain_ffn_f)
    normed_own_low = flow.close(low(normed_own))

    row_tasks = [flow.launch(plane_gather_split(normed_own_low))]
    row_pass = flow.launch(passing(normed_own_low))
    shared_here = w_shared_gate.shape[1] // dp_size
    shared = lax.all_to_all(
        jnp.stack([w_shared_gate.T, w_shared_up.T, w_shared_down]),
        "dp",
        split_axis=1,
        concat_axis=2,
        tiled=True,
    )
    group = w_gate.shape[2]
    routed_here = exp_here * group
    hidden = routed_here + shared_here
    gate_weight = jnp.concatenate([w_gate.swapaxes(1, 2).reshape(routed_here, width), shared[0]])
    up_weight = jnp.concatenate([w_up.swapaxes(1, 2).reshape(routed_here, width), shared[1]])
    down_weight = jnp.concatenate([w_down.reshape(routed_here, width), shared[2]])
    gate_weight, up_weight, down_weight = flow.close((gate_weight, up_weight, down_weight))
    for _ in range(2):
        flow.close(())

    def gating(rows, standing_rows):
        probs = jax.nn.softmax(
            jnp.einsum("td,ed->te", rows, router_weight, preferred_element_type=jnp.float32),
            axis=-1,
        )
        gates = jnp.where(standing_rows > 0.5, probs, 0.0)
        picked = jnp.sum(gates, axis=-1, keepdims=True)
        return probs, gates / picked, picked

    expert_index = jnp.arange(experts, dtype=jnp.int32)[None, :]
    column = jnp.arange(hidden, dtype=jnp.int32)[None, :]
    row_piece = row_pass.result
    in_tasks, out_tasks, gate_parts, kept_parts = [], [], [], []
    in_part = None
    for step in range(planes):
        rows = row_tasks[step].result
        if step + 1 < planes:
            row_tasks.append(flow.launch(plane_gather(row_piece)))
            if step + 2 < planes:
                row_pass = flow.launch(passing(row_piece))
        if step > 0:
            in_tasks.append(flow.launch(plane_scatter(in_part, True)))
        if step == planes - 1:
            in_moving = flow.launch(passing(low(in_tasks[1].result)))
        gate_pre = jnp.einsum("td,fd->tf", rows, gate_weight, preferred_element_type=jnp.float32)
        up_pre = jnp.einsum("td,fd->tf", rows, up_weight, preferred_element_type=jnp.float32)
        gate_pre, up_pre, rows = flow.close((gate_pre, up_pre, rows))
        if step + 2 < planes:
            row_piece = row_pass.result

        cots = cot_tasks[step].result
        marks = mark_chunks[step].astype(jnp.float32)
        _, chunk_gates, _ = gating(rows, marks)
        chunk_gates = jnp.where(marks > 1.5, chunk_gates, 0.0)
        scale = jnp.ones((rows.shape[0], hidden), jnp.float32)
        for e in reversed(range(exp_here)):
            here = expert_index == dp_index * exp_here + e
            gate_column = jnp.sum(jnp.where(here, chunk_gates, 0.0), axis=-1, keepdims=True)
            scale = jnp.where(column < (e + 1) * group, gate_column, scale)
        sigmoid = jax.nn.sigmoid(gate_pre)
        silu = gate_pre * sigmoid
        act = silu * up_pre
        act_scaled = low(act * scale)
        out_part = low(jnp.dot(act_scaled, down_weight, preferred_element_type=jnp.float32))
        act_grad = jnp.einsum("td,fd->tf", cots, down_weight, preferred_element_type=jnp.float32)
        meeting = act * act_grad
        gate_parts.append(
            jnp.stack(
                [
                    jnp.sum(jnp.where(column // group == e, meeting, 0.0), axis=-1)
                    for e in range(exp_here)
                ]
            )
        )
        scaled_grad = act_grad * scale
        gate_grad = low(scaled_grad * up_pre * sigmoid * (1.0 + gate_pre * (1.0 - sigmoid)))
        up_grad = low(scaled_grad * silu)
        gate_grad, up_grad, act_scaled, out_part, rows, cots = flow.close(
            (gate_grad, up_grad, act_scaled, out_part, rows, cots)
        )

        after = (planes - 1 - step) * 3
        places = {0: (after + 6, 0), 1: (after, 1), 2: (after + 1, 1), 3: (after + 5, 0)}[step]
        out_tasks.append(flow.launch(plane_scatter(out_part, False, *places)))
        if step == 0:
            cot_tasks.append(flow.launch(plane_gather(cot_piece, 3, 2)))
        in_part = low(
            jnp.dot(gate_grad, gate_weight, preferred_element_type=jnp.float32)
            + jnp.dot(up_grad, up_weight, preferred_element_type=jnp.float32)
        )
        in_part, gate_grad, up_grad, act_scaled, rows, cots = flow.close(
            (in_part, gate_grad, up_grad, act_scaled, rows, cots)
        )
        kept_parts.append((rows, cots, gate_grad, up_grad, act_scaled))

    in_tasks.append(flow.launch(plane_scatter(in_part, True)))
    in_moving = flow.launch(
        passing(low(in_tasks[2].result + in_moving.result.astype(jnp.float32)))
    )
    gate_sums = jnp.stack(gate_parts).reshape(-1, exp_here, 2, 2, 2, own_count)
    gate_sums = gate_sums[:, :, 0] + core_hop(gate_sums[:, :, 1])
    gate_sums = gate_sums[:, :, 0] + y_hop(gate_sums[:, :, 1])
    block = jnp.arange(dp_size, dtype=jnp.int32)
    place = ((dp_index // 2 - block // 2) % planes) * 2 + (block + dp_index) % 2
    gate_sums = gate_sums.transpose(0, 2, 1, 3).reshape(dp_size, exp_here, own_count)[place]
    gate_weight_grad = sum(
        jnp.einsum("tf,td->fd", gate_grad, rows, preferred_element_type=jnp.float32)
        for rows, _, gate_grad, _, _ in kept_parts
    )
    gate_weight_grad, kept_parts, gate_sums = flow.close(
        (gate_weight_grad, kept_parts, gate_sums)
    )
    gate_sums = lax.all_to_all(gate_sums, "dp", split_axis=0, concat_axis=0, tiled=True)
    gate_sums = gate_sums.reshape(experts, own_count).T
    up_weight_grad = sum(
        jnp.einsum("tf,td->fd", up_grad, rows, preferred_element_type=jnp.float32)
        for rows, _, _, up_grad, _ in kept_parts
    )
    gate_sums, up_weight_grad, kept_parts = flow.close((gate_sums, up_weight_grad, kept_parts))
    flow.close(())
    in_moving = flow.launch(
        passing(low(in_tasks[3].result + in_moving.result.astype(jnp.float32)))
    )
    kept_parts = flow.close(kept_parts)
    out_moving = flow.launch(passing(low(out_tasks[1].result)))
    ffn_sum = in_tasks[0].result + in_moving.result.astype(jnp.float32)
    probs_own, gates_own, picked_own = gating(normed_own_low, standing_own)
    gate_sums = jnp.where(standing_own > 1.5, gate_sums, 0.0)
    picked_grad = (
        gate_sums - jnp.sum(gate_sums * gates_own, axis=-1, keepdims=True)
    ) / picked_own
    probs_grad = jnp.where(standing_own > 0.5, picked_grad, 0.0)
    logit_grad = low(
        probs_own * (probs_grad - jnp.sum(probs_own * probs_grad, axis=-1, keepdims=True))
    )
    router_grad = jnp.einsum(
        "te,td->ed", logit_grad, normed_own_low, preferred_element_type=jnp.float32
    )
    ffn_in = ffn_sum + jnp.dot(logit_grad, router_weight, preferred_element_type=jnp.float32)
    ffn_resid_grad, gain_ffn_grad = norm_backward(resid_own, inverse_own, gain_ffn_f, ffn_in)
    mid_grad_own = cot_own.astype(jnp.float32) + ffn_resid_grad
    shared_parts = [gate_weight_grad, up_weight_grad]
    mid_low, kept_parts, shared_parts = flow.close(
        (tensor_gather(low(mid_grad_own), tensor_index), kept_parts, shared_parts)
    )
    out_moving = flow.launch(
        passing(low(out_tasks[2].result + out_moving.result.astype(jnp.float32)))
    )
    down_weight_grad = sum(
        jnp.einsum("tf,td->fd", act_scaled, cots, preferred_element_type=jnp.float32)
        for _, cots, _, _, act_scaled in kept_parts[: planes // 2]
    )

    def shared_sum(grads):
        grads = jnp.stack([low(grad[routed_here:]) for grad in grads])
        return lax.all_to_all(grads, "dp", split_axis=2, concat_axis=1, tiled=True).astype(
            jnp.float32
        )

    shared_grads = shared_sum(shared_parts)
    output_weight_grad = jnp.einsum(
        "th,td->hd", heads_low, mid_low, preferred_element_type=jnp.float32
    )
    heads_grad = low(
        jnp.einsum("td,hd->th", mid_low, output_weight, preferred_element_type=jnp.float32)
    ).reshape(tok_count, heads_here, V_HEAD)
    heads_grad, output_weight_grad, down_weight_grad, kept_parts = flow.close(
        (heads_grad, output_weight_grad, down_weight_grad, kept_parts)
    )
    down_weight_grad += sum(
        jnp.einsum("tf,td->fd", act_scaled, cots, preferred_element_type=jnp.float32)
        for _, cots, _, _, act_scaled in kept_parts[planes // 2 :]
    )
    output_task = flow.launch(
        dp_scatter_steps(
            lambda i: lax.dynamic_slice_in_dim(
                output_weight_grad, i * w_output.shape[1], w_output.shape[1], 1
            ),
            dp_index,
        )
    )
    masked = block_scores(query_low, key_full, seq_ids, 0)
    attn_probs = jnp.exp(masked - log_total)
    prob_grad = jnp.einsum("qhc,khc->hqk", heads_grad, value_low, preferred_element_type=jnp.float32)
    row_dot = jnp.sum(attn_probs * prob_grad, axis=-1, keepdims=True)
    score_grad = low(attn_probs * (prob_grad - row_dot))
    score_grad, probs_low, down_weight_grad = flow.close(
        (score_grad, low(attn_probs), down_weight_grad)
    )
    out_moving = flow.launch(
        passing(low(out_tasks[3].result + out_moving.result.astype(jnp.float32)))
    )
    query_grad = (
        jnp.einsum("hqk,khc->qhc", score_grad, key_full, preferred_element_type=jnp.float32)
        * softmax_scale
    )
    key_grad = (
        jnp.einsum("hqk,qhc->khc", score_grad, query_low, preferred_element_type=jnp.float32)
        * softmax_scale
    )
    value_grad = jnp.einsum(
        "hqk,qhc->khc", probs_low, heads_grad, preferred_element_type=jnp.float32
    )
    query_grad, key_grad, value_grad = flow.close((query_grad, key_grad, value_grad))
    query_pre_grad = low(
        jnp.concatenate(
            [
                query_grad[..., :QK_NOPE],
                rotate(query_grad[..., QK_NOPE:], cosine[:, None, :], -sine_part[:, None, :]),
            ],
            axis=-1,
        )
    ).reshape(tok_count, heads_here * head_width)
    query_weight_grad = jnp.einsum(
        "td,tq->dq", normed_attn_low, query_pre_grad, preferred_element_type=jnp.float32
    )
    expand_grad = low(jnp.concatenate([key_grad[..., :QK_NOPE], value_grad], axis=-1)).reshape(
        tok_count, heads_here * (QK_NOPE + V_HEAD)
    )
    latent_grad = jnp.einsum(
        "te,re->tr", expand_grad, expand_weight, preferred_element_type=jnp.float32
    )
    expand_weight_grad = jnp.einsum(
        "tr,te->re", latent_low, expand_grad, preferred_element_type=jnp.float32
    )
    latent_grad, query_weight_grad, expand_weight_grad = flow.close(
        (latent_grad, query_weight_grad, expand_weight_grad)
    )
    rope_grad = jnp.sum(key_grad[..., QK_NOPE:], axis=1)
    latent_pre_grad, gain_latent_grad = norm_backward(
        latent_part, inverse_latent, gain_latent_f, latent_grad
    )
    latent_all_grad = low(
        jnp.concatenate([latent_pre_grad, rotate(rope_grad, cosine, -sine_part)], axis=-1)
    )
    attn_in = jnp.einsum(
        "tq,dq->td", query_pre_grad, query_weight, preferred_element_type=jnp.float32
    ) + jnp.dot(latent_all_grad, latent_weight, preferred_element_type=jnp.float32)
    latent_weight_grad = jnp.einsum(
        "tc,td->cd", latent_all_grad, normed_attn_low, preferred_element_type=jnp.float32
    )
    gain_attn_grad = jnp.sum(attn_in * (resid_in * inverse_attn), axis=0)
    attn_in_own = tensor_scatter(attn_in, tensor_index)
    input_grad, _ = norm_backward(
        own_rows(resid_in), own_rows(inverse_attn), gain_attn_f, attn_in_own
    )
    tokens_grad = tensor_gather(low(mid_grad_own + input_grad), tensor_index)

    out_sum = out_tasks[0].result + out_moving.result.astype(jnp.float32)
    result = tensor_gather(low(resid_own + out_sum), tensor_index)

    output_share = drained(output_task)
    query_share = dp_scatter(
        lambda i: lax.dynamic_slice_in_dim(query_weight_grad, i * lat_block, lat_block, 0),
        dp_index,
    )
    expand_block = w_expand.shape[0]
    expand_share = dp_scatter(
        lambda i: lax.dynamic_slice_in_dim(expand_weight_grad, i * expand_block, expand_block, 0),
        dp_index,
    )

    gain_latent_rows = padded(gain_latent_grad.reshape(dp_size, -1), 1, lat_block).reshape(width)
    gain_grads = jnp.stack([gain_attn_grad, gain_ffn_grad, gain_latent_rows])
    side_grad = jnp.concatenate(
        [
            low(latent_weight_grad),
            low(router_grad),
            padded(low(gain_grads), 0, side_rows - mark_start),
        ]
    ).reshape(2, 2, side_rows_here, width)
    kept_side = lax.dynamic_index_in_dim(side_grad, core, 1, keepdims=False)
    sent_side = lax.dynamic_index_in_dim(side_grad, 1 - core, 1, keepdims=False)
    side_grad = kept_side.astype(jnp.float32) + core_hop(sent_side).astype(jnp.float32)
    kept_side = lax.dynamic_index_in_dim(side_grad, level, 0, keepdims=False)
    sent_side = lax.dynamic_index_in_dim(side_grad, 1 - level, 0, keepdims=False)
    side_grad = kept_side + y_hop(low(sent_side)).astype(jnp.float32)
    side_piece = dp_scatter(
        lambda i: lax.dynamic_slice_in_dim(side_grad, i * lat_block, lat_block, 1), dp_index
    )
    grad_full = tensor_gather(low(side_piece), tensor_index).astype(jnp.float32)
    latent_share = grad_full[:lat_width].T
    router_share = grad_full[lat_width:mark_start].T
    gain_attn_share = grad_full[mark_start]
    gain_ffn_share = grad_full[mark_start + 1]
    gain_latent_share = grad_full[mark_start + 2, : gain_latent.shape[0]]

    def routed_grad(grad):
        return grad[:routed_here].reshape(exp_here, group, width)

    routed_grads = (
        routed_grad(gate_weight_grad).swapaxes(1, 2),
        routed_grad(up_weight_grad).swapaxes(1, 2),
        routed_grad(down_weight_grad),
    )
    shared_down_grad = lax.all_to_all(
        low(down_weight_grad[routed_here:]), "dp", split_axis=1, concat_axis=0, tiled=True
    ).astype(jnp.float32)

    return (
        result,
        tokens_grad,
        gain_attn_share,
        query_share,
        latent_share,
        gain_latent_share,
        expand_share,
        output_share,
        gain_ffn_share,
        router_share,
        shared_grads[0].T,
        shared_grads[1].T,
        shared_down_grad,
        *routed_grads,
    )


def solution(mesh):
    dense = mesh.shape["dp"] == 8 and mesh.shape["tensor"] == 4
    return jax.shard_map(
        body_dense if dense else body,
        mesh=mesh,
        in_specs=(
            P("dp", None),
            P("dp", None),
            P("dp", None),
            P("dp"),
            P("dp"),
            P("dp"),
            P("dp", "tensor"),
            P("dp", None),
            P("dp"),
            P("dp", "tensor"),
            P("tensor", "dp"),
            P("dp"),
            P("dp", None),
            P("dp", "tensor"),
            P("dp", "tensor"),
            P("tensor", "dp"),
            P("dp", None, "tensor"),
            P("dp", None, "tensor"),
            P("dp", "tensor", None),
        ),
        out_specs=(
            P("dp", None),
            P("dp", None),
            P("dp"),
            P("dp", "tensor"),
            P("dp", None),
            P("dp"),
            P("dp", "tensor"),
            P("tensor", "dp"),
            P("dp"),
            P("dp", None),
            P("dp", "tensor"),
            P("dp", "tensor"),
            P("tensor", "dp"),
            P("dp", None, "tensor"),
            P("dp", None, "tensor"),
            P("dp", "tensor", None),
        ),
        check_vma=False,
    )
```

```python
import jax
import jax.numpy as jnp
from jax import lax
from jax.sharding import PartitionSpec as P

QK_NOPE = 128
QK_ROPE = 64
V_HEAD = 128
KV_RANK = 512
TOP = 6


EPSILON = 1e-06
MASKED = -1e30


def norm_forward(values, gain_full):
    inverse = lax.rsqrt(jnp.mean(values * values, axis=-1, keepdims=True) + EPSILON)
    return (values * inverse * gain_full, inverse)


def norm_backward(values, inverse, gain_full, grad_out):
    normed = values * inverse
    scaled = grad_out * gain_full
    grad_in = inverse * (scaled - normed * jnp.mean(scaled * normed, axis=-1, keepdims=True))
    return (grad_in, jnp.sum(grad_out * normed, axis=0))


def rope_tables(positions, width):
    half_width = width // 2
    frequency = jnp.power(10000.0, -jnp.arange(half_width, dtype=jnp.float32) / half_width)
    angles = positions.astype(jnp.float32)[:, None] * frequency[None, :]
    return (jnp.cos(angles), jnp.sin(angles))


def rotate(values, cosine, sine_part):
    half_width = values.shape[-1] // 2
    front_half = values[..., :half_width]
    back_half = values[..., half_width:]
    return jnp.concatenate(
        [front_half * cosine - back_half * sine_part, back_half * cosine + front_half * sine_part],
        axis=-1,
    )


def slot_layout(routes, experts, capacity):
    flat_routes = routes.reshape(-1)
    onehot = (flat_routes[:, None] == jnp.arange(experts, dtype=jnp.int32)[None, :]).astype(
        jnp.int32
    )
    before = jnp.cumsum(onehot, axis=0) - onehot
    slot_rank = jnp.sum(before * onehot, axis=1)
    route_kept = slot_rank < capacity
    slot_index = flat_routes * capacity + jnp.minimum(slot_rank, capacity - 1)
    return (slot_index.reshape(routes.shape), route_kept.reshape(routes.shape))


def slot_owner(slot_index, route_kept, kept_gates, slot_total):
    pair_count = slot_index.size
    target = jnp.where(route_kept.reshape(-1), slot_index.reshape(-1), slot_total)
    token_rows = jnp.arange(pair_count, dtype=jnp.int32) // slot_index.shape[-1]
    slot_token = jnp.zeros((slot_total,), jnp.int32).at[target].set(token_rows, mode="drop")
    slot_live = jnp.zeros((slot_total,), jnp.bool_).at[target].set(True, mode="drop")
    slot_gate = (
        jnp.zeros((slot_total,), jnp.float32).at[target].set(kept_gates.reshape(-1), mode="drop")
    )
    return (slot_token, slot_live, slot_gate)


def block_scores(query_block, key_block, seq_ids, row_start):
    row_count = query_block.shape[0]
    key_count = key_block.shape[0]
    raw_scores = jnp.einsum(
        "qhc,khc->hqk", query_block, key_block, preferred_element_type=jnp.float32
    ) * (QK_NOPE + QK_ROPE) ** (-0.5)
    query_index = row_start + jnp.arange(row_count, dtype=jnp.int32)
    key_index = jnp.arange(key_count, dtype=jnp.int32)
    allowed = (seq_ids[:, None] == seq_ids[None, :]) & (key_index[None, :] <= query_index[:, None])
    return jnp.where(allowed[None], raw_scores, MASKED)


def body(
    tokens,
    cotangent,
    routes,
    seq_ids,
    positions,
    gain_attn,
    w_query,
    w_latent,
    gain_latent,
    w_expand,
    w_output,
    gain_ffn,
    w_router,
    w_shared_gate,
    w_shared_up,
    w_shared_down,
    w_gate,
    w_up,
    w_down,
):
    (
        gain_attn_all,
        query_weight,
        latent_weight,
        gain_latent_all,
        expand_weight,
        output_weight,
        gain_ffn_all,
        router_weight,
        shared_gate_weight,
        shared_up_weight,
        shared_down_weight,
    ) = (
        lax.all_gather(gain_attn, "dp", axis=0, tiled=True),
        lax.all_gather(w_query, "dp", axis=0, tiled=True),
        lax.all_gather(w_latent, "dp", axis=0, tiled=True),
        lax.all_gather(gain_latent, "dp", axis=0, tiled=True),
        lax.all_gather(w_expand, "dp", axis=0, tiled=True),
        lax.all_gather(w_output, "dp", axis=1, tiled=True),
        lax.all_gather(gain_ffn, "dp", axis=0, tiled=True),
        lax.all_gather(w_router, "dp", axis=0, tiled=True),
        lax.all_gather(w_shared_gate, "dp", axis=0, tiled=True),
        lax.all_gather(w_shared_up, "dp", axis=0, tiled=True),
        lax.all_gather(w_shared_down, "dp", axis=1, tiled=True),
    )
    tok_count = tokens.shape[0]
    head_width = QK_NOPE + QK_ROPE
    heads_here = query_weight.shape[1] // head_width
    softmax_scale = head_width ** (-0.5)
    gain_attn_f = gain_attn_all.astype(jnp.float32)
    gain_latent_f = gain_latent_all.astype(jnp.float32)
    resid_in = tokens.astype(jnp.float32)
    normed_attn, inverse_attn = norm_forward(resid_in, gain_attn_f)
    normed_attn_low = normed_attn.astype(jnp.bfloat16)
    cosine, sine_part = rope_tables(positions, QK_ROPE)
    query_raw = jnp.dot(normed_attn_low, query_weight, preferred_element_type=jnp.float32).reshape(
        tok_count, heads_here, head_width
    )
    query_low = jnp.concatenate(
        [
            query_raw[..., :QK_NOPE],
            rotate(query_raw[..., QK_NOPE:], cosine[:, None, :], sine_part[:, None, :]),
        ],
        axis=-1,
    ).astype(jnp.bfloat16)
    latent_raw = jnp.dot(normed_attn_low, latent_weight, preferred_element_type=jnp.float32)
    latent_part = latent_raw[:, :KV_RANK]
    latent_normed, inverse_latent = norm_forward(latent_part, gain_latent_f)
    latent_low = latent_normed.astype(jnp.bfloat16)
    key_rope_low = rotate(latent_raw[:, KV_RANK:], cosine, sine_part).astype(jnp.bfloat16)
    expanded = (
        jnp.dot(latent_low, expand_weight, preferred_element_type=jnp.float32)
        .astype(jnp.bfloat16)
        .reshape(tok_count, heads_here, QK_NOPE + V_HEAD)
    )
    value_low = expanded[..., QK_NOPE:]
    key_full = jnp.concatenate(
        [
            expanded[..., :QK_NOPE],
            jnp.broadcast_to(key_rope_low[:, None, :], (tok_count, heads_here, QK_ROPE)),
        ],
        axis=-1,
    )
    row_start = 0
    row_stop = row_start + tok_count
    masked = block_scores(query_low, key_full, seq_ids, row_start)
    row_max = jnp.max(masked, axis=-1, keepdims=True)
    exponent = jnp.exp(masked - row_max)
    exp_total = jnp.sum(exponent, axis=-1, keepdims=True)
    attn_probs = (exponent / exp_total).astype(jnp.bfloat16)
    log_totals = [row_max + jnp.log(exp_total)]
    head_blocks = jnp.einsum(
        "hqk,khc->qhc", attn_probs, value_low, preferred_element_type=jnp.float32
    )
    heads_low = head_blocks.astype(jnp.bfloat16).reshape(tok_count, heads_here * V_HEAD)
    attn_part = jnp.dot(heads_low, output_weight, preferred_element_type=jnp.float32)
    resid_mid = resid_in + lax.psum(attn_part, "tensor")
    gain_ffn_f = gain_ffn_all.astype(jnp.float32)
    normed_ffn, inverse_ffn = norm_forward(resid_mid, gain_ffn_f)
    normed_ffn_low = normed_ffn.astype(jnp.bfloat16)
    experts = router_weight.shape[1]
    router_probs = jax.nn.softmax(
        jnp.dot(normed_ffn_low, router_weight, preferred_element_type=jnp.float32), axis=-1
    )
    route_hits = routes[:, :, None] == jnp.arange(experts, dtype=jnp.int32)[None, None, :]
    picked = jnp.sum(jnp.where(route_hits, router_probs[:, None, :], 0.0), axis=-1)
    picked_total = jnp.sum(picked, axis=-1, keepdims=True)
    gates = picked / picked_total
    tensor_size = lax.axis_size("tensor")
    dp_size = lax.axis_size("dp")
    exp_here = w_gate.shape[0]
    model_width = tokens.shape[1]
    capacity = tensor_size * -(-(5 * tok_count * TOP) // (4 * experts * tensor_size))
    slot_index, route_kept = slot_layout(routes, experts, capacity)
    kept_gates = jnp.where(route_kept, gates, 0.0)
    kept_float = route_kept.astype(jnp.float32)
    slot_token, slot_live, slot_gate = slot_owner(
        slot_index, route_kept, kept_gates, experts * capacity
    )
    send_rows = jnp.where(
        slot_live[:, None], normed_ffn_low[slot_token], jnp.zeros((), jnp.bfloat16)
    ).reshape(dp_size, exp_here, capacity, model_width)
    grad_send = (
        (cotangent[slot_token].astype(jnp.float32) * slot_gate[:, None])
        .astype(jnp.bfloat16)
        .reshape(dp_size, exp_here, capacity, model_width)
    )
    received, grad_recv = (
        lax.all_to_all(send_rows, "dp", split_axis=0, concat_axis=0, tiled=True),
        lax.all_to_all(grad_send, "dp", split_axis=0, concat_axis=0, tiled=True),
    )
    gate_pre = jnp.einsum("secd,edf->secf", received, w_gate, preferred_element_type=jnp.float32)
    up_pre = jnp.einsum("secd,edf->secf", received, w_up, preferred_element_type=jnp.float32)
    gate_sigmoid = jax.nn.sigmoid(gate_pre)
    gate_silu = gate_pre * gate_sigmoid
    expert_act = (gate_silu * up_pre).astype(jnp.bfloat16)
    expert_out = jnp.einsum(
        "secf,efd->secd", expert_act, w_down, preferred_element_type=jnp.float32
    ).astype(jnp.bfloat16)
    returned = lax.all_to_all(expert_out, "dp", split_axis=0, concat_axis=0, tiled=True).reshape(
        experts * capacity, model_width
    )
    gathered = returned[slot_index].astype(jnp.float32)
    routed_part = jnp.sum(gathered * kept_gates[:, :, None], axis=1)
    shared_gate = jnp.dot(normed_ffn_low, shared_gate_weight, preferred_element_type=jnp.float32)
    shared_up = jnp.dot(normed_ffn_low, shared_up_weight, preferred_element_type=jnp.float32)
    shared_sigmoid = jax.nn.sigmoid(shared_gate)
    shared_silu = shared_gate * shared_sigmoid
    shared_act = (shared_silu * shared_up).astype(jnp.bfloat16)
    shared_part = jnp.dot(shared_act, shared_down_weight, preferred_element_type=jnp.float32)
    moe_total = lax.psum((routed_part + shared_part).astype(jnp.bfloat16), "tensor").astype(
        jnp.float32
    )
    result = (resid_mid + moe_total).astype(jnp.bfloat16)
    cot_float = cotangent.astype(jnp.float32)
    act_grad = jnp.einsum("secd,efd->secf", grad_recv, w_down, preferred_element_type=jnp.float32)
    w_down_grad = jnp.einsum(
        "secf,secd->efd", expert_act, grad_recv, preferred_element_type=jnp.float32
    )
    gate_grad = (act_grad * up_pre * gate_sigmoid * (1.0 + gate_pre * (1.0 - gate_sigmoid))).astype(
        jnp.bfloat16
    )
    up_grad = (act_grad * gate_silu).astype(jnp.bfloat16)
    w_gate_grad = jnp.einsum(
        "secd,secf->edf", received, gate_grad, preferred_element_type=jnp.float32
    )
    w_up_grad = jnp.einsum("secd,secf->edf", received, up_grad, preferred_element_type=jnp.float32)
    rows_grad = (
        jnp.einsum("secf,edf->secd", gate_grad, w_gate, preferred_element_type=jnp.float32)
        + jnp.einsum("secf,edf->secd", up_grad, w_up, preferred_element_type=jnp.float32)
    ).astype(jnp.bfloat16)
    grad_back = lax.all_to_all(rows_grad, "dp", split_axis=0, concat_axis=0, tiled=True).reshape(
        experts * capacity, model_width
    )
    routed_in_grad = jnp.sum(
        grad_back[slot_index].astype(jnp.float32) * kept_float[:, :, None], axis=1
    )
    gate_grad_part = jnp.sum(gathered * cot_float[:, None, :], axis=-1) * kept_float
    shared_act_grad = jnp.einsum(
        "td,fd->tf", cotangent, shared_down_weight, preferred_element_type=jnp.float32
    )
    shared_down_grad = jnp.einsum(
        "tf,td->fd", shared_act, cotangent, preferred_element_type=jnp.float32
    )
    shared_gate_grad = (
        shared_act_grad * shared_up * shared_sigmoid * (1.0 + shared_gate * (1.0 - shared_sigmoid))
    ).astype(jnp.bfloat16)
    shared_up_grad = (shared_act_grad * shared_silu).astype(jnp.bfloat16)
    shared_gate_weight_grad = jnp.einsum(
        "td,tf->df", normed_ffn_low, shared_gate_grad, preferred_element_type=jnp.float32
    )
    shared_up_weight_grad = jnp.einsum(
        "td,tf->df", normed_ffn_low, shared_up_grad, preferred_element_type=jnp.float32
    )
    shared_in_grad = jnp.einsum(
        "tf,df->td", shared_gate_grad, shared_gate_weight, preferred_element_type=jnp.float32
    ) + jnp.einsum(
        "tf,df->td", shared_up_grad, shared_up_weight, preferred_element_type=jnp.float32
    )
    ffn_in_sum, gate_grad_sum = lax.psum(
        (routed_in_grad + shared_in_grad, gate_grad_part), "tensor"
    )
    picked_grad = (
        gate_grad_sum - jnp.sum(gate_grad_sum * gates, axis=-1, keepdims=True)
    ) / picked_total
    probs_grad = jnp.sum(jnp.where(route_hits, picked_grad[:, :, None], 0.0), axis=1)
    logit_grad = (
        router_probs * (probs_grad - jnp.sum(router_probs * probs_grad, axis=-1, keepdims=True))
    ).astype(jnp.bfloat16)
    router_grad = jnp.einsum(
        "td,te->de", normed_ffn_low, logit_grad, preferred_element_type=jnp.float32
    )
    ffn_in = ffn_in_sum + jnp.einsum(
        "te,de->td", logit_grad, router_weight, preferred_element_type=jnp.float32
    )
    ffn_resid_grad, gain_ffn_grad = norm_backward(resid_mid, inverse_ffn, gain_ffn_f, ffn_in)
    mid_grad = cot_float + ffn_resid_grad
    mid_low = mid_grad.astype(jnp.bfloat16)
    output_weight_grad = jnp.einsum(
        "th,td->hd", heads_low, mid_low, preferred_element_type=jnp.float32
    )
    heads_grad = (
        jnp.einsum("td,hd->th", mid_low, output_weight, preferred_element_type=jnp.float32)
        .astype(jnp.bfloat16)
        .reshape(tok_count, heads_here, V_HEAD)
    )
    query_grad_blocks = []
    key_grad = jnp.zeros((tok_count, heads_here, head_width), jnp.float32)
    value_grad = jnp.zeros((tok_count, heads_here, V_HEAD), jnp.float32)
    for block_number, row_start in enumerate(range(0, tok_count, tok_count)):
        row_stop = row_start + tok_count
        masked = block_scores(query_low, key_full, seq_ids, row_start)
        attn_probs = jnp.exp(masked - log_totals[block_number])
        probs_low = attn_probs.astype(jnp.bfloat16)
        prob_grad = jnp.einsum(
            "qhc,khc->hqk", heads_grad, value_low, preferred_element_type=jnp.float32
        )
        row_dot = jnp.sum(attn_probs * prob_grad, axis=-1, keepdims=True)
        score_grad = (attn_probs * (prob_grad - row_dot)).astype(jnp.bfloat16)
        query_grad_blocks.append(
            jnp.einsum("hqk,khc->qhc", score_grad, key_full, preferred_element_type=jnp.float32)
            * softmax_scale
        )
        key_grad = key_grad.at[:row_stop].add(
            jnp.einsum("hqk,qhc->khc", score_grad, query_low, preferred_element_type=jnp.float32)
            * softmax_scale
        )
        value_grad = value_grad.at[:row_stop].add(
            jnp.einsum("hqk,qhc->khc", probs_low, heads_grad, preferred_element_type=jnp.float32)
        )
    query_grad = query_grad_blocks[0]
    query_pre_grad = jnp.concatenate(
        [
            query_grad[..., :QK_NOPE],
            rotate(query_grad[..., QK_NOPE:], cosine[:, None, :], -sine_part[:, None, :]),
        ],
        axis=-1,
    )
    query_pre_grad = query_pre_grad.astype(jnp.bfloat16).reshape(tok_count, heads_here * head_width)
    attn_in_part = jnp.einsum(
        "tq,dq->td", query_pre_grad, query_weight, preferred_element_type=jnp.float32
    )
    query_weight_grad = jnp.einsum(
        "td,tq->dq", normed_attn_low, query_pre_grad, preferred_element_type=jnp.float32
    )
    expand_grad = (
        jnp.concatenate([key_grad[..., :QK_NOPE], value_grad], axis=-1)
        .astype(jnp.bfloat16)
        .reshape(tok_count, heads_here * (QK_NOPE + V_HEAD))
    )
    latent_part_grad = jnp.einsum(
        "te,re->tr", expand_grad, expand_weight, preferred_element_type=jnp.float32
    )
    expand_weight_grad = jnp.einsum(
        "tr,te->re", latent_low, expand_grad, preferred_element_type=jnp.float32
    )
    rope_part_grad = jnp.sum(key_grad[..., QK_NOPE:], axis=1)
    attn_in_sum, latent_sum, rope_sum = lax.psum(
        (attn_in_part, latent_part_grad, rope_part_grad), "tensor"
    )
    latent_pre_grad, gain_latent_grad = norm_backward(
        latent_part, inverse_latent, gain_latent_f, latent_sum
    )
    latent_all_grad = jnp.concatenate(
        [latent_pre_grad, rotate(rope_sum, cosine, -sine_part)], axis=-1
    ).astype(jnp.bfloat16)
    attn_in = attn_in_sum + jnp.einsum(
        "tc,dc->td", latent_all_grad, latent_weight, preferred_element_type=jnp.float32
    )
    latent_weight_grad = jnp.einsum(
        "td,tc->dc", normed_attn_low, latent_all_grad, preferred_element_type=jnp.float32
    )
    input_grad, gain_attn_grad = norm_backward(resid_in, inverse_attn, gain_attn_f, attn_in)
    tokens_grad = (mid_grad + input_grad).astype(jnp.bfloat16)
    (
        gain_attn_share,
        query_share,
        latent_share,
        gain_latent_share,
        expand_share,
        output_share,
        gain_ffn_share,
        router_share,
        shared_gate_share,
        shared_up_share,
        shared_down_share,
    ) = (
        lax.psum_scatter(
            gain_attn_grad.astype(jnp.bfloat16), "dp", scatter_dimension=0, tiled=True
        ).astype(jnp.float32),
        lax.psum_scatter(
            query_weight_grad.astype(jnp.bfloat16), "dp", scatter_dimension=0, tiled=True
        ).astype(jnp.float32),
        lax.psum_scatter(
            latent_weight_grad.astype(jnp.bfloat16), "dp", scatter_dimension=0, tiled=True
        ).astype(jnp.float32),
        lax.psum_scatter(
            gain_latent_grad.astype(jnp.bfloat16), "dp", scatter_dimension=0, tiled=True
        ).astype(jnp.float32),
        lax.psum_scatter(
            expand_weight_grad.astype(jnp.bfloat16), "dp", scatter_dimension=0, tiled=True
        ).astype(jnp.float32),
        lax.psum_scatter(
            output_weight_grad.astype(jnp.bfloat16), "dp", scatter_dimension=1, tiled=True
        ).astype(jnp.float32),
        lax.psum_scatter(
            gain_ffn_grad.astype(jnp.bfloat16), "dp", scatter_dimension=0, tiled=True
        ).astype(jnp.float32),
        lax.psum_scatter(
            router_grad.astype(jnp.bfloat16), "dp", scatter_dimension=0, tiled=True
        ).astype(jnp.float32),
        lax.psum_scatter(
            shared_gate_weight_grad.astype(jnp.bfloat16), "dp", scatter_dimension=0, tiled=True
        ).astype(jnp.float32),
        lax.psum_scatter(
            shared_up_weight_grad.astype(jnp.bfloat16), "dp", scatter_dimension=0, tiled=True
        ).astype(jnp.float32),
        lax.psum_scatter(
            shared_down_grad.astype(jnp.bfloat16), "dp", scatter_dimension=1, tiled=True
        ).astype(jnp.float32),
    )
    return (
        result,
        tokens_grad,
        gain_attn_share,
        query_share,
        latent_share,
        gain_latent_share,
        expand_share,
        output_share,
        gain_ffn_share,
        router_share,
        shared_gate_share,
        shared_up_share,
        shared_down_share,
        w_gate_grad,
        w_up_grad,
        w_down_grad,
    )

def hop(values, axis, bit):
    return lax.ppermute(values, axis, [(i, i ^ bit) for i in range(lax.axis_size(axis))])


def core_hop(values):
    return hop(values, "tensor", 1)


def y_hop(values):
    return hop(values, "tensor", 2)


def x_hop(values):
    return hop(values, "dp", 1)


def z_hop(values):
    count = lax.axis_size("dp")
    return lax.ppermute(values, "dp", [(i, (i + 2) % count) for i in range(count)])


def low(values):
    return values.astype(jnp.bfloat16)


class Flow:
    def __init__(self):
        self.tasks = []

    def launch(self, steps):
        task = Task(steps)
        self.tasks.append(task)
        return task

    def close(self, values):
        live = [task for task in self.tasks if not task.done]
        values, arrived = lax.optimization_barrier((values, [task.sent for task in live]))
        for task, got in zip(live, arrived):
            task.advance(got)
        return values


class Task:
    def __init__(self, steps):
        self.steps, self.done, self.result = steps, False, None
        self.advance(None)

    def advance(self, got):
        try:
            self.sent = self.steps.send(got)
        except StopIteration as stop:
            self.done, self.result = True, stop.value


def held(values, count):
    for _ in range(count):
        (values,) = yield [values]
    return values


def passing(values):
    (got,) = yield [z_hop(values)]
    return got


def plane_gather_split(own):
    half = own.shape[0] // 2
    first, second = own[:half], own[half:]
    first_x, second_y = yield [x_hop(first), y_hop(second)]
    first_pair = jnp.concatenate([first, first_x])
    second_pair = jnp.concatenate([second, second_y])
    first_y, second_x = yield [y_hop(first_pair), x_hop(second_pair)]
    quarter = jnp.concatenate(
        [
            own,
            first_x,
            second_x[:half],
            first_y[:half],
            second_y,
            first_y[half:],
            second_x[half:],
        ]
    )
    (far,) = yield [core_hop(quarter)]
    return jnp.concatenate([quarter, far])


def plane_gather(own, before=0, windows=1):
    (far,) = yield [x_hop(own)]
    far = yield from held(far, before)
    pair = jnp.concatenate([own, far])
    far = y_hop(pair)
    for _ in range(windows - 1):
        yield []
    (far,) = yield [far]
    quarter = jnp.concatenate([pair, far])
    (far,) = yield [core_hop(quarter)]
    return jnp.concatenate([quarter, far])


def plane_scatter(part, x_first, before=0, between=0):
    part = part.reshape(2, 2, 2, part.shape[0] // 8, part.shape[1])
    (far,) = yield [core_hop(part[1])]
    far = yield from held(far, before)
    total = part[0].astype(jnp.float32) + far.astype(jnp.float32)
    near, away = (total[:, 0], total[:, 1]) if x_first else (total[0], total[1])
    (far,) = yield [x_hop(low(away)) if x_first else y_hop(low(away))]
    far = yield from held(far, between)
    near = near + far.astype(jnp.float32)
    (far,) = yield [y_hop(low(near[1])) if x_first else x_hop(low(near[1]))]
    return near[0] + far.astype(jnp.float32)


def tensor_scatter(values, tensor_index):
    rows = values.shape[0] // 4
    width = values.shape[1]
    core = tensor_index % 2
    level = tensor_index // 2
    blocks = values.reshape(2, 2, rows, width)
    mine = lax.dynamic_index_in_dim(blocks, core, 1, keepdims=False)
    other = lax.dynamic_index_in_dim(blocks, 1 - core, 1, keepdims=False)
    total = mine.astype(jnp.float32) + core_hop(low(other)).astype(jnp.float32)
    near = lax.dynamic_index_in_dim(total, level, 0, keepdims=False)
    far = lax.dynamic_index_in_dim(total, 1 - level, 0, keepdims=False)
    return near + y_hop(low(far)).astype(jnp.float32)


def tensor_gather(own, tensor_index):
    own_y = y_hop(own)
    pair = jnp.stack([own, own_y])
    pair_core = core_hop(pair)
    core = tensor_index % 2
    level = tensor_index // 2
    even = jnp.where(core == 0, pair, pair_core)
    odd = jnp.where(core == 0, pair_core, pair)
    near = jnp.concatenate([even[0], odd[0]])
    far = jnp.concatenate([even[1], odd[1]])
    return jnp.concatenate(
        [jnp.where(level == 0, near, far), jnp.where(level == 0, far, near)]
    )


def laid_out(arrived, axes, dp_index):
    planes = len(arrived[0]) // 2
    plane = dp_index // 2
    side = dp_index % 2
    wholes = []
    for pieces, axis in zip(arrived, axes):
        extent = pieces[0].shape[axis]
        shape = list(pieces[0].shape)
        shape[axis] *= 2 * planes
        whole = jnp.zeros(shape, pieces[0].dtype)
        for k, piece in enumerate(pieces):
            home = (plane - k // 2) % planes * 2 + (side if k % 2 == 0 else 1 - side)
            whole = lax.dynamic_update_slice_in_dim(whole, piece, home * extent, axis)
        wholes.append(whole)
    return wholes


def dp_ring(pieces, axes, dp_index):
    planes = lax.axis_size("dp") // 2
    arrived = [[] for _ in axes]
    for step in range(planes):
        sent = [x_hop(piece) for piece in pieces]
        if step + 1 < planes:
            sent += [z_hop(piece) for piece in pieces]
        got = yield sent
        for i in range(len(axes)):
            arrived[i] += [pieces[i], got[i]]
        pieces = got[len(axes) :]
    return laid_out(arrived, axes, dp_index)


def side_ring(own, dp_index, tensor_index):
    steps = dp_ring([own], [1], dp_index)
    sent = next(steps)
    while True:
        try:
            sent = steps.send(sent)
        except StopIteration as stop:
            (whole,) = stop.value
            break
    (whole,) = yield [whole]
    (far,) = yield [y_hop(whole)]
    pair = jnp.stack([whole, far])
    (far,) = yield [core_hop(pair)]
    core = tensor_index % 2
    level = tensor_index // 2
    even = jnp.where(core == 0, pair, far)
    odd = jnp.where(core == 0, far, pair)
    near = jnp.stack([even, odd], axis=1)
    whole = jnp.where(level == 0, near, near[::-1])
    return whole.reshape((4 * own.shape[0],) + whole.shape[3:])


def dp_scatter_steps(block, dp_index):
    planes = lax.axis_size("dp") // 2
    plane = dp_index // 2
    side = dp_index % 2
    bases = [(plane - step) % planes * 2 for step in list(range(1, planes)) + [0]]
    half = len(bases) // 2
    away = [low(block(base + 1 - side)) for base in bases]
    first, second = yield [x_hop(jnp.stack(away[:half])), x_hop(jnp.stack(away[half:]))]
    received = [first[i] for i in range(half)] + [second[i] for i in range(len(bases) - half)]
    moving = None
    for base, far in zip(bases, received):
        piece = block(base + side) + far.astype(jnp.float32)
        if moving is not None:
            (got,) = yield [z_hop(low(moving))]
            piece = piece + got.astype(jnp.float32)
        moving = piece
    return moving


def drained(task):
    while not task.done:
        task.advance(task.sent)
    return task.result


def dp_scatter(block, dp_index):
    return drained(Task(dp_scatter_steps(block, dp_index)))


def padded(values, axis, size):
    pads = [(0, 0)] * values.ndim
    pads[axis] = (0, size - values.shape[axis])
    return jnp.pad(values, pads)


def lanes(size):
    return -(-size // 128) * 128


def body_dense(
    tokens,
    cotangent,
    routes,
    seq_ids,
    positions,
    gain_attn,
    w_query,
    w_latent,
    gain_latent,
    w_expand,
    w_output,
    gain_ffn,
    w_router,
    w_shared_gate,
    w_shared_up,
    w_shared_down,
    w_gate,
    w_up,
    w_down,
):
    tensor_size = lax.axis_size("tensor")
    dp_size = lax.axis_size("dp")
    dp_index = lax.axis_index("dp")
    tensor_index = lax.axis_index("tensor")
    tok_count, width = tokens.shape
    own_count = tok_count // tensor_size
    own_start = tensor_index * own_count
    experts = w_router.shape[1]
    exp_here = w_gate.shape[0]
    capacity = tensor_size * -(-(5 * tok_count * TOP) // (4 * experts * tensor_size))

    def own_rows(values):
        return lax.dynamic_slice_in_dim(values, own_start, own_count, 0)

    lat_width = w_latent.shape[1]
    lat_block = w_latent.shape[0]
    routed = jnp.sum(
        (routes[:, :, None] == jnp.arange(experts, dtype=jnp.int32)[None, None, :]).astype(
            jnp.float32
        ),
        axis=1,
    )
    order = jnp.arange(tok_count, dtype=jnp.int32)
    earlier = (order[None, :] < order[:, None]).astype(jnp.bfloat16)
    rank = jnp.dot(earlier, low(routed), preferred_element_type=jnp.float32)
    standing = routed * (1.0 + (rank < capacity).astype(jnp.float32))
    standing_own = own_rows(standing)
    cot_own = own_rows(cotangent)

    folds = tok_count // lat_block
    mark_start = lat_width + experts
    gain_start = mark_start + folds * experts
    side_rows = lanes(gain_start + 3)
    side = jnp.concatenate(
        [w_latent.T, w_router.T]
        + [
            low(standing[fold * lat_block : (fold + 1) * lat_block]).T
            for fold in range(folds)
        ]
        + [jnp.stack([gain_attn, gain_ffn, padded(gain_latent, 0, lat_block)])]
    )
    side_rows_here = side_rows // tensor_size
    side = lax.dynamic_slice_in_dim(
        padded(side, 0, side_rows), tensor_index * side_rows_here, side_rows_here, 0
    )

    flow = Flow()
    side_task = flow.launch(side_ring(side, dp_index, tensor_index))
    weights = flow.close((w_query, w_expand, w_output))
    weight_task = flow.launch(dp_ring(weights, [0, 0, 1], dp_index))
    for _ in range(2):
        flow.close(())

    core = tensor_index % 2
    level = tensor_index // 2
    planes = dp_size // 2
    side_all = side_task.result
    latent_weight = side_all[:lat_width]
    router_weight = side_all[lat_width:mark_start]
    marks_all = side_all[mark_start:gain_start].reshape(folds, experts, dp_size, lat_block)
    marks_all = marks_all.transpose(2, 0, 3, 1).reshape(planes, 8, own_count, experts)
    gains_all = side_all[gain_start : gain_start + 3].astype(jnp.float32)
    gain_attn_f = gains_all[0]
    gain_ffn_f = gains_all[1]
    gain_latent_f = gains_all[2].reshape(dp_size, lat_block)[:, : gain_latent.shape[0]].reshape(
        KV_RANK
    )
    near = jnp.arange(8, dtype=jnp.int32)
    near_x = near % 2 ^ dp_index % 2
    near_y = near // 2 % 2 ^ level
    near_core = near // 4 ^ core
    near_block = near_x * 4 + near_y * 2 + near_core
    mark_chunks = [
        jnp.take(
            lax.dynamic_index_in_dim(
                marks_all, (dp_index // 2 - step) % planes, 0, keepdims=False
            ),
            near_block,
            axis=0,
        ).reshape(8 * own_count, experts)
        for step in range(planes)
    ]
    flow.close(())
    cot_pass = flow.launch(passing(cot_own))

    head_width = QK_NOPE + QK_ROPE
    heads_here = w_query.shape[1] // head_width
    softmax_scale = head_width ** (-0.5)
    resid_in = tokens.astype(jnp.float32)
    normed_attn, inverse_attn = norm_forward(resid_in, gain_attn_f)
    normed_attn_low = low(normed_attn)
    cosine, sine_part = rope_tables(positions, QK_ROPE)
    latent_raw = jnp.einsum(
        "td,cd->tc", normed_attn_low, latent_weight, preferred_element_type=jnp.float32
    )
    latent_part = latent_raw[:, :KV_RANK]
    latent_normed, inverse_latent = norm_forward(latent_part, gain_latent_f)
    latent_low = low(latent_normed)
    key_rope_low = low(rotate(latent_raw[:, KV_RANK:], cosine, sine_part))
    normed_attn_low, latent_low, key_rope_low, w_shared_gate, w_shared_up, w_shared_down = (
        flow.close(
            (normed_attn_low, latent_low, key_rope_low, w_shared_gate, w_shared_up, w_shared_down)
        )
    )

    query_weight, expand_weight, output_weight = weight_task.result
    cot_tasks = [flow.launch(plane_gather(cot_own))]
    cot_piece = cot_pass.result
    cot_pass = flow.launch(passing(cot_piece))
    query_raw = jnp.dot(normed_attn_low, query_weight, preferred_element_type=jnp.float32).reshape(
        tok_count, heads_here, head_width
    )
    query_low = low(
        jnp.concatenate(
            [
                query_raw[..., :QK_NOPE],
                rotate(query_raw[..., QK_NOPE:], cosine[:, None, :], sine_part[:, None, :]),
            ],
            axis=-1,
        )
    )
    expanded = low(jnp.dot(latent_low, expand_weight, preferred_element_type=jnp.float32))
    query_low, expanded = flow.close((query_low, expanded))

    cot_tasks.append(flow.launch(plane_gather(cot_piece, 4, 2)))
    cot_piece = cot_pass.result
    cot_pass = flow.launch(passing(cot_piece))
    expanded = expanded.reshape(tok_count, heads_here, QK_NOPE + V_HEAD)
    value_low = expanded[..., QK_NOPE:]
    key_full = jnp.concatenate(
        [
            expanded[..., :QK_NOPE],
            jnp.broadcast_to(key_rope_low[:, None, :], (tok_count, heads_here, QK_ROPE)),
        ],
        axis=-1,
    )
    masked = block_scores(query_low, key_full, seq_ids, 0)
    row_max = jnp.max(masked, axis=-1, keepdims=True)
    exponent = jnp.exp(masked - row_max)
    exp_total = jnp.sum(exponent, axis=-1, keepdims=True)
    probs_low = low(exponent / exp_total)
    log_total = row_max + jnp.log(exp_total)
    heads_low = low(
        jnp.einsum("hqk,khc->qhc", probs_low, value_low, preferred_element_type=jnp.float32)
    ).reshape(tok_count, heads_here * V_HEAD)
    attn_part = jnp.dot(heads_low, output_weight, preferred_element_type=jnp.float32)
    attn_part = flow.close(attn_part)

    cot_tasks.append(flow.launch(plane_gather(cot_piece, 6, 2)))
    cot_piece = cot_pass.result
    resid_own = own_rows(tokens).astype(jnp.float32) + tensor_scatter(attn_part, tensor_index)
    normed_own, inverse_own = norm_forward(resid_own, gain_ffn_f)
    normed_own_low = flow.close(low(normed_own))

    row_tasks = [flow.launch(plane_gather_split(normed_own_low))]
    row_pass = flow.launch(passing(normed_own_low))
    shared_here = w_shared_gate.shape[1] // dp_size
    shared = lax.all_to_all(
        jnp.stack([w_shared_gate.T, w_shared_up.T, w_shared_down]),
        "dp",
        split_axis=1,
        concat_axis=2,
        tiled=True,
    )
    group = w_gate.shape[2]
    routed_here = exp_here * group
    hidden = routed_here + shared_here
    gate_weight = jnp.concatenate([w_gate.swapaxes(1, 2).reshape(routed_here, width), shared[0]])
    up_weight = jnp.concatenate([w_up.swapaxes(1, 2).reshape(routed_here, width), shared[1]])
    down_weight = jnp.concatenate([w_down.reshape(routed_here, width), shared[2]])
    gate_weight, up_weight, down_weight = flow.close((gate_weight, up_weight, down_weight))
    for _ in range(2):
        flow.close(())

    def gating(rows, standing_rows):
        probs = jax.nn.softmax(
            jnp.einsum("td,ed->te", rows, router_weight, preferred_element_type=jnp.float32),
            axis=-1,
        )
        gates = jnp.where(standing_rows > 0.5, probs, 0.0)
        picked = jnp.sum(gates, axis=-1, keepdims=True)
        return probs, gates / picked, picked

    expert_index = jnp.arange(experts, dtype=jnp.int32)[None, :]
    column = jnp.arange(hidden, dtype=jnp.int32)[None, :]
    row_piece = row_pass.result
    in_tasks, out_tasks, gate_parts, kept_parts = [], [], [], []
    in_part = None
    for step in range(planes):
        rows = row_tasks[step].result
        if step + 1 < planes:
            row_tasks.append(flow.launch(plane_gather(row_piece)))
            if step + 2 < planes:
                row_pass = flow.launch(passing(row_piece))
        if step > 0:
            in_tasks.append(flow.launch(plane_scatter(in_part, True)))
        if step == planes - 1:
            in_moving = flow.launch(passing(low(in_tasks[1].result)))
        gate_pre = jnp.einsum("td,fd->tf", rows, gate_weight, preferred_element_type=jnp.float32)
        up_pre = jnp.einsum("td,fd->tf", rows, up_weight, preferred_element_type=jnp.float32)
        gate_pre, up_pre, rows = flow.close((gate_pre, up_pre, rows))
        if step + 2 < planes:
            row_piece = row_pass.result

        cots = cot_tasks[step].result
        marks = mark_chunks[step].astype(jnp.float32)
        _, chunk_gates, _ = gating(rows, marks)
        chunk_gates = jnp.where(marks > 1.5, chunk_gates, 0.0)
        scale = jnp.ones((rows.shape[0], hidden), jnp.float32)
        for e in reversed(range(exp_here)):
            here = expert_index == dp_index * exp_here + e
            gate_column = jnp.sum(jnp.where(here, chunk_gates, 0.0), axis=-1, keepdims=True)
            scale = jnp.where(column < (e + 1) * group, gate_column, scale)
        sigmoid = jax.nn.sigmoid(gate_pre)
        silu = gate_pre * sigmoid
        act = silu * up_pre
        act_scaled = low(act * scale)
        out_part = low(jnp.dot(act_scaled, down_weight, preferred_element_type=jnp.float32))
        act_grad = jnp.einsum("td,fd->tf", cots, down_weight, preferred_element_type=jnp.float32)
        meeting = act * act_grad
        gate_parts.append(
            jnp.stack(
                [
                    jnp.sum(jnp.where(column // group == e, meeting, 0.0), axis=-1)
                    for e in range(exp_here)
                ]
            )
        )
        scaled_grad = act_grad * scale
        gate_grad = low(scaled_grad * up_pre * sigmoid * (1.0 + gate_pre * (1.0 - sigmoid)))
        up_grad = low(scaled_grad * silu)
        gate_grad, up_grad, act_scaled, out_part, rows, cots = flow.close(
            (gate_grad, up_grad, act_scaled, out_part, rows, cots)
        )

        after = (planes - 1 - step) * 3
        places = {0: (after + 6, 0), 1: (after, 1), 2: (after + 1, 1), 3: (after + 5, 0)}[step]
        out_tasks.append(flow.launch(plane_scatter(out_part, False, *places)))
        if step == 0:
            cot_tasks.append(flow.launch(plane_gather(cot_piece, 3, 2)))
        in_part = low(
            jnp.dot(gate_grad, gate_weight, preferred_element_type=jnp.float32)
            + jnp.dot(up_grad, up_weight, preferred_element_type=jnp.float32)
        )
        in_part, gate_grad, up_grad, act_scaled, rows, cots = flow.close(
            (in_part, gate_grad, up_grad, act_scaled, rows, cots)
        )
        kept_parts.append((rows, cots, gate_grad, up_grad, act_scaled))

    in_tasks.append(flow.launch(plane_scatter(in_part, True)))
    in_moving = flow.launch(
        passing(low(in_tasks[2].result + in_moving.result.astype(jnp.float32)))
    )
    gate_sums = jnp.stack(gate_parts).reshape(-1, exp_here, 2, 2, 2, own_count)
    gate_sums = gate_sums[:, :, 0] + core_hop(gate_sums[:, :, 1])
    gate_sums = gate_sums[:, :, 0] + y_hop(gate_sums[:, :, 1])
    block = jnp.arange(dp_size, dtype=jnp.int32)
    place = ((dp_index // 2 - block // 2) % planes) * 2 + (block + dp_index) % 2
    gate_sums = gate_sums.transpose(0, 2, 1, 3).reshape(dp_size, exp_here, own_count)[place]
    gate_weight_grad = sum(
        jnp.einsum("tf,td->fd", gate_grad, rows, preferred_element_type=jnp.float32)
        for rows, _, gate_grad, _, _ in kept_parts
    )
    gate_weight_grad, kept_parts, gate_sums = flow.close(
        (gate_weight_grad, kept_parts, gate_sums)
    )
    gate_sums = lax.all_to_all(gate_sums, "dp", split_axis=0, concat_axis=0, tiled=True)
    gate_sums = gate_sums.reshape(experts, own_count).T
    up_weight_grad = sum(
        jnp.einsum("tf,td->fd", up_grad, rows, preferred_element_type=jnp.float32)
        for rows, _, _, up_grad, _ in kept_parts
    )
    gate_sums, up_weight_grad, kept_parts = flow.close((gate_sums, up_weight_grad, kept_parts))
    flow.close(())
    in_moving = flow.launch(
        passing(low(in_tasks[3].result + in_moving.result.astype(jnp.float32)))
    )
    kept_parts = flow.close(kept_parts)
    out_moving = flow.launch(passing(low(out_tasks[1].result)))
    ffn_sum = in_tasks[0].result + in_moving.result.astype(jnp.float32)
    probs_own, gates_own, picked_own = gating(normed_own_low, standing_own)
    gate_sums = jnp.where(standing_own > 1.5, gate_sums, 0.0)
    picked_grad = (
        gate_sums - jnp.sum(gate_sums * gates_own, axis=-1, keepdims=True)
    ) / picked_own
    probs_grad = jnp.where(standing_own > 0.5, picked_grad, 0.0)
    logit_grad = low(
        probs_own * (probs_grad - jnp.sum(probs_own * probs_grad, axis=-1, keepdims=True))
    )
    router_grad = jnp.einsum(
        "te,td->ed", logit_grad, normed_own_low, preferred_element_type=jnp.float32
    )
    ffn_in = ffn_sum + jnp.dot(logit_grad, router_weight, preferred_element_type=jnp.float32)
    ffn_resid_grad, gain_ffn_grad = norm_backward(resid_own, inverse_own, gain_ffn_f, ffn_in)
    mid_grad_own = cot_own.astype(jnp.float32) + ffn_resid_grad
    shared_parts = [gate_weight_grad, up_weight_grad]
    mid_low, kept_parts, shared_parts = flow.close(
        (tensor_gather(low(mid_grad_own), tensor_index), kept_parts, shared_parts)
    )
    out_moving = flow.launch(
        passing(low(out_tasks[2].result + out_moving.result.astype(jnp.float32)))
    )
    down_weight_grad = sum(
        jnp.einsum("tf,td->fd", act_scaled, cots, preferred_element_type=jnp.float32)
        for _, cots, _, _, act_scaled in kept_parts[: planes // 2]
    )

    def shared_sum(grads):
        grads = jnp.stack([low(grad[routed_here:]) for grad in grads])
        return lax.all_to_all(grads, "dp", split_axis=2, concat_axis=1, tiled=True)

    shared_grads = shared_sum(shared_parts)
    output_weight_grad = jnp.einsum(
        "th,td->hd", heads_low, mid_low, preferred_element_type=jnp.float32
    )
    heads_grad = low(
        jnp.einsum("td,hd->th", mid_low, output_weight, preferred_element_type=jnp.float32)
    ).reshape(tok_count, heads_here, V_HEAD)
    heads_grad, output_weight_grad, down_weight_grad, kept_parts = flow.close(
        (heads_grad, output_weight_grad, down_weight_grad, kept_parts)
    )
    down_weight_grad += sum(
        jnp.einsum("tf,td->fd", act_scaled, cots, preferred_element_type=jnp.float32)
        for _, cots, _, _, act_scaled in kept_parts[planes // 2 :]
    )
    output_task = flow.launch(
        dp_scatter_steps(
            lambda i: lax.dynamic_slice_in_dim(
                output_weight_grad, i * w_output.shape[1], w_output.shape[1], 1
            ),
            dp_index,
        )
    )
    masked = block_scores(query_low, key_full, seq_ids, 0)
    attn_probs = jnp.exp(masked - log_total)
    prob_grad = jnp.einsum("qhc,khc->hqk", heads_grad, value_low, preferred_element_type=jnp.float32)
    row_dot = jnp.sum(attn_probs * prob_grad, axis=-1, keepdims=True)
    score_grad = low(attn_probs * (prob_grad - row_dot))
    score_grad, probs_low, down_weight_grad = flow.close(
        (score_grad, low(attn_probs), down_weight_grad)
    )
    out_moving = flow.launch(
        passing(low(out_tasks[3].result + out_moving.result.astype(jnp.float32)))
    )
    query_grad = (
        jnp.einsum("hqk,khc->qhc", score_grad, key_full, preferred_element_type=jnp.float32)
        * softmax_scale
    )
    key_grad = (
        jnp.einsum("hqk,qhc->khc", score_grad, query_low, preferred_element_type=jnp.float32)
        * softmax_scale
    )
    value_grad = jnp.einsum(
        "hqk,qhc->khc", probs_low, heads_grad, preferred_element_type=jnp.float32
    )
    query_grad, key_grad, value_grad = flow.close((query_grad, key_grad, value_grad))
    query_pre_grad = low(
        jnp.concatenate(
            [
                query_grad[..., :QK_NOPE],
                rotate(query_grad[..., QK_NOPE:], cosine[:, None, :], -sine_part[:, None, :]),
            ],
            axis=-1,
        )
    ).reshape(tok_count, heads_here * head_width)
    query_weight_grad = jnp.einsum(
        "td,tq->dq", normed_attn_low, query_pre_grad, preferred_element_type=jnp.float32
    )
    expand_grad = low(jnp.concatenate([key_grad[..., :QK_NOPE], value_grad], axis=-1)).reshape(
        tok_count, heads_here * (QK_NOPE + V_HEAD)
    )
    latent_grad = jnp.einsum(
        "te,re->tr", expand_grad, expand_weight, preferred_element_type=jnp.float32
    )
    expand_weight_grad = jnp.einsum(
        "tr,te->re", latent_low, expand_grad, preferred_element_type=jnp.float32
    )
    shared_down_sent = low(down_weight_grad[routed_here:])
    weight_grads = [gate_weight_grad, up_weight_grad, down_weight_grad]
    latent_grad, query_weight_grad, expand_weight_grad, shared_grads, weight_grads = flow.close(
        (latent_grad, query_weight_grad, expand_weight_grad, shared_grads, weight_grads)
    )
    rope_grad = jnp.sum(key_grad[..., QK_NOPE:], axis=1)
    latent_pre_grad, gain_latent_grad = norm_backward(
        latent_part, inverse_latent, gain_latent_f, latent_grad
    )
    latent_all_grad = low(
        jnp.concatenate([latent_pre_grad, rotate(rope_grad, cosine, -sine_part)], axis=-1)
    )
    attn_in = jnp.einsum(
        "tq,dq->td", query_pre_grad, query_weight, preferred_element_type=jnp.float32
    ) + jnp.dot(latent_all_grad, latent_weight, preferred_element_type=jnp.float32)
    latent_weight_grad = jnp.einsum(
        "tc,td->cd", latent_all_grad, normed_attn_low, preferred_element_type=jnp.float32
    )
    gain_attn_grad = jnp.sum(attn_in * (resid_in * inverse_attn), axis=0)
    attn_in_own = tensor_scatter(attn_in, tensor_index)
    input_grad, _ = norm_backward(
        own_rows(resid_in), own_rows(inverse_attn), gain_attn_f, attn_in_own
    )
    tokens_grad = tensor_gather(low(mid_grad_own + input_grad), tensor_index)

    out_sum = out_tasks[0].result + out_moving.result.astype(jnp.float32)
    result = tensor_gather(low(resid_own + out_sum), tensor_index)

    output_share = drained(output_task)
    query_share = dp_scatter(
        lambda i: lax.dynamic_slice_in_dim(query_weight_grad, i * lat_block, lat_block, 0),
        dp_index,
    )
    expand_block = w_expand.shape[0]
    expand_share = dp_scatter(
        lambda i: lax.dynamic_slice_in_dim(expand_weight_grad, i * expand_block, expand_block, 0),
        dp_index,
    )

    gain_latent_rows = padded(gain_latent_grad.reshape(dp_size, -1), 1, lat_block).reshape(width)
    gain_grads = jnp.stack([gain_attn_grad, gain_ffn_grad, gain_latent_rows])
    side_grad = jnp.concatenate(
        [
            low(latent_weight_grad),
            low(router_grad),
            padded(low(gain_grads), 0, side_rows - mark_start),
        ]
    ).reshape(2, 2, side_rows_here, width)
    kept_side = lax.dynamic_index_in_dim(side_grad, core, 1, keepdims=False)
    sent_side = lax.dynamic_index_in_dim(side_grad, 1 - core, 1, keepdims=False)
    side_grad = kept_side.astype(jnp.float32) + core_hop(sent_side).astype(jnp.float32)
    kept_side = lax.dynamic_index_in_dim(side_grad, level, 0, keepdims=False)
    sent_side = lax.dynamic_index_in_dim(side_grad, 1 - level, 0, keepdims=False)
    side_grad = kept_side + y_hop(low(sent_side)).astype(jnp.float32)
    side_piece = dp_scatter(
        lambda i: lax.dynamic_slice_in_dim(side_grad, i * lat_block, lat_block, 1), dp_index
    )
    grad_full = tensor_gather(low(side_piece), tensor_index).astype(jnp.float32)
    latent_share = grad_full[:lat_width].T
    router_share = grad_full[lat_width:mark_start].T
    gain_attn_share = grad_full[mark_start]
    gain_ffn_share = grad_full[mark_start + 1]
    gain_latent_share = grad_full[mark_start + 2, : gain_latent.shape[0]]

    def routed_grad(grad):
        return grad[:routed_here].reshape(exp_here, group, width)

    routed_grads = (
        routed_grad(weight_grads[0]).swapaxes(1, 2),
        routed_grad(weight_grads[1]).swapaxes(1, 2),
        routed_grad(weight_grads[2]),
    )
    shared_down_grad = lax.all_to_all(
        shared_down_sent, "dp", split_axis=1, concat_axis=0, tiled=True
    ).astype(jnp.float32)

    return (
        result,
        tokens_grad,
        gain_attn_share,
        query_share,
        latent_share,
        gain_latent_share,
        expand_share,
        output_share,
        gain_ffn_share,
        router_share,
        shared_grads[0].astype(jnp.float32).T,
        shared_grads[1].astype(jnp.float32).T,
        shared_down_grad,
        *routed_grads,
    )


def solution(mesh):
    dense = mesh.shape["dp"] == 8 and mesh.shape["tensor"] == 4
    return jax.shard_map(
        body_dense if dense else body,
        mesh=mesh,
        in_specs=(
            P("dp", None),
            P("dp", None),
            P("dp", None),
            P("dp"),
            P("dp"),
            P("dp"),
            P("dp", "tensor"),
            P("dp", None),
            P("dp"),
            P("dp", "tensor"),
            P("tensor", "dp"),
            P("dp"),
            P("dp", None),
            P("dp", "tensor"),
            P("dp", "tensor"),
            P("tensor", "dp"),
            P("dp", None, "tensor"),
            P("dp", None, "tensor"),
            P("dp", "tensor", None),
        ),
        out_specs=(
            P("dp", None),
            P("dp", None),
            P("dp"),
            P("dp", "tensor"),
            P("dp", None),
            P("dp"),
            P("dp", "tensor"),
            P("tensor", "dp"),
            P("dp"),
            P("dp", None),
            P("dp", "tensor"),
            P("dp", "tensor"),
            P("tensor", "dp"),
            P("dp", None, "tensor"),
            P("dp", None, "tensor"),
            P("dp", "tensor", None),
        ),
        check_vma=False,
    )
```
